32 devices in a mesh: batch: 8 (over y, x, core), mp: 4 (over z).
Axes of the slice: x: 2, y: 2, z: 4, core: 2. Of those that a mesh axis runs over, the one named last changes fastest.
Arguments:
- hidden_in: bfloat16 [16, 512, 768], P('batch', 'mp'), may hold values from -6 to 6
- memory: bfloat16 [16, 1024, 768], P('batch', 'mp'), may hold values from -6 to 6
- tgt_len: int32 [16], P('batch'), may hold values from 256 to 512, as said below
- src_len: int32 [16], P('batch'), may hold values from 128 to 1024, as said below
- target_ids: int32 [16, 512], P('batch'), may hold values from 0 to 32127
- task_ids: int32 [16], P('batch'), may hold values from 0 to 2
- task_weight: float32 [3], replicated, may hold values from 3 to 30
- gain_self: bfloat16 [768], P('batch'), may hold values from 0.25 to 1.75
- q_self: bfloat16 [768, 768], P('batch', 'mp'), may hold values from -0.0546875 to 0.0546875
- k_self: bfloat16 [768, 768], P('batch', 'mp'), may hold values from -0.21875 to 0.21875
- v_self: bfloat16 [768, 768], P('batch', 'mp'), may hold values from -0.21875 to 0.21875
- o_self: bfloat16 [768, 768], P('batch', 'mp'), may hold values from -0.875 to 0.875
- gain_cross: bfloat16 [768], P('batch'), may hold values from 0.25 to 1.75
- q_cross: bfloat16 [768, 768], P('batch', 'mp'), may hold values from -0.0546875 to 0.0546875
- k_cross: bfloat16 [768, 768], P('batch', 'mp'), may hold values from -0.21875 to 0.21875
- v_cross: bfloat16 [768, 768], P('batch', 'mp'), may hold values from -0.21875 to 0.21875
- o_cross: bfloat16 [768, 768], P('batch', 'mp'), may hold values from -0.875 to 0.875
- gain_mlp: bfloat16 [768], P('batch'), may hold values from 0.25 to 1.75
- mlp_gate: bfloat16 [768, 2048], P('batch', 'mp'), may hold values from -0.21875 to 0.21875
- mlp_up: bfloat16 [768, 2048], P('batch', 'mp'), may hold values from -0.21875 to 0.21875
- mlp_down: bfloat16 [768, 2048], P('batch', 'mp'), may hold values from -0.1875 to 0.1875
- gain_exit: bfloat16 [768], P('batch'), may hold values from 0.25 to 1.75
- embed_table: bfloat16 [768, 32128], P('batch', 'mp'), may hold values from -12 to 12
Outputs:
- block_out: bfloat16 [16, 512, 768], P('batch', 'mp')
- pair_loss: float32 [16], P('batch')
- hidden_grad: float32 [16, 512, 768], P('batch', 'mp')
- memory_grad: float32 [16, 1024, 768], P('batch', 'mp')
- gain_self_grad: float32 [768], P('batch')
- q_self_grad: float32 [768, 768], P('batch', 'mp')
- k_self_grad: float32 [768, 768], P('batch', 'mp')
- v_self_grad: float32 [768, 768], P('batch', 'mp')
- o_self_grad: float32 [768, 768], P('batch', 'mp')
- gain_cross_grad: float32 [768], P('batch')
- q_cross_grad: float32 [768, 768], P('batch', 'mp')
- k_cross_grad: float32 [768, 768], P('batch', 'mp')
- v_cross_grad: float32 [768, 768], P('batch', 'mp')
- o_cross_grad: float32 [768, 768], P('batch', 'mp')
- gain_mlp_grad: float32 [768], P('batch')
- mlp_gate_grad: float32 [768, 2048], P('batch', 'mp')
- mlp_up_grad: float32 [768, 2048], P('batch', 'mp')
- mlp_down_grad: float32 [768, 2048], P('batch', 'mp')
- gain_exit_grad: float32 [768], P('batch')
- embed_table_grad: float32 [768, 32128], P('batch', 'mp')
The draws below stay inside these ranges and needn't reach their ends.
Inputs may be any that keep to these rules, and one draw needn't show every extreme that they name: `tgt_len`: some pair has a target of exactly 512 positions. `src_len`: some pair has a source of exactly 1024 positions.
All inputs are finite; a program needn't handle non-finite values.
Results may differ from the reference program's by a relative error of at most 0.025.
The reference program's roundings to bfloat16 on the way count: a program that leaves them out, or rounds other values in their place, can miss the bound.
Values may be sent and summed in bfloat16 or wider, within the bound.
No kernel may reach another device: no remote copies, remote signals or barrier semaphores. Data moves between devices by JAX's collectives and lax.ppermute only.
A program may use at most 320 MiB of HBM per device.

```python
import math
import jax
import jax.numpy as jnp
import numpy as np
from jax import lax

D = 768
H = 12
DH = 64
FF = 2048
V = 32128
TASKS = 3
PAIRS = 2
TGT = 512
SRC = 1024
NPAIRS = 16
N_BATCH = 8


def ragged_lengths(key, count, least, most):
    former, latter = jax.random.split(key)
    lengths = jax.random.randint(former, (count,), least, most + 1)
    chosen = jax.random.randint(latter, (), 0, count)
    return jnp.where(jnp.arange(count) == chosen, most, lengths).astype(jnp.int32)


def draw_tgt_len(key, part):
    return ragged_lengths(jax.random.fold_in(key, 11), NPAIRS, TGT // 2, TGT)


def draw_src_len(key, part):
    return ragged_lengths(jax.random.fold_in(key, 23), NPAIRS, SRC // 8, SRC)


def touch_ends(result, rng, low, top_value):
    longest = result.shape.index(max(result.shape))
    spots = []
    for shift in (0, 1):
        where = [jax.random.randint(jax.random.fold_in(rng, axis), (), 0, length) for axis, length in enumerate(result.shape)]
        where[longest] = (where[longest] + shift) % result.shape[longest]
        spots.append(tuple(where))
    return result.at[spots[0]].set(low).at[spots[1]].set(top_value)


def with_spikes(array, stream_key, source, target, shards_of, factor):
    def block_of(position):
        return (jnp.arange(array.shape[position]) // (array.shape[position] // shards_of)).reshape((-1,) + (1,) * (array.ndim - 1 - position))

    one_side = jax.random.permutation(stream_key, shards_of)[block_of(target)]
    other_side = (block_of(target) + shards_of // 2) % shards_of
    return jnp.where((block_of(source) == one_side) | (block_of(source) == other_side), factor * array, array)


def level_of(key, extent, cuts, low, high):
    def one(dim, shards_of):
        heights = jax.random.uniform(jax.random.fold_in(jax.random.fold_in(key, 6), dim), (shards_of,), jnp.float32, low / len(cuts), high / len(cuts))
        return jnp.repeat(jnp.exp(heights), extent[dim] // shards_of).reshape((-1,) + (1,) * (len(extent) - dim - 1))

    factor_of = one(*cuts[0])
    for cut in cuts[1:]:
        factor_of = factor_of * one(*cut)
    return factor_of


def cumulative_ranks(amount, skew):
    loads = [(1 << 20) // math.isqrt(rank ** skew) + 1 for rank in range(1, amount + 1)]
    scale = 1 + sum(loads) // (1 << 30)
    return np.cumsum(np.array([max(1, weight // scale) for weight in loads]))


def skewed_ids(key, extent, amount, skew):
    table = cumulative_ranks(amount, skew)
    ticket = jax.random.randint(jax.random.fold_in(key, 1), extent, 0, int(table[amount - 1]))
    rank = jnp.searchsorted(jnp.asarray(table, jnp.int32), ticket, side="right")
    return jax.random.permutation(jax.random.fold_in(key, 2), amount)[rank].astype(jnp.int32)


def bell_draw(stream_key, extent, spread, most, pieces=(), held_as=jnp.bfloat16):
    result = jax.random.normal(stream_key, extent, jnp.float32) * spread
    if len(pieces) > 0:
        result = level_of(stream_key, extent, pieces, -0.22, 0.18) * result
    return jnp.clip(result, min=-most, max=most).astype(held_as)


def gaussian_with(key, shape, spread, most, shards, heavy, dtype=jnp.bfloat16):
    result = spread * jax.random.normal(key, shape, jnp.float32)
    if shards:
        result = result * level_of(key, shape, shards, -0.22, 0.18)
    return jnp.clip(with_spikes(result, jax.random.fold_in(key, 3), *heavy), -most, most).astype(dtype)


def setup_inputs(seed: int = 0) -> dict:
    splits = jax.random.split(jax.random.key(seed), 24)
    return {
        "hidden_in": gaussian_with(splits[0], (NPAIRS, TGT, D), 1.0, 6.0, ((0, 8), (1, 4)), (0, 2, 8, 2.0)),
        "memory": bell_draw(splits[1], (NPAIRS, SRC, D), 1.0, 6.0, ((0, 8), (1, 4))),
        "tgt_len": draw_tgt_len(jax.random.fold_in(splits[23], 71), 0),
        "src_len": draw_src_len(jax.random.fold_in(splits[23], 71), 0),
        "target_ids": touch_ends(skewed_ids(splits[4], (NPAIRS, TGT), V, 2), jax.random.fold_in(splits[4], 3), 0, V - 1).astype(jnp.int32),
        "task_ids": touch_ends(jax.random.randint(splits[5], (NPAIRS,), 0, TASKS), jax.random.fold_in(splits[5], 1), 0, TASKS - 1).astype(jnp.int32),
        "task_weight": jnp.clip(jnp.exp(jax.random.uniform(splits[6], (TASKS,), jnp.float32, math.log(3.0), math.log(30.0))), 3.0, 30.0),
        "gain_self": jnp.clip(1.0 + 0.15 * jax.random.normal(splits[7], (D,), jnp.float32), 0.25, 1.75).astype(jnp.bfloat16),
        "q_self": bell_draw(splits[8], (D, H * DH), (D * 16) ** -0.5, 0.0546875, ((0, 8), (1, 4))),
        "k_self": bell_draw(splits[9], (D, H * DH), D ** -0.5, 0.21875, ((0, 8), (1, 4))),
        "v_self": bell_draw(splits[10], (D, H * DH), D ** -0.5, 0.21875, ((0, 8), (1, 4))),
        "o_self": bell_draw(splits[11], (D, H * DH), (H * DH // 16) ** -0.5, 0.875, ((0, 8), (1, 4))),
        "gain_cross": jnp.clip(1.0 + 0.15 * jax.random.normal(splits[12], (D,), jnp.float32), 0.25, 1.75).astype(jnp.bfloat16),
        "q_cross": bell_draw(splits[13], (D, H * DH), (D * 16) ** -0.5, 0.0546875, ((0, 8), (1, 4))),
        "k_cross": bell_draw(splits[14], (D, H * DH), D ** -0.5, 0.21875, ((0, 8), (1, 4))),
        "v_cross": bell_draw(splits[15], (D, H * DH), D ** -0.5, 0.21875, ((0, 8), (1, 4))),
        "o_cross": bell_draw(splits[16], (D, H * DH), (H * DH // 16) ** -0.5, 0.875, ((0, 8), (1, 4))),
        "gain_mlp": jnp.clip(1.0 + 0.15 * jax.random.normal(splits[17], (D,), jnp.float32), 0.25, 1.75).astype(jnp.bfloat16),
        "mlp_gate": bell_draw(splits[18], (D, FF), D ** -0.5, 0.21875, ((0, 8), (1, 4))),
        "mlp_up": bell_draw(splits[19], (D, FF), D ** -0.5, 0.21875, ((0, 8), (1, 4))),
        "mlp_down": bell_draw(splits[20], (D, FF), (FF // 2) ** -0.5, 0.1875, ((0, 8), (1, 4))),
        "gain_exit": jnp.clip(1.0 + 0.15 * jax.random.normal(splits[21], (D,), jnp.float32), 0.25, 1.75).astype(jnp.bfloat16),
        "embed_table": bell_draw(splits[22], (D, V), 2.0, 12.0, ((0, 8), (1, 4))),
    }


EPSILON = 1e-06
MASKED_OUT = -1000000000.0
GELU_SCALE = 0.7978845608028654
PRECISE = lax.Precision.HIGHEST

@jax.custom_vjp
def low(v):
    return lax.optimization_barrier(v.astype(jnp.bfloat16)).astype(jnp.float32)

@jax.custom_vjp
def low_back(v):
    return v

def low_keep(v):
    return (low(v), None)

def low_pass(kept, grad):
    return (grad,)

def back_keep(v):
    return (v, None)

def back_low(kept, grad):
    return (low(grad),)
low.defvjp(low_keep, low_pass)
low_back.defvjp(back_keep, back_low)

def both_ways(values):
    return low_back(low(values))

def product(form, former, latter):
    return jnp.einsum(form, former, latter, precision=PRECISE)

def gelu_tanh(values):
    return 0.5 * values * (1.0 + jnp.tanh(GELU_SCALE * (values + 0.044715 * values * values * values)))

def rms_norm(values, gain_vec):
    return values * lax.rsqrt(lax.optimization_barrier(jnp.mean(values * values, -1, keepdims=True)) + EPSILON) * gain_vec

def split_heads(values):
    return values.reshape(values.shape[0], values.shape[1], H, DH)

def attend(queries, key_rows, value_rows, allowed):
    scores = low_back(product('qhd,khd->hqk', queries, key_rows))
    scores = jnp.where(allowed[None], scores, MASKED_OUT)
    highest = lax.optimization_barrier(jnp.max(scores, -1, keepdims=True))
    raised = jnp.exp(scores - highest)
    attn_weights = raised / lax.optimization_barrier(jnp.sum(raised, -1, keepdims=True))
    return product('hqk,khd->qhd', low(attn_weights), value_rows)

def forward_group(weights, row_input, memory_rows, tgt_group, src_group, id_group, weight_group):
    gain_self, q_self, k_self, v_self, o_self, gain_cross, q_cross, k_cross, v_cross, o_cross, gain_mlp, mlp_gate, mlp_up, mlp_down, gain_exit, embed_table = weights
    pair_count = row_input.shape[0]
    positions = jnp.arange(TGT)
    sources = jnp.arange(SRC)
    causal = positions[None, :] <= positions[:, None]
    valid_mask = (positions[None, :] < tgt_group[:, None]).astype(jnp.float32)

    def self_pair(inputs):
        queries, key_rows, value_rows, length = inputs
        return attend(queries, key_rows, value_rows, causal & (positions[None, :] < length))

    def cross_pair(inputs):
        queries, key_rows, value_rows, length = inputs
        allowed = jnp.broadcast_to(sources[None, :] < length, (TGT, SRC))
        return attend(queries, key_rows, value_rows, allowed)

    def head_pair(inputs):
        row_block, id_rows, valid_rows = inputs
        logits = low_back(product('td,dv->tv', row_block, embed_table)) * D ** (-0.5)
        highest = lax.optimization_barrier(jnp.max(logits, -1, keepdims=True))
        log_totals = highest[:, 0] + jnp.log(lax.optimization_barrier(jnp.sum(jnp.exp(logits - highest), -1)))
        picked = lax.optimization_barrier(jnp.sum(jnp.where(jnp.arange(V)[None, :] == id_rows[:, None], logits, 0.0), -1))
        return (log_totals - picked) * valid_rows
    rows_one = low(rms_norm(row_input, gain_self))
    queries_one = both_ways(product('ptd,de->pte', rows_one, q_self))
    keys_one = both_ways(product('ptd,de->pte', rows_one, k_self))
    values_one = both_ways(product('ptd,de->pte', rows_one, v_self))
    mixed_one = lax.map(jax.checkpoint(self_pair), (split_heads(queries_one), split_heads(keys_one), split_heads(values_one), tgt_group))
    attended_one = both_ways(mixed_one.reshape(pair_count, TGT, H * DH))
    residual_one = row_input + low_back(product('pte,de->ptd', attended_one, o_self))
    rows_two = low(rms_norm(residual_one, gain_cross))
    queries_two = both_ways(product('ptd,de->pte', rows_two, q_cross))
    keys_two = both_ways(product('psd,de->pse', memory_rows, k_cross))
    values_two = both_ways(product('psd,de->pse', memory_rows, v_cross))
    mixed_two = lax.map(jax.checkpoint(cross_pair), (split_heads(queries_two), split_heads(keys_two), split_heads(values_two), src_group))
    attended_two = both_ways(mixed_two.reshape(pair_count, TGT, H * DH))
    residual_two = residual_one + low_back(product('pte,de->ptd', attended_two, o_cross))
    rows_three = low(rms_norm(residual_two, gain_mlp))
    gate = low_back(product('ptd,df->ptf', rows_three, mlp_gate))
    up_proj = low_back(product('ptd,df->ptf', rows_three, mlp_up))
    hidden = low(gelu_tanh(gate) * up_proj)
    residual_three = residual_two + low_back(product('ptf,df->ptd', hidden, mlp_down))
    rows_four = low(rms_norm(residual_three, gain_exit))
    losses = lax.map(jax.checkpoint(head_pair), (rows_four, id_group, valid_mask))
    objective = jnp.sum(weight_group[:, None] * losses)
    pair_loss = lax.optimization_barrier(jnp.sum(losses, -1)) / tgt_group.astype(jnp.float32)
    return (objective, (residual_three, pair_loss))

def reference(hidden_in, memory, tgt_len, src_len, target_ids, task_ids, task_weight, gain_self, q_self, k_self, v_self, o_self, gain_cross, q_cross, k_cross, v_cross, o_cross, gain_mlp, mlp_gate, mlp_up, mlp_down, gain_exit, embed_table):
    params = tuple((item.astype(jnp.float32) for item in (gain_self, q_self, k_self, v_self, o_self, gain_cross, q_cross, k_cross, v_cross, o_cross, gain_mlp, mlp_gate, mlp_up, mlp_down, gain_exit, embed_table)))
    pair_weight = lax.optimization_barrier(jnp.sum(jnp.where(task_ids[:, None] == jnp.arange(TASKS)[None, :], task_weight.astype(jnp.float32)[None, :], 0.0), -1))

    def grouped(values):
        return values.reshape((N_BATCH, PAIRS) + values.shape[1:])

    def step(running, group):
        row_group, mem_group, tgt_group, src_group, id_group, weight_group = group

        def objective_of(weights, row_values, mem_values):
            return forward_group(weights, row_values, mem_values, tgt_group, src_group, id_group, weight_group)
        objective, pullback, extras = jax.vjp(objective_of, params, row_group.astype(jnp.float32), mem_group.astype(jnp.float32), has_aux=True)
        weight_grads, row_grad, mem_grad = pullback(jnp.ones_like(objective))
        running = jax.tree.map(lambda former, latter: former + latter, running, weight_grads)
        return (running, (extras[0].astype(jnp.bfloat16), extras[1], row_grad, mem_grad))
    initial = jax.tree.map(jnp.zeros_like, params)
    totals, stacked = lax.scan(step, initial, (grouped(hidden_in), grouped(memory), grouped(tgt_len), grouped(src_len), grouped(target_ids), grouped(pair_weight)))

    def flatten(values):
        return values.reshape((NPAIRS,) + values.shape[2:])
    block_out = flatten(stacked[0])
    pair_loss = flatten(stacked[1])
    hidden_grad = flatten(stacked[2])
    memory_grad = flatten(stacked[3])
    return (block_out, pair_loss, hidden_grad, memory_grad, totals[0], totals[1], totals[2], totals[3], totals[4], totals[5], totals[6], totals[7], totals[8], totals[9], totals[10], totals[11], totals[12], totals[13], totals[14], totals[15])
```

```python
import functools

import jax
import jax.numpy as jnp
from jax import lax
from jax.experimental import pallas as pl
from jax.experimental.pallas import tpu as pltpu
from jax.sharding import PartitionSpec as P

DH = 64
LANES = 128
EPSILON = 1e-06
MASKED_OUT = -1000000000.0
GELU_SCALE = 0.7978845608028654
VMEM_LIMIT = 56 * 1024 * 1024
VOCAB_BLOCK = 1024
BF16 = jnp.bfloat16
F32 = jnp.float32


def params():
    return pltpu.CompilerParams(
        dimension_semantics=("arbitrary",), vmem_limit_bytes=VMEM_LIMIT
    )


def mm(a, b):
    return lax.dot_general(a, b, (((1,), (0,)), ((), ())), preferred_element_type=F32)


def mm_nt(a, b):
    return lax.dot_general(a, b, (((1,), (1,)), ((), ())), preferred_element_type=F32)


def mm_tn(a, b):
    return lax.dot_general(a, b, (((0,), (0,)), ((), ())), preferred_element_type=F32)


def block_positions(scal_ref, count, size, dim):
    shape = (size, 1) if dim == 0 else (1, size)
    pieces = [
        lax.broadcasted_iota(jnp.int32, shape, dim) + scal_ref[i] * size for i in range(count)
    ]
    return jnp.concatenate(pieces, axis=dim)


def allowed_mask(scal_ref, rows, keys, causal):
    key_pos = block_positions(scal_ref, 4, keys // 4, 1)
    allowed = jnp.broadcast_to(key_pos < scal_ref[4], (rows, keys))
    if causal:
        row_pos = block_positions(scal_ref, 4, rows // 4, 0)
        allowed = allowed & (key_pos <= row_pos)
    return allowed


def head_lanes(rows, head):
    lane = lax.broadcasted_iota(jnp.int32, (rows, LANES), 1)
    return (lane < DH) if head == 0 else (lane >= DH)


def attend_kernel(causal, scal_ref, q_ref, k_ref, v_ref, out_ref, lse_ref):
    rows, keys = q_ref.shape[0], k_ref.shape[0]
    allowed = allowed_mask(scal_ref, rows, keys, causal)
    q, k, v = q_ref[...], k_ref[...], v_ref[...]
    outs, lses = [], []
    for head in range(2):
        q_head = jnp.where(head_lanes(rows, head), q, jnp.zeros_like(q))
        scores = jnp.where(allowed, mm_nt(q_head, k), MASKED_OUT)
        highest = jnp.max(scores, -1, keepdims=True)
        raised = jnp.exp(scores - highest)
        totals = jnp.sum(raised, -1, keepdims=True)
        weights = (raised * (1.0 / totals)).astype(BF16)
        outs.append(mm(weights, v))
        lses.append(highest + jnp.log(totals))
    first = head_lanes(rows, 0)
    out_ref[...] = jnp.where(first, outs[0], outs[1]).astype(out_ref.dtype)
    lse_ref[...] = jnp.where(first, lses[0], lses[1])


def attend(scal, q, k, v, causal):
    rows, width = q.shape
    keys = k.shape[0]
    cost = pl.CostEstimate(
        flops=8 * rows * keys * width,
        transcendentals=rows * keys * width // DH,
        bytes_accessed=2 * (2 * rows + 2 * keys) * width + 4 * rows * width,
    )
    row_spec = pl.BlockSpec((rows, LANES), lambda j, s: (0, j))
    key_spec = pl.BlockSpec((keys, LANES), lambda j, s: (0, j))
    return pl.pallas_call(
        functools.partial(attend_kernel, causal),
        out_shape=(
            jax.ShapeDtypeStruct((rows, width), BF16),
            jax.ShapeDtypeStruct((rows, width), F32),
        ),
        grid_spec=pltpu.PrefetchScalarGridSpec(
            num_scalar_prefetch=1,
            grid=(width // LANES,),
            in_specs=[row_spec, key_spec, key_spec],
            out_specs=(row_spec, row_spec),
        ),
        compiler_params=params(),
        cost_estimate=cost,
        name="attend",
    )(scal, q, k, v)


def attend_back_kernel(
    causal, scal_ref, q_ref, k_ref, v_ref, lse_ref, d_ref, dq_ref, dk_ref, dv_ref
):
    rows, keys = q_ref.shape[0], k_ref.shape[0]
    allowed = allowed_mask(scal_ref, rows, keys, causal)
    q, k, v, d_out = q_ref[...], k_ref[...], v_ref[...], d_ref[...]
    dqs, dks, dvs = [], [], []
    for head in range(2):
        mine = head_lanes(rows, head)
        q_head = jnp.where(mine, q, jnp.zeros_like(q))
        d_head = jnp.where(mine, d_out, jnp.zeros_like(d_out))
        scores = jnp.where(allowed, mm_nt(q_head, k), MASKED_OUT)
        weights = jnp.exp(scores - lse_ref[:, head * DH : head * DH + 1])
        d_weights = mm_nt(d_head, v)
        inner = jnp.sum(weights * d_weights, -1, keepdims=True)
        d_scores = (weights * (d_weights - inner)).astype(BF16)
        dqs.append(mm(d_scores, k))
        dks.append(mm_tn(d_scores, q))
        dvs.append(mm_tn(weights.astype(BF16), d_out))
    dq_ref[...] = jnp.where(head_lanes(rows, 0), dqs[0], dqs[1]).astype(BF16)
    first = head_lanes(keys, 0)
    dk_ref[...] = jnp.where(first, dks[0], dks[1]).astype(BF16)
    dv_ref[...] = jnp.where(first, dvs[0], dvs[1]).astype(BF16)


def attend_back(scal, q, k, v, lse, d_out, causal):
    rows, width = q.shape
    keys = k.shape[0]
    cost = pl.CostEstimate(
        flops=20 * rows * keys * width,
        transcendentals=rows * keys * width // DH,
        bytes_accessed=2 * (3 * rows + 4 * keys) * width + 4 * rows * width,
    )
    row_spec = pl.BlockSpec((rows, LANES), lambda j, s: (0, j))
    key_spec = pl.BlockSpec((keys, LANES), lambda j, s: (0, j))
    return pl.pallas_call(
        functools.partial(attend_back_kernel, causal),
        out_shape=(
            jax.ShapeDtypeStruct((rows, width), BF16),
            jax.ShapeDtypeStruct((keys, width), BF16),
            jax.ShapeDtypeStruct((keys, width), BF16),
        ),
        grid_spec=pltpu.PrefetchScalarGridSpec(
            num_scalar_prefetch=1,
            grid=(width // LANES,),
            in_specs=[row_spec, key_spec, key_spec, row_spec, row_spec],
            out_specs=(row_spec, key_spec, key_spec),
        ),
        compiler_params=params(),
        cost_estimate=cost,
        name="attend_back",
    )(scal, q, k, v, lse, d_out)


STAT = 64
WEIGHT_LANE = 64
ID_LANE = 65
TURNED = 8


def head_kernel(vocab, scale, rows_ref, table_ref, ids_ref, prob_ref, stat_ref, turned_ref):
    step = pl.program_id(0)
    block = table_ref.shape[1]
    table = table_ref[...]
    chunk = 256
    first = step == 0
    for start in range(0, rows_ref.shape[0], chunk):
        part = pl.ds(start, chunk)
        column = lax.broadcasted_iota(jnp.int32, (chunk, block), 1) + step * block
        logits = mm(rows_ref[part, :], table) * scale
        logits = jnp.where(column < vocab, logits, MASKED_OUT)
        highest = jnp.max(logits, -1, keepdims=True)
        raised = jnp.exp(logits - highest)
        totals = jnp.sum(raised, -1, keepdims=True)
        prob_ref[part, :] = raised.astype(BF16)
        picked = jnp.sum(jnp.where(column == ids_ref[part, :], logits, 0.0), -1, keepdims=True)
        stats = jnp.where(first, 0.0, stat_ref[part, :])
        old_high = jnp.where(first, MASKED_OUT, stats[:, STAT : STAT + 1])
        old_total = stats[:, STAT + 1 : STAT + 2]
        old_picked = stats[:, STAT + 2 : STAT + 3]
        new_high = jnp.maximum(old_high, highest)
        new_total = old_total * jnp.exp(old_high - new_high) + totals * jnp.exp(highest - new_high)
        lane = lax.broadcasted_iota(jnp.int32, (chunk, LANES), 1)
        stats = jnp.where(lane == step, highest, stats)
        stats = jnp.where(lane == STAT, new_high, stats)
        stats = jnp.where(lane == STAT + 1, new_total, stats)
        stat_ref[part, :] = jnp.where(lane == STAT + 2, old_picked + picked, stats)

    @pl.when(step == pl.num_programs(0) - 1)
    def _():
        turned_ref[...] = stat_ref[...].T[STAT : STAT + TURNED]


def head_forward(rows, table, ids, scale):
    count, width = rows.shape
    vocab = table.shape[1]
    steps = pl.cdiv(vocab, VOCAB_BLOCK)
    return pl.pallas_call(
        functools.partial(head_kernel, vocab, scale),
        out_shape=(
            jax.ShapeDtypeStruct((count, vocab), BF16),
            jax.ShapeDtypeStruct((count, LANES), F32),
            jax.ShapeDtypeStruct((TURNED, count), F32),
        ),
        grid=(steps,),
        in_specs=[
            pl.BlockSpec((count, width), lambda j: (0, 0)),
            pl.BlockSpec((width, VOCAB_BLOCK), lambda j: (0, j)),
            pl.BlockSpec((count, 1), lambda j: (0, 0)),
        ],
        out_specs=(
            pl.BlockSpec((count, VOCAB_BLOCK), lambda j: (0, j)),
            pl.BlockSpec((count, LANES), lambda j: (0, 0)),
            pl.BlockSpec((TURNED, count), lambda j: (0, 0)),
        ),
        compiler_params=params(),
        cost_estimate=pl.CostEstimate(
            flops=2 * count * width * vocab,
            transcendentals=count * vocab,
            bytes_accessed=2 * (count + width) * vocab + 2 * count * width,
        ),
        name="head_forward",
    )(rows, table, ids)


def combine_kernel(stat_ref, share_refs, info_ref, coef_ref, loss_ref):
    count = stat_ref.shape[0]
    shares = [ref[...] for ref in share_refs]
    highest = functools.reduce(jnp.maximum, [share[0:1] for share in shares])
    totals = sum(share[1:2] * jnp.exp(share[0:1] - highest) for share in shares)
    picked = sum(share[2:3] for share in shares)
    log_totals = highest + jnp.log(totals)
    info = info_ref[...]
    loss_ref[...] = jnp.broadcast_to((log_totals - picked) * info[1:2], (TURNED, count))
    row = lax.broadcasted_iota(jnp.int32, (LANES, count), 0)
    wide = jnp.where(row == 0, log_totals, jnp.where(row == 1, info[0:1], info[2:3]))
    turned = wide.T
    weight = turned[:, 1:2]
    lane = lax.broadcasted_iota(jnp.int32, (count, LANES), 1)
    coef = weight * jnp.exp(jnp.minimum(stat_ref[...] - turned[:, 0:1], 0.0))
    coef = jnp.where(lane == WEIGHT_LANE, weight, coef)
    coef_ref[...] = jnp.where(lane == ID_LANE, turned[:, 2:3], coef)


def combine(stats, shares, info):
    count = stats.shape[0]

    def kernel(stat_ref, *refs):
        combine_kernel(stat_ref, refs[: len(shares)], *refs[len(shares) :])

    return pl.pallas_call(
        kernel,
        out_shape=(
            jax.ShapeDtypeStruct((count, LANES), F32),
            jax.ShapeDtypeStruct((TURNED, count), F32),
        ),
        compiler_params=pltpu.CompilerParams(vmem_limit_bytes=VMEM_LIMIT),
        cost_estimate=pl.CostEstimate(
            flops=10 * count * LANES, transcendentals=count * LANES, bytes_accessed=8 * count * LANES
        ),
        name="combine",
    )(stats, *shares, info)


def logit_grads(vocab, step, prob_ref, coef_ref):
    prob = prob_ref[...].astype(F32)
    coef = coef_ref[...]
    lane = lax.broadcasted_iota(jnp.int32, coef.shape, 1)
    factor = jnp.sum(jnp.where(lane == step, coef, 0.0), -1, keepdims=True)
    weight = coef[:, WEIGHT_LANE : WEIGHT_LANE + 1]
    ids = coef[:, ID_LANE : ID_LANE + 1].astype(jnp.int32)
    column = lax.broadcasted_iota(jnp.int32, prob.shape, 1) + step * prob.shape[1]
    grads = prob * factor - jnp.where(column == ids, weight, 0.0)
    return jnp.where(column < vocab, grads, 0.0).astype(BF16)


def table_grad_kernel(vocab, parts, *refs):
    step = pl.program_id(0)
    total = 0.0
    for i in range(parts):
        turned_ref, prob_ref, coef_ref = refs[3 * i : 3 * i + 3]
        total = total + mm(turned_ref[...], logit_grads(vocab, step, prob_ref, coef_ref))
    refs[-1][...] = total.astype(refs[-1].dtype)


def table_grad(parts):
    width = parts[0][0].shape[0]
    vocab = parts[0][1].shape[1]
    steps = pl.cdiv(vocab, VOCAB_BLOCK)
    count = sum(part[0].shape[1] for part in parts)
    specs, operands = [], []
    for turned, prob, coef in parts:
        rows = turned.shape[1]
        specs += [
            pl.BlockSpec((width, rows), lambda j: (0, 0)),
            pl.BlockSpec((rows, VOCAB_BLOCK), lambda j: (0, j)),
            pl.BlockSpec((rows, LANES), lambda j: (0, 0)),
        ]
        operands += [turned, prob, coef]
    return pl.pallas_call(
        functools.partial(table_grad_kernel, vocab, len(parts)),
        out_shape=jax.ShapeDtypeStruct((width, vocab), BF16),
        grid=(steps,),
        in_specs=specs,
        out_specs=pl.BlockSpec((width, VOCAB_BLOCK), lambda j: (0, j)),
        compiler_params=params(),
        cost_estimate=pl.CostEstimate(
            flops=2 * count * width * vocab,
            transcendentals=0,
            bytes_accessed=2 * (count + width) * vocab + 2 * count * width,
        ),
        name="table_grad",
    )(*operands)


def row_grad_kernel(vocab, table_ref, prob_ref, coef_ref, out_ref):
    step = pl.program_id(0)
    grads = logit_grads(vocab, step, prob_ref, coef_ref)
    table = table_ref[...]
    column = lax.broadcasted_iota(jnp.int32, table.shape, 1) + step * table.shape[1]
    table = jnp.where(column < vocab, table, jnp.zeros_like(table))
    terms = mm_nt(grads, table)

    @pl.when(step == 0)
    def _():
        out_ref[...] = terms

    @pl.when(step > 0)
    def _():
        out_ref[...] += terms


def row_grad(table, prob, coef):
    width = table.shape[0]
    count, vocab = prob.shape
    steps = pl.cdiv(vocab, VOCAB_BLOCK)
    return pl.pallas_call(
        functools.partial(row_grad_kernel, vocab),
        out_shape=jax.ShapeDtypeStruct((count, width), F32),
        grid=(steps,),
        in_specs=[
            pl.BlockSpec((width, VOCAB_BLOCK), lambda j: (0, j)),
            pl.BlockSpec((count, VOCAB_BLOCK), lambda j: (0, j)),
            pl.BlockSpec((count, LANES), lambda j: (0, 0)),
        ],
        out_specs=pl.BlockSpec((count, width), lambda j: (0, 0)),
        compiler_params=params(),
        cost_estimate=pl.CostEstimate(
            flops=2 * count * width * vocab,
            transcendentals=0,
            bytes_accessed=2 * (count + width) * vocab + 4 * count * width,
        ),
        name="row_grad",
    )(table, prob, coef)


def gelu_tanh(values):
    return (
        0.5 * values * (1.0 + jnp.tanh(GELU_SCALE * (values + 0.044715 * values * values * values)))
    )


def gated_unit(gate_in, up_in):
    return gelu_tanh(gate_in) * up_in


def norm_rows(values, gain_vec):
    inverse = lax.rsqrt(jnp.mean(values * values, -1, keepdims=True) + EPSILON)
    return (values * inverse * gain_vec, inverse)


def norm_back(values, inverse, gain_vec, upstream):
    scaled = upstream * gain_vec
    inner_sum = jnp.mean(scaled * values, -1, keepdims=True)
    d_values = inverse * scaled - values * (inverse * inverse * inverse) * inner_sum
    d_gain = jnp.sum(upstream * values * inverse, axis=0)
    return (d_values, d_gain)


def swap(values, step):
    return lax.ppermute(values, "mp", [(i, i ^ step) for i in range(4)])


def gather_batch(values, axis):
    return lax.all_gather(values, "batch", axis=axis, tiled=True)


def scatter_batch(values, axis):
    return lax.psum_scatter(values, "batch", scatter_dimension=axis, tiled=True)


def after(values, earlier):
    return lax.optimization_barrier((values, earlier))[0]


def both_slices(weights):
    return jnp.concatenate([weights, swap(weights, 2)], axis=-1)


def own_slice(grads):
    cut = grads.shape[-1] // 2
    return grads[..., :cut].astype(F32) + swap(grads[..., cut:], 2).astype(F32)


def local(
    hidden_in,
    memory,
    tgt_len,
    src_len,
    target_ids,
    task_ids,
    task_weight,
    gain_self,
    q_self,
    k_self,
    v_self,
    o_self,
    gain_cross,
    q_cross,
    k_cross,
    v_cross,
    o_cross,
    gain_mlp,
    mlp_gate,
    mlp_up,
    mlp_down,
    gain_exit,
    embed_table,
):
    place = lax.axis_index("mp")
    pair = place // 2
    lower = pair == 0
    others = [place, place ^ 2, place ^ 1, place ^ 3]
    block = hidden_in.shape[1]
    own_rows = 2 * block
    width = hidden_in.shape[2]
    vocab = embed_table.shape[1]

    def of_pair(values):
        return jnp.where(lower, values[0], values[1])

    def of_other(values):
        return jnp.where(lower, values[1], values[0])

    def pair_rows(values):
        mine, other = of_pair(values), of_other(values)
        return [mine, swap(other, 2), swap(mine, 1), swap(other, 3)]

    def placed(own, far):
        far = swap(far.astype(BF16), 2).astype(own.dtype)
        return jnp.stack([jnp.where(lower, own, far), jnp.where(lower, far, own)])

    self_part = both_slices(jnp.stack([q_self, k_self, v_self, o_self]))
    w_self = gather_batch(self_part, 1)
    cross_part = both_slices(jnp.stack([q_cross, k_cross, v_cross, o_cross]))
    w_cross = gather_batch(after(cross_part, w_self), 1)
    mlp_part = both_slices(jnp.stack([mlp_gate, mlp_up, mlp_down]))
    gains = lax.all_gather(jnp.stack([gain_self, gain_cross, gain_mlp, gain_exit]), "batch", axis=1, tiled=True)
    gain_self, gain_cross, gain_mlp, gain_exit = (gains[i].astype(F32) for i in range(4))

    pair_tgt = jnp.where(lower, tgt_len[0], tgt_len[1])
    pair_src = jnp.where(lower, src_len[0], src_len[1])
    self_scal = jnp.stack(others + [pair_tgt]).astype(jnp.int32)
    cross_scal = jnp.stack(others + [pair_src]).astype(jnp.int32)

    pieces = pair_rows(hidden_in)
    all_in = jnp.concatenate(pieces, axis=0).astype(F32)
    residual = all_in[:own_rows]
    normed_one, inverse_one = norm_rows(all_in, gain_self)
    rows_one = normed_one.astype(BF16)
    q_one = mm(rows_one, w_self[0]).astype(BF16)
    k_one = mm(rows_one, w_self[1]).astype(BF16)
    v_one = mm(rows_one, w_self[2]).astype(BF16)
    mixed_one, lse_one = attend(self_scal, q_one, k_one, v_one, True)

    def gather_pair(own):
        return jnp.concatenate([own, swap(own, 1)], axis=0)

    def reduce_pair(terms):
        return terms[:own_rows] + swap(terms[own_rows:].astype(BF16), 1).astype(F32)

    w_mlp = gather_batch(after(mlp_part, (w_cross, mixed_one)), 1)
    residual_one = residual + reduce_pair(mm_nt(mixed_one, w_self[3]))

    memory_rows = jnp.concatenate(pair_rows(memory), axis=0)
    k_two = mm(memory_rows, w_cross[1]).astype(BF16)
    v_two = mm(memory_rows, w_cross[2]).astype(BF16)
    normed_two, inverse_two = norm_rows(residual_one, gain_cross)
    rows_two = gather_pair(normed_two.astype(BF16))
    q_two = mm(rows_two, w_cross[0]).astype(BF16)
    mixed_two, lse_two = attend(cross_scal, q_two, k_two, v_two, False)
    table = gather_batch(after(embed_table, (w_mlp, mixed_two)), 0)
    residual_two = residual_one + reduce_pair(mm_nt(mixed_two, w_cross[3]))

    normed_three, inverse_three = norm_rows(residual_two, gain_mlp)
    rows_three = gather_pair(normed_three.astype(BF16))
    gate = mm(rows_three, w_mlp[0])
    up_proj = mm(rows_three, w_mlp[1])
    hidden = gated_unit(gate, up_proj).astype(BF16)
    residual_three = residual_two + reduce_pair(mm_nt(hidden, w_mlp[2]))
    finished = residual_three.astype(BF16)
    block_out = placed(finished[:block], finished[block:])

    normed_four, inverse_four = norm_rows(residual_three, gain_exit)
    own_four = normed_four.astype(BF16)
    near_four = jnp.concatenate([own_four, swap(own_four, 1)], axis=0)
    far_four = jnp.concatenate([swap(own_four, 2), swap(own_four, 3)], axis=0)
    slot_blocks = [
        (of, other)
        for of, order in ((pair, others), (1 - pair, [others[i] for i in (1, 0, 3, 2)]))
        for other in order
    ]
    row_order = jnp.stack([of * 4 + other for of, other in slot_blocks])
    ids = target_ids.reshape(8, block)[row_order].reshape(8 * block)
    local_ids = ids - place * vocab
    local_ids = jnp.where((local_ids >= 0) & (local_ids < vocab), local_ids, -1)
    positions = (
        jnp.stack([other * block for _, other in slot_blocks])[:, None] + jnp.arange(block)[None, :]
    ).reshape(8 * block)
    slot_pair = jnp.repeat(jnp.stack([pair, 1 - pair]), 4 * block)
    lengths = jnp.where(slot_pair == 0, tgt_len[0], tgt_len[1])
    valid = (positions < lengths).astype(F32)
    tasks = task_weight.shape[0]
    task_scale = jnp.sum(
        jnp.where(task_ids[:, None] == jnp.arange(tasks)[None, :], task_weight[None, :], 0.0), -1
    )
    logit_scale = width ** (-0.5)
    row_scale = jnp.where(slot_pair == 0, task_scale[0], task_scale[1]) * valid * logit_scale

    info = jnp.stack([row_scale, valid, local_ids.astype(F32)])
    info = jnp.concatenate([info, jnp.zeros((TURNED - 3, info.shape[1]), F32)])
    half_rows = 2 * own_rows
    near_prob, near_stats, near_turned = head_forward(
        near_four, table, local_ids[:half_rows, None], logit_scale
    )
    far_prob, far_stats, far_turned = head_forward(
        far_four, table, local_ids[half_rows:, None], logit_scale
    )
    mine = jnp.concatenate([near_turned, far_turned], axis=1)
    shares = [mine]
    for step in (1, 2, 3):
        moved = swap(mine, step)
        shares.append(
            jnp.concatenate(
                [
                    moved[:, (slot ^ step) * own_rows : ((slot ^ step) + 1) * own_rows]
                    for slot in range(4)
                ],
                axis=1,
            )
        )
    coef, losses = combine(jnp.concatenate([near_stats, far_stats]), shares, info)
    half_sums = jnp.sum(losses[0].reshape(2, half_rows), -1)
    pair_sums = jnp.where(lower, half_sums, half_sums[::-1])
    pair_loss = pair_sums / tgt_len.astype(F32)

    near_coef, far_coef = coef[:half_rows], coef[half_rows:]
    far_rows_grad = row_grad(table, far_prob, far_coef)
    table_terms = table_grad(
        [(near_four.T, near_prob, after(near_coef, far_rows_grad)), (far_four.T, far_prob, far_coef)]
    )
    embed_sum = scatter_batch(table_terms, 0)
    near_rows_grad = row_grad(table, near_prob, after(near_coef, table_terms))
    d_four = near_rows_grad[:own_rows]
    for step, part in (
        (2, far_rows_grad[:own_rows]),
        (3, far_rows_grad[own_rows:]),
        (1, near_rows_grad[own_rows:]),
    ):
        d_four = d_four + swap(part.astype(BF16), step).astype(F32)
    d_residual, exit_grad = norm_back(residual_three, inverse_four, gain_exit, d_four)

    d_branch = gather_pair(d_residual.astype(BF16))
    d_hidden = mm(d_branch, w_mlp[2])
    _, pullback = jax.vjp(gated_unit, gate, up_proj)
    d_gate, d_up = pullback(d_hidden)
    d_gate = d_gate.astype(BF16)
    d_up = d_up.astype(BF16)
    d_rows = reduce_pair(mm_nt(d_gate, w_mlp[0]) + mm_nt(d_up, w_mlp[1]))
    late_three, late_branch = after((rows_three, d_branch), embed_sum)
    mlp_grads = [mm_tn(late_three, d_gate), mm_tn(late_three, d_up), mm_tn(late_branch, hidden)]
    mlp_scattered = scatter_batch(jnp.stack(mlp_grads).astype(BF16), 1)
    mlp_sum = own_slice(mlp_scattered)
    d_input, mlp_grad = norm_back(residual_two, inverse_three, gain_mlp, d_rows)
    d_residual = d_residual + d_input

    d_branch = gather_pair(d_residual.astype(BF16))
    d_mixed = mm(d_branch, w_cross[3]).astype(BF16)
    out_grad = mm_tn(d_branch, mixed_two)
    d_q, d_k, d_v = attend_back(cross_scal, q_two, k_two, v_two, lse_two, d_mixed, False)
    d_rows = reduce_pair(mm_nt(d_q, w_cross[0]))
    memory_terms = mm_nt(d_k, w_cross[1]) + mm_nt(d_v, w_cross[2])
    half = memory_terms.shape[0] // 2
    memory_own = memory_terms[:half] + swap(memory_terms[half:].astype(BF16), 1).astype(F32)
    memory_grad = placed(memory_own[: half // 2], memory_own[half // 2 :])
    cross_grads = [
        mm_tn(rows_two, d_q),
        mm_tn(memory_rows, d_k),
        mm_tn(memory_rows, d_v),
        out_grad,
    ]
    d_input, cross_grad = norm_back(residual_one, inverse_two, gain_cross, d_rows)
    d_residual = d_residual + d_input

    d_branch = gather_pair(d_residual.astype(BF16))
    d_mixed = mm(d_branch, w_self[3]).astype(BF16)
    out_grad = mm_tn(d_branch, mixed_one)
    d_q, d_k, d_v = attend_back(self_scal, q_one, k_one, v_one, lse_one, d_mixed, True)
    d_terms = mm_nt(d_q, w_self[0]) + mm_nt(d_k, w_self[1]) + mm_nt(d_v, w_self[2])
    d_rows = reduce_pair(d_terms)
    self_grad = jnp.sum(d_terms * (all_in * inverse_one), axis=0)
    d_input, _ = norm_back(residual, inverse_one[:own_rows], gain_self, d_rows)
    late_one = after(rows_one, mlp_scattered)
    self_grads = [mm_tn(late_one, d_q), mm_tn(late_one, d_k), mm_tn(late_one, d_v), out_grad]
    gain_grads = jnp.stack([self_grad, cross_grad, mlp_grad, exit_grad], axis=1)
    gain_slab = jnp.pad(gain_grads, ((0, 0), (0, d_q.shape[1] - 4)))
    last_sum = scatter_batch(jnp.stack(self_grads + cross_grads + [gain_slab]).astype(BF16), 1)
    last_split = own_slice(last_sum[:8])
    self_sum, cross_sum = last_split[:4], last_split[4:]
    gain_own = last_sum[8, :, :LANES]
    gain_sums = gain_own.astype(F32) + sum(swap(gain_own, step).astype(F32) for step in (1, 2, 3))
    d_residual = d_residual + d_input
    hidden_grad = placed(d_residual[:block], d_residual[block:])

    return (
        block_out,
        pair_loss,
        hidden_grad,
        memory_grad,
        gain_sums[:, 0],
        self_sum[0],
        self_sum[1],
        self_sum[2],
        self_sum[3],
        gain_sums[:, 1],
        cross_sum[0],
        cross_sum[1],
        cross_sum[2],
        cross_sum[3],
        gain_sums[:, 2],
        mlp_sum[0],
        mlp_sum[1],
        mlp_sum[2],
        gain_sums[:, 3],
        embed_sum.astype(F32),
    )


def solution(mesh):
    assert mesh.shape["mp"] == 4
    rows = P("batch", "mp", None)
    vector = P("batch")
    matrix = P("batch", "mp")
    sub = (vector, matrix, matrix, matrix, matrix)
    mlp = (vector, matrix, matrix, matrix)
    weights = sub + sub + mlp + (vector, matrix)
    in_specs = (rows, rows, vector, vector, P("batch", None), vector, P()) + weights
    out_specs = (rows, vector, rows, rows) + weights
    return jax.shard_map(local, mesh=mesh, in_specs=in_specs, out_specs=out_specs, check_vma=False)
```

```python
import functools

import jax
import jax.numpy as jnp
from jax import lax
from jax.experimental import pallas as pl
from jax.experimental.pallas import tpu as pltpu
from jax.sharding import PartitionSpec as P

DH = 64
LANES = 128
EPSILON = 1e-06
MASKED_OUT = -1000000000.0
GELU_SCALE = 0.7978845608028654
VMEM_LIMIT = 56 * 1024 * 1024
VOCAB_BLOCK = 2048
HIDDEN_BLOCK = 256
LOG2_E = 1.4426950408889634
BF16 = jnp.bfloat16
F32 = jnp.float32


def params():
    return pltpu.CompilerParams(
        dimension_semantics=("arbitrary",), vmem_limit_bytes=VMEM_LIMIT
    )


def mm(a, b):
    return lax.dot_general(a, b, (((1,), (0,)), ((), ())), preferred_element_type=F32)


def mm_nt(a, b):
    return lax.dot_general(a, b, (((1,), (1,)), ((), ())), preferred_element_type=F32)


def mm_tn(a, b):
    return lax.dot_general(a, b, (((0,), (0,)), ((), ())), preferred_element_type=F32)


def block_positions(scal_ref, size, dim):
    shape = (size, 1) if dim == 0 else (1, size)
    pieces = [lax.broadcasted_iota(jnp.int32, shape, dim) + scal_ref[i] * size for i in range(4)]
    return jnp.concatenate(pieces, axis=dim)


def score_bias(scal_ref, rows, keys, causal):
    key_pos = block_positions(scal_ref, keys // 4, 1)
    allowed = key_pos < scal_ref[4]
    if causal:
        row_pos = block_positions(scal_ref, rows // 4, 0)
        allowed = allowed & (key_pos <= row_pos)
    return jnp.where(allowed, 0.0, MASKED_OUT)


def head_lanes(rows, head):
    lane = lax.broadcasted_iota(jnp.int32, (rows, LANES), 1)
    return (lane < DH) if head == 0 else (lane >= DH)


def attend_heads(q, k, v, bias):
    rows = q.shape[0]
    outs, lses = [], []
    for head in range(2):
        q_head = jnp.where(head_lanes(rows, head), q, jnp.zeros_like(q))
        scores = mm_nt(q_head, k) + bias
        highest = jnp.max(scores, -1, keepdims=True)
        raised = jnp.exp(scores - highest)
        totals = jnp.sum(raised, -1, keepdims=True)
        outs.append(mm(raised.astype(BF16), v) * (1.0 / totals))
        lses.append(highest + jnp.log(totals))
    first = head_lanes(rows, 0)
    return jnp.where(first, outs[0], outs[1]).astype(BF16), jnp.where(first, lses[0], lses[1])


def attend_heads_back(q, k, v, lse, d_out, bias):
    rows, keys = q.shape[0], k.shape[0]
    dqs, dks, dvs = [], [], []
    for head in range(2):
        mine = head_lanes(rows, head)
        q_head = jnp.where(mine, q, jnp.zeros_like(q))
        d_head = jnp.where(mine, d_out, jnp.zeros_like(d_out))
        weights = jnp.exp(mm_nt(q_head, k) + bias - lse[:, head * DH : head * DH + 1])
        d_weights = mm_nt(d_head, v)
        inner = jnp.sum(weights * d_weights, -1, keepdims=True)
        d_scores = (weights * (d_weights - inner)).astype(BF16)
        dqs.append(mm(d_scores, k))
        dks.append(mm_tn(d_scores, q))
        dvs.append(mm_tn(weights.astype(BF16), d_out))
    first = head_lanes(keys, 0)
    return (
        jnp.where(head_lanes(rows, 0), dqs[0], dqs[1]).astype(BF16),
        jnp.where(first, dks[0], dks[1]).astype(BF16),
        jnp.where(first, dvs[0], dvs[1]).astype(BF16),
    )


def leave(total, own_ref, other_ref):
    @pl.when(pl.program_id(0) == pl.num_programs(0) - 1)
    def _():
        half = own_ref.shape[0]
        own_ref[...] = total[:half, :]
        other_ref[...] = total[half:, :].astype(BF16)


def stack_rows(own_ref, other_ref, rows):
    half = own_ref.shape[0]
    rows[:half, :] = own_ref[...]
    rows[half:, :] = other_ref[...]


def whole(shape):
    return pl.BlockSpec(shape, lambda j, *_: (0,) * len(shape))


def columns(rows, block):
    return pl.BlockSpec((rows, block), lambda j, *_: (0, j))


def weight_block(count, place, width, block):
    return pl.BlockSpec((count, width, block), lambda j, *_: (place, 0, j))


def sized(shape, dtype):
    return jax.ShapeDtypeStruct(shape, dtype)


def sublayer(kernel, name, scal, operands, specs, outs, out_specs, scratch, steps, flops, moved):
    return pl.pallas_call(
        kernel,
        out_shape=outs,
        grid_spec=pltpu.PrefetchScalarGridSpec(
            num_scalar_prefetch=1,
            grid=(steps,),
            in_specs=specs,
            out_specs=out_specs,
            scratch_shapes=scratch,
        ),
        compiler_params=params(),
        cost_estimate=pl.CostEstimate(flops=flops, transcendentals=0, bytes_accessed=moved),
        name=name,
    )(scal, *operands)


def self_forward_kernel(
    scal_ref, *refs
):
    pieces, (gain_ref, w_ref) = refs[:4], refs[4:6]
    q_ref, k_ref, v_ref, mixed_ref, lse_ref, rows_ref, own_ref, other_ref, total, bias = refs[6:]
    count = rows_ref.shape[0]

    @pl.when(pl.program_id(0) == 0)
    def _():
        size = pieces[0].shape[0]
        for i, piece in enumerate(pieces):
            normed, _ = norm_rows(piece[...].astype(F32), gain_ref[...])
            rows_ref[i * size : (i + 1) * size, :] = normed.astype(BF16)
        bias[...] = score_bias(scal_ref, count, count, True)
        total[...] = jnp.zeros_like(total)

    rows = rows_ref[...]
    q_ref[...] = mm(rows, w_ref[0]).astype(BF16)
    k_ref[...] = mm(rows, w_ref[1]).astype(BF16)
    v_ref[...] = mm(rows, w_ref[2]).astype(BF16)
    mixed, lse_ref[...] = attend_heads(q_ref[...], k_ref[...], v_ref[...], bias[...])
    mixed_ref[...] = mixed
    total[...] += mm_nt(mixed, w_ref[3])
    leave(total, own_ref, other_ref)


def self_forward(scal, pieces, gain, weights):
    block, width = pieces[0].shape
    count, cols = 4 * block, weights.shape[2]
    half = count // 2
    narrow = sized((count, cols), BF16)
    return sublayer(
        self_forward_kernel,
        "self_forward",
        scal,
        (*pieces, gain, weights),
        [whole((block, width))] * 4 + [whole((1, width)), weight_block(4, 0, width, LANES)],
        (narrow, narrow, narrow, narrow, sized((count, cols), F32))
        + (sized((count, width), BF16), sized((half, width), F32), sized((half, width), BF16)),
        [columns(count, LANES)] * 5
        + [whole((count, width)), whole((half, width)), whole((half, width))],
        [pltpu.VMEM((count, width), F32), pltpu.VMEM((count, count), F32)],
        cols // LANES,
        8 * count * width * cols + 8 * count * count * cols,
        8 * width * cols + 12 * count * cols + 8 * count * width,
    )


def cross_forward_kernel(
    scal_ref, h_own_ref, h_other_ref, w_ref, k_ref, v_ref,
    q_ref, mixed_ref, lse_ref, own_ref, other_ref, rows, total,
):
    @pl.when(pl.program_id(0) == 0)
    def _():
        stack_rows(h_own_ref, h_other_ref, rows)
        total[...] = jnp.zeros_like(total)

    bias = score_bias(scal_ref, rows.shape[0], k_ref.shape[0], False)
    q_ref[...] = mm(rows[...], w_ref[0]).astype(BF16)
    mixed, lse_ref[...] = attend_heads(q_ref[...], k_ref[...], v_ref[...], bias)
    mixed_ref[...] = mixed
    total[...] += mm_nt(mixed, w_ref[3])
    leave(total, own_ref, other_ref)


def cross_forward(scal, own, other, weights, k, v):
    half, width = own.shape
    count, cols, keys = 2 * half, weights.shape[2], k.shape[0]
    return sublayer(
        cross_forward_kernel,
        "cross_forward",
        scal,
        (own, other, weights, k, v),
        [whole((half, width))] * 2
        + [weight_block(4, 1, width, LANES), columns(keys, LANES), columns(keys, LANES)],
        (sized((count, cols), BF16), sized((count, cols), BF16), sized((count, cols), F32))
        + (sized((half, width), F32), sized((half, width), BF16)),
        [columns(count, LANES)] * 3 + [whole((half, width))] * 2,
        [pltpu.VMEM((count, width), BF16), pltpu.VMEM((count, width), F32)],
        cols // LANES,
        4 * count * width * cols + 8 * count * keys * cols,
        8 * width * cols + 8 * count * cols + 4 * keys * cols + 8 * count * width,
    )


def mlp_forward_kernel(
    scal_ref, h_own_ref, h_other_ref, w_ref,
    gate_ref, up_ref, hidden_ref, own_ref, other_ref, rows, total,
):
    @pl.when(pl.program_id(0) == 0)
    def _():
        stack_rows(h_own_ref, h_other_ref, rows)
        total[...] = jnp.zeros_like(total)

    gate = mm(rows[...], w_ref[0])
    up = mm(rows[...], w_ref[1])
    hidden = gated_unit(gate, up).astype(BF16)
    gate_ref[...] = gate
    up_ref[...] = up
    hidden_ref[...] = hidden
    total[...] += mm_nt(hidden, w_ref[2])
    leave(total, own_ref, other_ref)


def mlp_forward(scal, own, other, weights):
    half, width = own.shape
    count, cols = 2 * half, weights.shape[2]
    return sublayer(
        mlp_forward_kernel,
        "mlp_forward",
        scal,
        (own, other, weights),
        [whole((half, width))] * 2 + [weight_block(3, 0, width, HIDDEN_BLOCK)],
        (sized((count, cols), F32), sized((count, cols), F32), sized((count, cols), BF16))
        + (sized((half, width), F32), sized((half, width), BF16)),
        [columns(count, HIDDEN_BLOCK)] * 3 + [whole((half, width))] * 2,
        [pltpu.VMEM((count, width), BF16), pltpu.VMEM((count, width), F32)],
        cols // HIDDEN_BLOCK,
        6 * count * width * cols,
        6 * width * cols + 10 * count * cols + 5 * count * width,
    )


def mlp_back_kernel(
    scal_ref, e_own_ref, e_other_ref, w_ref, gate_ref, up_ref,
    d_gate_ref, d_up_ref, own_ref, other_ref, rows, total,
):
    @pl.when(pl.program_id(0) == 0)
    def _():
        stack_rows(e_own_ref, e_other_ref, rows)
        total[...] = jnp.zeros_like(total)

    d_hidden = mm(rows[...], w_ref[2])
    gate, up = gate_ref[...], up_ref[...]
    inner = GELU_SCALE * (gate + 0.044715 * gate * gate * gate)
    bent = jnp.tanh(inner)
    slope = GELU_SCALE * (1.0 + 3.0 * 0.044715 * gate * gate)
    d_gelu = 0.5 * (1.0 + bent) + 0.5 * gate * (1.0 - bent * bent) * slope
    d_gate = (d_hidden * up * d_gelu).astype(BF16)
    d_up = (d_hidden * (0.5 * gate * (1.0 + bent))).astype(BF16)
    d_gate_ref[...] = d_gate
    d_up_ref[...] = d_up
    total[...] += mm_nt(d_gate, w_ref[0]) + mm_nt(d_up, w_ref[1])
    leave(total, own_ref, other_ref)


def mlp_back(scal, own, other, weights, gate, up):
    half, width = own.shape
    count, cols = 2 * half, weights.shape[2]
    return sublayer(
        mlp_back_kernel,
        "mlp_back",
        scal,
        (own, other, weights, gate, up),
        [whole((half, width))] * 2
        + [weight_block(3, 0, width, HIDDEN_BLOCK)]
        + [columns(count, HIDDEN_BLOCK)] * 2,
        (sized((count, cols), BF16), sized((count, cols), BF16))
        + (sized((half, width), F32), sized((half, width), BF16)),
        [columns(count, HIDDEN_BLOCK)] * 2 + [whole((half, width))] * 2,
        [pltpu.VMEM((count, width), BF16), pltpu.VMEM((count, width), F32)],
        cols // HIDDEN_BLOCK,
        6 * count * width * cols,
        6 * width * cols + 12 * count * cols + 5 * count * width,
    )


def mlp_grads_kernel(
    scal_ref, h_own_ref, h_other_ref, e_own_ref, e_other_ref, d_gate_ref, d_up_ref, hidden_ref,
    out_ref,
):
    half = h_own_ref.shape[0]
    for i, (own, other, d_ref) in enumerate(
        (
            (h_own_ref, h_other_ref, d_gate_ref),
            (h_own_ref, h_other_ref, d_up_ref),
            (e_own_ref, e_other_ref, hidden_ref),
        )
    ):
        terms = mm_tn(own[...], d_ref[:half, :]) + mm_tn(other[...], d_ref[half:, :])
        out_ref[i] = terms.astype(BF16)


def mlp_grads(scal, rows, branch, d_gate, d_up, hidden):
    half, width = rows[0].shape
    count, cols = hidden.shape
    return sublayer(
        mlp_grads_kernel,
        "mlp_grads",
        scal,
        (*rows, *branch, d_gate, d_up, hidden),
        [whole((half, width))] * 4 + [columns(count, HIDDEN_BLOCK)] * 3,
        sized((3, width, cols), BF16),
        weight_block(3, 0, width, HIDDEN_BLOCK),
        [],
        cols // HIDDEN_BLOCK,
        6 * count * width * cols,
        6 * width * cols + 6 * count * cols + 4 * count * width,
    )


def attention_back_kernel(
    causal, scal_ref, e_own_ref, e_other_ref, w_ref, q_ref, k_ref, v_ref, lse_ref,
    dq_ref, dk_ref, dv_ref, own_ref, other_ref, gain_ref, rows, total, bias, *pieces,
):
    @pl.when(pl.program_id(0) == 0)
    def _():
        stack_rows(e_own_ref, e_other_ref, rows)
        total[...] = jnp.zeros_like(total)
        bias[...] = score_bias(scal_ref, rows.shape[0], k_ref.shape[0], causal)

    d_mixed = mm(rows[...], w_ref[3]).astype(BF16)
    dq, dk, dv = attend_heads_back(
        q_ref[...], k_ref[...], v_ref[...], lse_ref[...], d_mixed, bias[...]
    )
    dq_ref[...] = dq
    dk_ref[...] = dk
    dv_ref[...] = dv
    terms = mm_nt(dq, w_ref[0])
    if causal:
        terms += mm_nt(dk, w_ref[1]) + mm_nt(dv, w_ref[2])
    total[...] += terms
    leave(total, own_ref, other_ref)

    if causal:
        @pl.when(pl.program_id(0) == pl.num_programs(0) - 1)
        def _():
            size = pieces[0].shape[0]
            summed = 0.0
            for i, piece in enumerate(pieces):
                values = piece[...].astype(F32)
                unit, _ = norm_rows(values, 1.0)
                part = total[i * size : (i + 1) * size, :] * unit
                summed = summed + jnp.sum(part, 0, keepdims=True)
            gain_ref[...] = jnp.broadcast_to(summed, gain_ref.shape)


def cross_back(scal, own, other, weights, q, k, v, lse):
    half, width = own.shape
    count, cols, keys = 2 * half, weights.shape[2], k.shape[0]

    def kernel(scal_ref, *refs):
        attention_back_kernel(False, scal_ref, *refs[:12], None, *refs[12:])

    return sublayer(
        kernel,
        "cross_back",
        scal,
        (own, other, weights, q, k, v, lse),
        [whole((half, width))] * 2
        + [weight_block(4, 1, width, LANES), columns(count, LANES)]
        + [columns(keys, LANES)] * 2
        + [columns(count, LANES)],
        (sized((count, cols), BF16), sized((keys, cols), BF16), sized((keys, cols), BF16))
        + (sized((half, width), F32), sized((half, width), BF16)),
        [columns(count, LANES), columns(keys, LANES), columns(keys, LANES)]
        + [whole((half, width))] * 2,
        [
            pltpu.VMEM((count, width), BF16),
            pltpu.VMEM((count, width), F32),
            pltpu.VMEM((1, keys), F32),
        ],
        cols // LANES,
        4 * count * width * cols + 20 * count * keys * cols,
        8 * width * cols + 8 * count * cols + 8 * keys * cols + 8 * count * width,
    )


def self_back(scal, own, other, weights, q, k, v, lse, pieces):
    half, width = own.shape
    count, cols = 2 * half, weights.shape[2]
    block = pieces[0].shape[0]

    def kernel(scal_ref, *refs):
        attention_back_kernel(True, scal_ref, *refs[:7], *refs[11:], *refs[7:11])

    narrow = sized((count, cols), BF16)
    return sublayer(
        kernel,
        "self_back",
        scal,
        (own, other, weights, q, k, v, lse, *pieces),
        [whole((half, width))] * 2
        + [weight_block(4, 0, width, LANES)]
        + [columns(count, LANES)] * 4
        + [whole((block, width))] * 4,
        (narrow, narrow, narrow, sized((half, width), F32), sized((half, width), BF16))
        + (sized((8, width), F32),),
        [columns(count, LANES)] * 3 + [whole((half, width))] * 2 + [whole((8, width))],
        [
            pltpu.VMEM((count, width), BF16),
            pltpu.VMEM((count, width), F32),
            pltpu.VMEM((count, count), F32),
        ],
        cols // LANES,
        8 * count * width * cols + 20 * count * count * cols,
        8 * width * cols + 20 * count * cols + 10 * count * width,
    )


def cross_grads_kernel(
    scal_ref, h_own, h_other, e_own, e_other, memory, dq, dk, dv, mixed, out_ref
):
    half = e_own.shape[0]

    def whole_grad(rows, d_ref):
        return mm_tn(rows[...], d_ref[...]).astype(BF16)

    def split_grad(own, other, d_ref):
        return (mm_tn(own[...], d_ref[:half, :]) + mm_tn(other[...], d_ref[half:, :])).astype(BF16)

    out_ref[0] = split_grad(h_own, h_other, dq)
    out_ref[1] = whole_grad(memory, dk)
    out_ref[2] = whole_grad(memory, dv)
    out_ref[3] = split_grad(e_own, e_other, mixed)


def cross_grads(scal, rows, branch, memory, narrow):
    half, width = rows[0].shape
    cols, keys = narrow[0].shape[1], memory.shape[0]
    return sublayer(
        cross_grads_kernel,
        "cross_grads",
        scal,
        (*rows, *branch, memory, *narrow),
        [whole((half, width))] * 4
        + [whole((keys, width))]
        + [columns(array.shape[0], LANES) for array in narrow],
        sized((8, width, cols), BF16),
        weight_block(4, 1, width, LANES),
        [],
        cols // LANES,
        (8 * half + 4 * keys) * width * cols,
        8 * width * cols + (8 * half + 4 * keys) * cols + 8 * half * width,
    )


def self_grads_kernel(scal_ref, h, e_own, e_other, dq, dk, dv, mixed, rest_ref, out_ref):
    half = e_own.shape[0]
    for i, d_ref in enumerate((dq, dk, dv)):
        out_ref[i] = mm_tn(h[...], d_ref[...]).astype(BF16)
    terms = mm_tn(e_own[...], mixed[:half, :]) + mm_tn(e_other[...], mixed[half:, :])
    out_ref[3] = terms.astype(BF16)


def self_grads(scal, rows, branch, narrow, rest):
    count, width = rows.shape
    cols = narrow[0].shape[1]
    return pl.pallas_call(
        self_grads_kernel,
        out_shape=sized(rest.shape, BF16),
        grid_spec=pltpu.PrefetchScalarGridSpec(
            num_scalar_prefetch=1,
            grid=(cols // LANES,),
            in_specs=[whole((count, width))]
            + [whole((count // 2, width))] * 2
            + [columns(count, LANES)] * 4
            + [pl.BlockSpec(memory_space=pl.ANY)],
            out_specs=weight_block(4, 0, width, LANES),
        ),
        input_output_aliases={8: 0},
        compiler_params=params(),
        cost_estimate=pl.CostEstimate(
            flops=8 * count * width * cols,
            transcendentals=0,
            bytes_accessed=8 * width * cols + 8 * count * cols + 4 * count * width,
        ),
        name="self_grads",
    )(scal, rows, *branch, *narrow, rest)


SUMS = 32
PICKS = 64
WEIGHT_LANE = 126
ID_LANE = 127
TURNED = 8


def column_bias(vocab, step, block):
    column = lax.broadcasted_iota(jnp.int32, (1, block), 1) + step * block
    return jnp.where(column < vocab, 0.0, MASKED_OUT)


def head_kernel(vocab, scale, rows_ref, table_ref, ids_ref, prob_ref, stat_ref, turned_ref):
    step = pl.program_id(0)
    block = table_ref.shape[1]
    table = table_ref[...]
    chunk = 128
    bias = column_bias(vocab, step, block)
    column = lax.broadcasted_iota(jnp.int32, (1, block), 1)
    lane = lax.broadcasted_iota(jnp.int32, (chunk, LANES), 1)
    for start in range(0, rows_ref.shape[0], chunk):
        part = pl.ds(start, chunk)
        products = mm(rows_ref[part, :], table) + bias
        highest = jnp.max(products, -1, keepdims=True)
        raised = jnp.exp2((products - highest) * (scale * LOG2_E))
        prob_ref[part, :] = raised.astype(BF16)
        totals = jnp.sum(raised, -1, keepdims=True)
        target = ids_ref[part, :] - step * block
        picked = jnp.sum(jnp.where(column == target, products, 0.0), -1, keepdims=True)
        stats = jnp.where(step == 0, 0.0, stat_ref[part, :])
        stats = jnp.where(lane == step, highest * scale, stats)
        stats = jnp.where(lane == SUMS + step, totals, stats)
        stat_ref[part, :] = jnp.where(lane == PICKS + step, picked * scale, stats)

    @pl.when(step == pl.num_programs(0) - 1)
    def _():
        stats = stat_ref[...].T
        steps = pl.num_programs(0)
        row = lax.broadcasted_iota(jnp.int32, (SUMS, stats.shape[1]), 0)
        tops = jnp.where(row < steps, stats[:SUMS], MASKED_OUT)
        highest = jnp.max(tops, 0, keepdims=True)
        totals = jnp.sum(stats[SUMS:PICKS] * jnp.exp(tops - highest), 0, keepdims=True)
        picked = jnp.sum(stats[PICKS : PICKS + SUMS], 0, keepdims=True)
        row = lax.broadcasted_iota(jnp.int32, (TURNED, stats.shape[1]), 0)
        turned_ref[...] = jnp.where(row == 0, highest, jnp.where(row == 1, totals, picked))


def head_forward(rows, table, ids, scale):
    count, width = rows.shape
    vocab = table.shape[1]
    steps = pl.cdiv(vocab, VOCAB_BLOCK)
    return pl.pallas_call(
        functools.partial(head_kernel, vocab, scale),
        out_shape=(
            jax.ShapeDtypeStruct((count, vocab), BF16),
            jax.ShapeDtypeStruct((count, LANES), F32),
            jax.ShapeDtypeStruct((TURNED, count), F32),
        ),
        grid=(steps,),
        in_specs=[
            pl.BlockSpec((count, width), lambda j: (0, 0)),
            pl.BlockSpec((width, VOCAB_BLOCK), lambda j: (0, j)),
            pl.BlockSpec((count, 1), lambda j: (0, 0)),
        ],
        out_specs=(
            pl.BlockSpec((count, VOCAB_BLOCK), lambda j: (0, j)),
            pl.BlockSpec((count, LANES), lambda j: (0, 0)),
            pl.BlockSpec((TURNED, count), lambda j: (0, 0)),
        ),
        compiler_params=params(),
        cost_estimate=pl.CostEstimate(
            flops=2 * count * width * vocab,
            transcendentals=count * vocab,
            bytes_accessed=2 * (count + width) * vocab + 2 * count * width,
        ),
        name="head_forward",
    )(rows, table, ids)


def combine_kernel(near_stat_ref, far_stat_ref, *refs):
    share_refs, (info_ref, near_ref, far_ref, loss_ref) = refs[:4], refs[4:]
    half = near_stat_ref.shape[0]
    count = 2 * half
    own = count // 4
    shares = [
        jnp.concatenate(
            [ref[:, (slot ^ step) * own : ((slot ^ step) + 1) * own] for slot in range(4)], axis=1
        )
        for step, ref in enumerate(share_refs)
    ]
    highest = functools.reduce(jnp.maximum, [share[0:1] for share in shares])
    totals = sum(share[1:2] * jnp.exp(share[0:1] - highest) for share in shares)
    picked = sum(share[2:3] for share in shares)
    log_totals = highest + jnp.log(totals)
    info = info_ref[...]
    loss_ref[...] = jnp.broadcast_to((log_totals - picked) * info[1:2], (TURNED, count))
    row = lax.broadcasted_iota(jnp.int32, (LANES, count), 0)
    turned = jnp.where(row == 0, log_totals, jnp.where(row == 1, info[0:1], info[2:3])).T
    lane = lax.broadcasted_iota(jnp.int32, (half, LANES), 1)
    for stat_ref, coef_ref, start in ((near_stat_ref, near_ref, 0), (far_stat_ref, far_ref, half)):
        part = turned[start : start + half]
        weight = part[:, 1:2]
        coef = weight * jnp.exp(jnp.minimum(stat_ref[...] - part[:, 0:1], 0.0))
        coef = jnp.where(lane == WEIGHT_LANE, weight, coef)
        coef_ref[...] = jnp.where(lane == ID_LANE, part[:, 2:3], coef)


def combine(near_stats, far_stats, shares, info):
    half = near_stats.shape[0]
    return pl.pallas_call(
        combine_kernel,
        out_shape=(
            sized((half, LANES), F32),
            sized((half, LANES), F32),
            sized((TURNED, 2 * half), F32),
        ),
        compiler_params=pltpu.CompilerParams(vmem_limit_bytes=VMEM_LIMIT),
        cost_estimate=pl.CostEstimate(
            flops=20 * half * LANES,
            transcendentals=2 * half * LANES,
            bytes_accessed=16 * half * LANES,
        ),
        name="combine",
    )(near_stats, far_stats, *shares, info)


def logit_grads(vocab, step, part, prob_ref, coef_ref):
    block = prob_ref.shape[1]
    coef = coef_ref[part, :]
    lane = lax.broadcasted_iota(jnp.int32, coef.shape, 1)
    factor = jnp.sum(jnp.where(lane == step, coef, 0.0), -1, keepdims=True)
    weight = coef[:, WEIGHT_LANE : WEIGHT_LANE + 1]
    target = coef[:, ID_LANE : ID_LANE + 1].astype(jnp.int32) - step * block
    column = lax.broadcasted_iota(jnp.int32, (1, block), 1)
    inside = column < vocab - step * block
    prob = prob_ref[part, :].astype(F32)
    grads = prob * factor - jnp.where(column == target, weight, 0.0)
    return jnp.where(inside, grads, 0.0).astype(BF16)


def table_block(vocab, step, table_ref):
    table = table_ref[...]
    column = lax.broadcasted_iota(jnp.int32, (1, table.shape[1]), 1) + step * table.shape[1]
    return jnp.where(column < vocab, table, jnp.zeros_like(table))


def add_up(step, out_ref, terms):
    @pl.when(step == 0)
    def _():
        out_ref[...] = terms

    @pl.when(step > 0)
    def _():
        out_ref[...] += terms


def rows_grad_kernel(vocab, table_ref, prob_ref, coef_ref, first_ref, second_ref, total):
    step = pl.program_id(0)
    grads = logit_grads(vocab, step, slice(None), prob_ref, coef_ref)
    add_up(step, total, mm_nt(grads, table_block(vocab, step, table_ref)))

    @pl.when(step == pl.num_programs(0) - 1)
    def _():
        half = first_ref.shape[0]
        first_ref[...] = total[:half, :].astype(first_ref.dtype)
        second_ref[...] = total[half:, :].astype(second_ref.dtype)


def rows_grad(table, prob, coef, dtype):
    width = table.shape[0]
    count, vocab = prob.shape
    half = whole((count // 2, width))
    return pl.pallas_call(
        functools.partial(rows_grad_kernel, vocab),
        out_shape=(sized((count // 2, width), dtype), sized((count // 2, width), BF16)),
        grid=(pl.cdiv(vocab, VOCAB_BLOCK),),
        in_specs=[
            columns(width, VOCAB_BLOCK),
            columns(count, VOCAB_BLOCK),
            whole((count, LANES)),
        ],
        out_specs=(half, half),
        scratch_shapes=[pltpu.VMEM((count, width), F32)],
        compiler_params=params(),
        cost_estimate=pl.CostEstimate(
            flops=2 * count * width * vocab,
            transcendentals=0,
            bytes_accessed=2 * (count + width) * vocab + 4 * count * width,
        ),
        name="rows_grad",
    )(table, prob, coef)


def table_grad_kernel(
    vocab, near_rows_ref, near_prob_ref, near_coef_ref, far_rows_ref, far_prob_ref, far_coef_ref, out_ref
):
    step = pl.program_id(0)
    near = logit_grads(vocab, step, slice(None), near_prob_ref, near_coef_ref)
    far = logit_grads(vocab, step, slice(None), far_prob_ref, far_coef_ref)
    out_ref[...] = (mm_tn(near_rows_ref[...], near) + mm_tn(far_rows_ref[...], far)).astype(BF16)


def table_grad(near, far):
    count, width = near[0].shape
    vocab = near[1].shape[1]
    specs = [whole((count, width)), columns(count, VOCAB_BLOCK), whole((count, LANES))]
    return pl.pallas_call(
        functools.partial(table_grad_kernel, vocab),
        out_shape=sized((width, vocab), BF16),
        grid=(pl.cdiv(vocab, VOCAB_BLOCK),),
        in_specs=specs * 2,
        out_specs=columns(width, VOCAB_BLOCK),
        compiler_params=params(),
        cost_estimate=pl.CostEstimate(
            flops=4 * count * width * vocab,
            transcendentals=0,
            bytes_accessed=(4 * count + 2 * width) * vocab + 4 * count * width,
        ),
        name="table_grad",
    )(*near, *far)


def gelu_tanh(values):
    return (
        0.5 * values * (1.0 + jnp.tanh(GELU_SCALE * (values + 0.044715 * values * values * values)))
    )


def gated_unit(gate_in, up_in):
    return gelu_tanh(gate_in) * up_in


def norm_rows(values, gain_vec):
    inverse = lax.rsqrt(jnp.mean(values * values, -1, keepdims=True) + EPSILON)
    return (values * inverse * gain_vec, inverse)


def norm_back(values, inverse, gain_vec, upstream):
    scaled = upstream * gain_vec
    inner_sum = jnp.mean(scaled * values, -1, keepdims=True)
    d_values = inverse * scaled - values * (inverse * inverse * inverse) * inner_sum
    d_gain = jnp.sum(upstream * values * inverse, axis=0)
    return (d_values, d_gain)


def swap(values, step):
    return lax.ppermute(values, "mp", [(i, i ^ step) for i in range(4)])


def total_of_all(values):
    for axis in ("mp", "batch"):
        size, step = lax.axis_size(axis), 1
        while step < size:
            moved = lax.ppermute(values, axis, [(i, i ^ step) for i in range(size)])
            values, step = values + moved, 2 * step
    return values


def gather_batch(values, axis):
    return lax.all_gather(values, "batch", axis=axis, tiled=True)


def scatter_batch(values, axis):
    return lax.psum_scatter(values, "batch", scatter_dimension=axis, tiled=True)


def after(values, earlier):
    return lax.optimization_barrier((values, earlier))[0]


def both_slices(weights):
    return jnp.concatenate([weights, swap(weights, 2)], axis=-1)


def own_slice(grads):
    cut = grads.shape[-1] // 2
    return grads[..., :cut], swap(grads[..., cut:], 2)


def local(
    hidden_in,
    memory,
    tgt_len,
    src_len,
    target_ids,
    task_ids,
    task_weight,
    gain_self,
    q_self,
    k_self,
    v_self,
    o_self,
    gain_cross,
    q_cross,
    k_cross,
    v_cross,
    o_cross,
    gain_mlp,
    mlp_gate,
    mlp_up,
    mlp_down,
    gain_exit,
    embed_table,
):
    place = lax.axis_index("mp")
    pair = place // 2
    lower = pair == 0
    others = [place, place ^ 2, place ^ 1, place ^ 3]
    block = hidden_in.shape[1]
    own_rows = 2 * block
    width = hidden_in.shape[2]
    vocab = embed_table.shape[1]

    def of_pair(values):
        return jnp.where(lower, values[0], values[1])

    def of_other(values):
        return jnp.where(lower, values[1], values[0])

    def pair_rows(values):
        mine, other = of_pair(values), of_other(values)
        second = swap(other, 2)
        return [mine, second, swap(mine, 1), swap(second, 1)]

    def placed(own, received):
        far = received.astype(own.dtype)
        return jnp.stack([jnp.where(lower, own, far), jnp.where(lower, far, own)])

    gain_size = gain_self.shape[0]
    gains = lax.all_gather(
        jnp.stack([gain_self, gain_cross, gain_mlp, gain_exit]), "batch", axis=1, tiled=True
    )
    gain_self, gain_cross, gain_mlp, gain_exit = (gains[i].astype(F32) for i in range(4))
    attention = [q_self, k_self, v_self, o_self, q_cross, k_cross, v_cross, o_cross]
    depth, slim = q_self.shape
    packed = [jnp.concatenate(attention[i : i + 2], axis=1) for i in range(0, 8, 2)]
    moved = swap(jnp.stack(packed), 2)
    w_both = jnp.stack(
        [
            jnp.concatenate([own, moved[i // 2, :, i % 2 * slim : (i % 2 + 1) * slim]], axis=1)
            for i, own in enumerate(attention)
        ]
    )
    w_both = gather_batch(after(w_both, gains), 1)
    own_rows_in = of_pair(hidden_in)
    second = swap(after(of_other(hidden_in), moved), 2)
    pieces = [own_rows_in, second, swap(own_rows_in, 1), swap(second, 1)]
    mlp_part = both_slices(after(jnp.stack([mlp_gate, mlp_up, mlp_down]), second))
    memory_pieces = pair_rows(after(memory, (pieces[2], pieces[3], mlp_part)))

    pair_tgt = jnp.where(lower, tgt_len[0], tgt_len[1])
    pair_src = jnp.where(lower, src_len[0], src_len[1])
    self_scal = jnp.stack(others + [pair_tgt]).astype(jnp.int32)
    cross_scal = jnp.stack(others + [pair_src]).astype(jnp.int32)

    residual = jnp.concatenate(pieces[:2], axis=0).astype(F32)
    q_one, k_one, v_one, mixed_one, lse_one, rows_one, own_terms, other_terms = self_forward(
        self_scal, pieces, gain_self[None], w_both
    )
    memory_rows = jnp.concatenate(memory_pieces, axis=0)
    w_mlp = gather_batch(after(mlp_part, (w_both, pieces, memory_pieces[1])), 1)
    k_two = mm(memory_rows, w_both[5]).astype(BF16)
    v_two = mm(memory_rows, w_both[6]).astype(BF16)
    own_terms = after(own_terms, (k_two, v_two))
    residual_one = residual + own_terms + swap(other_terms, 1).astype(F32)

    normed_two, inverse_two = norm_rows(residual_one, gain_cross)
    own_two = normed_two.astype(BF16)
    rows_two = (own_two, swap(own_two, 1))
    q_two, mixed_two, lse_two, own_terms, other_terms = cross_forward(
        cross_scal, *rows_two, w_both, k_two, v_two
    )
    table = gather_batch(after(embed_table, (w_mlp, rows_two[1])), 0)
    residual_two = residual_one + own_terms + swap(other_terms, 1).astype(F32)

    normed_three, inverse_three = norm_rows(residual_two, gain_mlp)
    own_three = normed_three.astype(BF16)
    rows_three = (own_three, swap(own_three, 1))
    gate, up_proj, hidden, own_terms, other_terms = mlp_forward(self_scal, *rows_three, w_mlp)
    residual_three = residual_two + own_terms + swap(other_terms, 1).astype(F32)
    finished = residual_three.astype(BF16)

    normed_four, inverse_four = norm_rows(residual_three, gain_exit)
    own_four = normed_four.astype(BF16)
    near_four = jnp.concatenate([own_four, swap(own_four, 1)], axis=0)
    far_four = (swap(own_four, 2), swap(own_four, 3))
    slot_blocks = [
        (of, other)
        for of, order in ((pair, others), (1 - pair, [others[i] for i in (1, 0, 3, 2)]))
        for other in order
    ]
    row_order = jnp.stack([of * 4 + other for of, other in slot_blocks])
    ids = target_ids.reshape(8, block)[row_order].reshape(8 * block)
    local_ids = ids - place * vocab
    local_ids = jnp.where((local_ids >= 0) & (local_ids < vocab), local_ids, -1)
    positions = (
        jnp.stack([other * block for _, other in slot_blocks])[:, None] + jnp.arange(block)[None, :]
    ).reshape(8 * block)
    slot_pair = jnp.repeat(jnp.stack([pair, 1 - pair]), 4 * block)
    lengths = jnp.where(slot_pair == 0, tgt_len[0], tgt_len[1])
    valid = (positions < lengths).astype(F32)
    tasks = task_weight.shape[0]
    task_scale = jnp.sum(
        jnp.where(task_ids[:, None] == jnp.arange(tasks)[None, :], task_weight[None, :], 0.0), -1
    )
    logit_scale = width ** (-0.5)
    row_scale = jnp.where(slot_pair == 0, task_scale[0], task_scale[1]) * valid * logit_scale

    info = jnp.stack([row_scale, valid, local_ids.astype(F32)])
    info = jnp.concatenate([info, jnp.zeros((TURNED - 3, info.shape[1]), F32)])
    half_rows = 2 * own_rows
    near_prob, near_stats, near_turned = head_forward(
        near_four, table, local_ids[:half_rows, None], logit_scale
    )
    far_four = jnp.concatenate(after(far_four, near_turned), axis=0)
    far_prob, far_stats, far_turned = head_forward(
        far_four, table, local_ids[half_rows:, None], logit_scale
    )
    mine = jnp.concatenate([near_turned, far_turned], axis=1)
    finished = after(finished, near_turned)
    finished_far = swap(finished[block:], 2)
    block_out = placed(finished[:block], finished_far)
    shares = [mine] + [swap(mine, step) for step in (1, 2, 3)]
    near_coef, far_coef, losses = combine(near_stats, far_stats, shares, info)
    half_sums = jnp.sum(losses[0].reshape(2, half_rows), -1)
    pair_sums = jnp.where(lower, half_sums, half_sums[::-1])
    pair_loss = pair_sums / tgt_len.astype(F32)

    table_terms = table_grad(
        (near_four, near_prob, after(near_coef, finished_far)), (far_four, far_prob, far_coef)
    )
    embed_sum = scatter_batch(table_terms, 0)
    far_two, far_three = rows_grad(table, far_prob, after(far_coef, table_terms), BF16)
    d_own, near_one = rows_grad(table, near_prob, after(near_coef, far_two), F32)
    far_two = swap(far_two, 2)
    d_four = d_own + swap(after(near_one, far_two), 1).astype(F32)
    d_four += far_two.astype(F32) + swap(far_three, 3).astype(F32)
    d_residual, exit_grad = norm_back(residual_three, inverse_four, gain_exit, d_four)

    own_branch = d_residual.astype(BF16)
    branch_three = (own_branch, swap(own_branch, 1))
    d_gate, d_up, own_terms, other_terms = mlp_back(self_scal, *branch_three, w_mlp, gate, up_proj)
    mlp_terms = mlp_grads(self_scal, rows_three, branch_three, d_gate, d_up, hidden)
    d_rows = own_terms + after(swap(other_terms, 1), mlp_terms).astype(F32)
    d_input, mlp_grad = norm_back(residual_two, inverse_three, gain_mlp, d_rows)
    d_residual = d_residual + d_input

    own_branch = d_residual.astype(BF16)
    branch_two = (own_branch, after(swap(own_branch, 1), embed_sum))
    mlp_scattered = scatter_batch(after(mlp_terms, branch_two[1]), 1)
    mlp_here, mlp_moved = own_slice(mlp_scattered)
    mlp_sum = mlp_here.astype(F32) + mlp_moved.astype(F32)
    dq_two, dk_two, dv_two, own_terms, other_terms = cross_back(
        cross_scal, *branch_two, w_both, q_two, k_two, v_two, lse_two
    )
    cross_terms = cross_grads(
        self_scal, rows_two, branch_two, memory_rows, (dq_two, dk_two, dv_two, mixed_two)
    )
    d_rows = own_terms + after(swap(other_terms, 1), cross_terms).astype(F32)
    d_input, cross_grad = norm_back(residual_one, inverse_two, gain_cross, d_rows)
    d_residual = d_residual + d_input

    own_branch = d_residual.astype(BF16)
    memory_terms = mm_nt(dk_two, w_both[5]) + mm_nt(dv_two, w_both[6])
    branch_one = (own_branch, after(swap(own_branch, 1), memory_terms))
    half = memory_terms.shape[0] // 2
    memory_sent = after(memory_terms[half:].astype(BF16), branch_one[1])
    memory_received = swap(memory_sent, 1)
    memory_own = memory_terms[:half] + memory_received.astype(F32)
    dq_one, dk_one, dv_one, own_terms, other_terms, self_grad = self_back(
        self_scal, *branch_one, w_both, q_one, k_one, v_one, lse_one, pieces
    )
    last_grads = self_grads(
        self_scal,
        after(rows_one, (mlp_scattered, memory_received)),
        branch_one,
        (dq_one, dk_one, dv_one, mixed_one),
        cross_terms,
    )
    last_sum = scatter_batch(last_grads, 1)
    memory_far = swap(memory_own[half // 2 :].astype(BF16), 2)
    memory_grad = placed(memory_own[: half // 2], memory_far)
    received = after(swap(other_terms, 1), (last_grads, mlp_moved))
    d_rows = own_terms + received.astype(F32)
    d_input, _ = norm_back(residual, norm_rows(residual, 1.0)[1], gain_self, d_rows)
    d_residual = d_residual + d_input
    hidden_far = swap(after(d_residual[block:].astype(BF16), memory_far), 2)
    hidden_grad = placed(d_residual[:block], hidden_far)
    gain_grads = jnp.stack([self_grad[0], cross_grad, mlp_grad, exit_grad])
    gain_grads = total_of_all(after(gain_grads, received))
    gain_sums = lax.dynamic_slice_in_dim(
        gain_grads, lax.axis_index("batch") * gain_size, gain_size, axis=1
    )
    sent = last_sum[..., slim:]
    moved = swap(jnp.concatenate([sent[:4], sent[4:]], axis=-1), 2)
    self_sum = last_sum[:4, :, :slim].astype(F32) + moved[..., :slim].astype(F32)
    cross_sum = last_sum[4:, :, :slim].astype(F32) + moved[..., slim:].astype(F32)
    return (
        block_out,
        pair_loss,
        hidden_grad,
        memory_grad,
        gain_sums[0],
        self_sum[0],
        self_sum[1],
        self_sum[2],
        self_sum[3],
        gain_sums[1],
        cross_sum[0],
        cross_sum[1],
        cross_sum[2],
        cross_sum[3],
        gain_sums[2],
        mlp_sum[0],
        mlp_sum[1],
        mlp_sum[2],
        gain_sums[3],
        embed_sum.astype(F32),
    )


def solution(mesh):
    assert mesh.shape["mp"] == 4
    rows = P("batch", "mp", None)
    vector = P("batch")
    matrix = P("batch", "mp")
    sub = (vector, matrix, matrix, matrix, matrix)
    mlp = (vector, matrix, matrix, matrix)
    weights = sub + sub + mlp + (vector, matrix)
    in_specs = (rows, rows, vector, vector, P("batch", None), vector, P()) + weights
    out_specs = (rows, vector, rows, rows) + weights
    return jax.shard_map(local, mesh=mesh, in_specs=in_specs, out_specs=out_specs, check_vma=False)
```

```python
import functools

import jax
import jax.numpy as jnp
from jax import lax
from jax.experimental import pallas as pl
from jax.experimental.pallas import tpu as pltpu
from jax.sharding import PartitionSpec as P

DH = 64
LANES = 128
EPSILON = 1e-06
MASKED_OUT = -1000000000.0
GELU_SCALE = 0.7978845608028654
VMEM_LIMIT = 56 * 1024 * 1024
VOCAB_BLOCK = 2048
HIDDEN_BLOCK = 256
LOG2_E = 1.4426950408889634
BF16 = jnp.bfloat16
F32 = jnp.float32


def params():
    return pltpu.CompilerParams(
        dimension_semantics=("arbitrary",), vmem_limit_bytes=VMEM_LIMIT
    )


def mm(a, b):
    return lax.dot_general(a, b, (((1,), (0,)), ((), ())), preferred_element_type=F32)


def mm_nt(a, b):
    return lax.dot_general(a, b, (((1,), (1,)), ((), ())), preferred_element_type=F32)


def mm_tn(a, b):
    return lax.dot_general(a, b, (((0,), (0,)), ((), ())), preferred_element_type=F32)


def block_positions(scal_ref, size, dim):
    shape = (size, 1) if dim == 0 else (1, size)
    pieces = [lax.broadcasted_iota(jnp.int32, shape, dim) + scal_ref[i] * size for i in range(4)]
    return jnp.concatenate(pieces, axis=dim)


def score_bias(scal_ref, rows, keys, causal):
    key_pos = block_positions(scal_ref, keys // 4, 1)
    allowed = key_pos < scal_ref[4]
    if causal:
        row_pos = block_positions(scal_ref, rows // 4, 0)
        allowed = allowed & (key_pos <= row_pos)
    return jnp.where(allowed, 0.0, MASKED_OUT)


def head_lanes(rows, head):
    lane = lax.broadcasted_iota(jnp.int32, (rows, LANES), 1)
    return (lane < DH) if head == 0 else (lane >= DH)


def attend_heads(q, k, v, bias):
    rows = q.shape[0]
    outs, lses = [], []
    for head in range(2):
        q_head = jnp.where(head_lanes(rows, head), q, jnp.zeros_like(q))
        scores = mm_nt(q_head, k) + bias
        highest = jnp.max(scores, -1, keepdims=True)
        raised = jnp.exp(scores - highest)
        totals = jnp.sum(raised, -1, keepdims=True)
        outs.append(mm(raised.astype(BF16), v) * (1.0 / totals))
        lses.append(highest + jnp.log(totals))
    first = head_lanes(rows, 0)
    return jnp.where(first, outs[0], outs[1]).astype(BF16), jnp.where(first, lses[0], lses[1])


def attend_heads_back(q, k, v, lse, d_out, bias):
    rows, keys = q.shape[0], k.shape[0]
    dqs, dks, dvs = [], [], []
    for head in range(2):
        mine = head_lanes(rows, head)
        q_head = jnp.where(mine, q, jnp.zeros_like(q))
        d_head = jnp.where(mine, d_out, jnp.zeros_like(d_out))
        weights = jnp.exp(mm_nt(q_head, k) + bias - lse[:, head * DH : head * DH + 1])
        d_weights = mm_nt(d_head, v)
        inner = jnp.sum(weights * d_weights, -1, keepdims=True)
        d_scores = (weights * (d_weights - inner)).astype(BF16)
        dqs.append(mm(d_scores, k))
        dks.append(mm_tn(d_scores, q))
        dvs.append(mm_tn(weights.astype(BF16), d_out))
    first = head_lanes(keys, 0)
    return (
        jnp.where(head_lanes(rows, 0), dqs[0], dqs[1]).astype(BF16),
        jnp.where(first, dks[0], dks[1]).astype(BF16),
        jnp.where(first, dvs[0], dvs[1]).astype(BF16),
    )


def leave(total, own_ref, other_ref):
    @pl.when(pl.program_id(0) == pl.num_programs(0) - 1)
    def _():
        half = own_ref.shape[0]
        own_ref[...] = total[:half, :]
        other_ref[...] = total[half:, :].astype(BF16)


def stack_rows(own_ref, other_ref, rows):
    half = own_ref.shape[0]
    rows[:half, :] = own_ref[...]
    rows[half:, :] = other_ref[...]


def whole(shape):
    return pl.BlockSpec(shape, lambda j, *_: (0,) * len(shape))


def columns(rows, block):
    return pl.BlockSpec((rows, block), lambda j, *_: (0, j))


def weight_block(count, place, width, block):
    return pl.BlockSpec((count, width, block), lambda j, *_: (place, 0, j))


def sized(shape, dtype):
    return jax.ShapeDtypeStruct(shape, dtype)


def sublayer(kernel, name, scal, operands, specs, outs, out_specs, scratch, steps, flops, moved):
    return pl.pallas_call(
        kernel,
        out_shape=outs,
        grid_spec=pltpu.PrefetchScalarGridSpec(
            num_scalar_prefetch=1,
            grid=(steps,),
            in_specs=specs,
            out_specs=out_specs,
            scratch_shapes=scratch,
        ),
        compiler_params=params(),
        cost_estimate=pl.CostEstimate(flops=flops, transcendentals=0, bytes_accessed=moved),
        name=name,
    )(scal, *operands)


def self_forward_kernel(
    scal_ref, *refs
):
    pieces, (gain_ref, w_ref) = refs[:4], refs[4:6]
    q_ref, k_ref, v_ref, mixed_ref, lse_ref, rows_ref, own_ref, other_ref, total, bias = refs[6:]
    count = rows_ref.shape[0]

    @pl.when(pl.program_id(0) == 0)
    def _():
        size = pieces[0].shape[0]
        for i, piece in enumerate(pieces):
            normed, _ = norm_rows(piece[...].astype(F32), gain_ref[...])
            rows_ref[i * size : (i + 1) * size, :] = normed.astype(BF16)
        bias[...] = score_bias(scal_ref, count, count, True)
        total[...] = jnp.zeros_like(total)

    rows = rows_ref[...]
    q_ref[...] = mm(rows, w_ref[0]).astype(BF16)
    k_ref[...] = mm(rows, w_ref[1]).astype(BF16)
    v_ref[...] = mm(rows, w_ref[2]).astype(BF16)
    mixed, lse_ref[...] = attend_heads(q_ref[...], k_ref[...], v_ref[...], bias[...])
    mixed_ref[...] = mixed
    total[...] += mm_nt(mixed, w_ref[3])
    leave(total, own_ref, other_ref)


def self_forward(scal, pieces, gain, weights):
    block, width = pieces[0].shape
    count, cols = 4 * block, weights.shape[2]
    half = count // 2
    narrow = sized((count, cols), BF16)
    return sublayer(
        self_forward_kernel,
        "self_forward",
        scal,
        (*pieces, gain, weights),
        [whole((block, width))] * 4 + [whole((1, width)), weight_block(4, 0, width, LANES)],
        (narrow, narrow, narrow, narrow, sized((count, cols), F32))
        + (sized((count, width), BF16), sized((half, width), F32), sized((half, width), BF16)),
        [columns(count, LANES)] * 5
        + [whole((count, width)), whole((half, width)), whole((half, width))],
        [pltpu.VMEM((count, width), F32), pltpu.VMEM((count, count), F32)],
        cols // LANES,
        8 * count * width * cols + 8 * count * count * cols,
        8 * width * cols + 12 * count * cols + 8 * count * width,
    )


def cross_forward_kernel(
    scal_ref, h_own_ref, h_other_ref, w_ref, k_ref, v_ref,
    q_ref, mixed_ref, lse_ref, own_ref, other_ref, rows, total,
):
    @pl.when(pl.program_id(0) == 0)
    def _():
        stack_rows(h_own_ref, h_other_ref, rows)
        total[...] = jnp.zeros_like(total)

    bias = score_bias(scal_ref, rows.shape[0], k_ref.shape[0], False)
    q_ref[...] = mm(rows[...], w_ref[0]).astype(BF16)
    mixed, lse_ref[...] = attend_heads(q_ref[...], k_ref[...], v_ref[...], bias)
    mixed_ref[...] = mixed
    total[...] += mm_nt(mixed, w_ref[3])
    leave(total, own_ref, other_ref)


def cross_forward(scal, own, other, weights, k, v):
    half, width = own.shape
    count, cols, keys = 2 * half, weights.shape[2], k.shape[0]
    return sublayer(
        cross_forward_kernel,
        "cross_forward",
        scal,
        (own, other, weights, k, v),
        [whole((half, width))] * 2
        + [weight_block(4, 1, width, LANES), columns(keys, LANES), columns(keys, LANES)],
        (sized((count, cols), BF16), sized((count, cols), BF16), sized((count, cols), F32))
        + (sized((half, width), F32), sized((half, width), BF16)),
        [columns(count, LANES)] * 3 + [whole((half, width))] * 2,
        [pltpu.VMEM((count, width), BF16), pltpu.VMEM((count, width), F32)],
        cols // LANES,
        4 * count * width * cols + 8 * count * keys * cols,
        8 * width * cols + 8 * count * cols + 4 * keys * cols + 8 * count * width,
    )


def mlp_forward_kernel(
    scal_ref, h_own_ref, h_other_ref, w_ref,
    gate_ref, up_ref, hidden_ref, own_ref, other_ref, rows, total,
):
    @pl.when(pl.program_id(0) == 0)
    def _():
        stack_rows(h_own_ref, h_other_ref, rows)
        total[...] = jnp.zeros_like(total)

    gate = mm(rows[...], w_ref[0])
    up = mm(rows[...], w_ref[1])
    hidden = gated_unit(gate, up).astype(BF16)
    gate_ref[...] = gate
    up_ref[...] = up
    hidden_ref[...] = hidden
    total[...] += mm_nt(hidden, w_ref[2])
    leave(total, own_ref, other_ref)


def mlp_forward(scal, own, other, weights):
    half, width = own.shape
    count, cols = 2 * half, weights.shape[2]
    return sublayer(
        mlp_forward_kernel,
        "mlp_forward",
        scal,
        (own, other, weights),
        [whole((half, width))] * 2 + [weight_block(3, 0, width, HIDDEN_BLOCK)],
        (sized((count, cols), F32), sized((count, cols), F32), sized((count, cols), BF16))
        + (sized((half, width), F32), sized((half, width), BF16)),
        [columns(count, HIDDEN_BLOCK)] * 3 + [whole((half, width))] * 2,
        [pltpu.VMEM((count, width), BF16), pltpu.VMEM((count, width), F32)],
        cols // HIDDEN_BLOCK,
        6 * count * width * cols,
        6 * width * cols + 10 * count * cols + 5 * count * width,
    )


def mlp_back_kernel(
    scal_ref, e_own_ref, e_other_ref, w_ref, gate_ref, up_ref,
    d_gate_ref, d_up_ref, own_ref, other_ref, rows, total,
):
    @pl.when(pl.program_id(0) == 0)
    def _():
        stack_rows(e_own_ref, e_other_ref, rows)
        total[...] = jnp.zeros_like(total)

    d_hidden = mm(rows[...], w_ref[2])
    gate, up = gate_ref[...], up_ref[...]
    inner = GELU_SCALE * (gate + 0.044715 * gate * gate * gate)
    bent = jnp.tanh(inner)
    slope = GELU_SCALE * (1.0 + 3.0 * 0.044715 * gate * gate)
    d_gelu = 0.5 * (1.0 + bent) + 0.5 * gate * (1.0 - bent * bent) * slope
    d_gate = (d_hidden * up * d_gelu).astype(BF16)
    d_up = (d_hidden * (0.5 * gate * (1.0 + bent))).astype(BF16)
    d_gate_ref[...] = d_gate
    d_up_ref[...] = d_up
    total[...] += mm_nt(d_gate, w_ref[0]) + mm_nt(d_up, w_ref[1])
    leave(total, own_ref, other_ref)


def mlp_back(scal, own, other, weights, gate, up):
    half, width = own.shape
    count, cols = 2 * half, weights.shape[2]
    return sublayer(
        mlp_back_kernel,
        "mlp_back",
        scal,
        (own, other, weights, gate, up),
        [whole((half, width))] * 2
        + [weight_block(3, 0, width, HIDDEN_BLOCK)]
        + [columns(count, HIDDEN_BLOCK)] * 2,
        (sized((count, cols), BF16), sized((count, cols), BF16))
        + (sized((half, width), F32), sized((half, width), BF16)),
        [columns(count, HIDDEN_BLOCK)] * 2 + [whole((half, width))] * 2,
        [pltpu.VMEM((count, width), BF16), pltpu.VMEM((count, width), F32)],
        cols // HIDDEN_BLOCK,
        6 * count * width * cols,
        6 * width * cols + 12 * count * cols + 5 * count * width,
    )


def mlp_grads_kernel(
    scal_ref, h_own_ref, h_other_ref, e_own_ref, e_other_ref, d_gate_ref, d_up_ref, hidden_ref,
    out_ref,
):
    half = h_own_ref.shape[0]
    for i, (own, other, d_ref) in enumerate(
        (
            (h_own_ref, h_other_ref, d_gate_ref),
            (h_own_ref, h_other_ref, d_up_ref),
            (e_own_ref, e_other_ref, hidden_ref),
        )
    ):
        terms = mm_tn(own[...], d_ref[:half, :]) + mm_tn(other[...], d_ref[half:, :])
        out_ref[i] = terms.astype(BF16)


def mlp_grads(scal, rows, branch, d_gate, d_up, hidden):
    half, width = rows[0].shape
    count, cols = hidden.shape
    return sublayer(
        mlp_grads_kernel,
        "mlp_grads",
        scal,
        (*rows, *branch, d_gate, d_up, hidden),
        [whole((half, width))] * 4 + [columns(count, HIDDEN_BLOCK)] * 3,
        sized((3, width, cols), BF16),
        weight_block(3, 0, width, HIDDEN_BLOCK),
        [],
        cols // HIDDEN_BLOCK,
        6 * count * width * cols,
        6 * width * cols + 6 * count * cols + 4 * count * width,
    )


def attention_back_kernel(
    causal, scal_ref, e_own_ref, e_other_ref, w_ref, q_ref, k_ref, v_ref, lse_ref,
    dq_ref, dk_ref, dv_ref, own_ref, other_ref, gain_ref, rows, total, bias, *pieces,
):
    @pl.when(pl.program_id(0) == 0)
    def _():
        stack_rows(e_own_ref, e_other_ref, rows)
        total[...] = jnp.zeros_like(total)
        bias[...] = score_bias(scal_ref, rows.shape[0], k_ref.shape[0], causal)

    d_mixed = mm(rows[...], w_ref[3]).astype(BF16)
    dq, dk, dv = attend_heads_back(
        q_ref[...], k_ref[...], v_ref[...], lse_ref[...], d_mixed, bias[...]
    )
    dq_ref[...] = dq
    dk_ref[...] = dk
    dv_ref[...] = dv
    terms = mm_nt(dq, w_ref[0])
    if causal:
        terms += mm_nt(dk, w_ref[1]) + mm_nt(dv, w_ref[2])
    total[...] += terms
    leave(total, own_ref, other_ref)

    if causal:
        @pl.when(pl.program_id(0) == pl.num_programs(0) - 1)
        def _():
            size = pieces[0].shape[0]
            summed = 0.0
            for i, piece in enumerate(pieces):
                values = piece[...].astype(F32)
                unit, _ = norm_rows(values, 1.0)
                part = total[i * size : (i + 1) * size, :] * unit
                summed = summed + jnp.sum(part, 0, keepdims=True)
            gain_ref[...] = jnp.broadcast_to(summed, gain_ref.shape)


def cross_back(scal, own, other, weights, q, k, v, lse):
    half, width = own.shape
    count, cols, keys = 2 * half, weights.shape[2], k.shape[0]

    def kernel(scal_ref, *refs):
        attention_back_kernel(False, scal_ref, *refs[:12], None, *refs[12:])

    return sublayer(
        kernel,
        "cross_back",
        scal,
        (own, other, weights, q, k, v, lse),
        [whole((half, width))] * 2
        + [weight_block(4, 1, width, LANES), columns(count, LANES)]
        + [columns(keys, LANES)] * 2
        + [columns(count, LANES)],
        (sized((count, cols), BF16), sized((keys, cols), BF16), sized((keys, cols), BF16))
        + (sized((half, width), F32), sized((half, width), BF16)),
        [columns(count, LANES), columns(keys, LANES), columns(keys, LANES)]
        + [whole((half, width))] * 2,
        [
            pltpu.VMEM((count, width), BF16),
            pltpu.VMEM((count, width), F32),
            pltpu.VMEM((1, keys), F32),
        ],
        cols // LANES,
        4 * count * width * cols + 20 * count * keys * cols,
        8 * width * cols + 8 * count * cols + 8 * keys * cols + 8 * count * width,
    )


def self_back(scal, own, other, weights, q, k, v, lse, pieces):
    half, width = own.shape
    count, cols = 2 * half, weights.shape[2]
    block = pieces[0].shape[0]

    def kernel(scal_ref, *refs):
        attention_back_kernel(True, scal_ref, *refs[:7], *refs[11:], *refs[7:11])

    narrow = sized((count, cols), BF16)
    return sublayer(
        kernel,
        "self_back",
        scal,
        (own, other, weights, q, k, v, lse, *pieces),
        [whole((half, width))] * 2
        + [weight_block(4, 0, width, LANES)]
        + [columns(count, LANES)] * 4
        + [whole((block, width))] * 4,
        (narrow, narrow, narrow, sized((half, width), F32), sized((half, width), BF16))
        + (sized((8, width), F32),),
        [columns(count, LANES)] * 3 + [whole((half, width))] * 2 + [whole((8, width))],
        [
            pltpu.VMEM((count, width), BF16),
            pltpu.VMEM((count, width), F32),
            pltpu.VMEM((count, count), F32),
        ],
        cols // LANES,
        8 * count * width * cols + 20 * count * count * cols,
        8 * width * cols + 20 * count * cols + 10 * count * width,
    )


def cross_grads_kernel(scal_ref, h_own, h_other, e_own, e_other, *refs):
    memory, (dq, dk, dv, mixed, out_ref) = refs[:4], refs[4:]
    half = e_own.shape[0]

    def memory_grad(d_ref):
        size = memory[0].shape[0]
        terms = [mm_tn(m[...], d_ref[i * size : (i + 1) * size, :]) for i, m in enumerate(memory)]
        return sum(terms).astype(BF16)

    def split_grad(own, other, d_ref):
        return (mm_tn(own[...], d_ref[:half, :]) + mm_tn(other[...], d_ref[half:, :])).astype(BF16)

    out_ref[0] = split_grad(h_own, h_other, dq)
    out_ref[1] = memory_grad(dk)
    out_ref[2] = memory_grad(dv)
    out_ref[3] = split_grad(e_own, e_other, mixed)


def cross_grads(scal, rows, branch, memory, narrow):
    half, width = rows[0].shape
    cols, keys = narrow[0].shape[1], narrow[1].shape[0]
    return sublayer(
        cross_grads_kernel,
        "cross_grads",
        scal,
        (*rows, *branch, *memory, *narrow),
        [whole((half, width))] * 4
        + [whole((keys // 4, width))] * 4
        + [columns(array.shape[0], LANES) for array in narrow],
        sized((8, width, cols), BF16),
        weight_block(4, 1, width, LANES),
        [],
        cols // LANES,
        (8 * half + 4 * keys) * width * cols,
        8 * width * cols + (8 * half + 4 * keys) * cols + 8 * half * width,
    )


def self_grads_kernel(scal_ref, h, e_own, e_other, dq, dk, dv, mixed, rest_ref, out_ref):
    half = e_own.shape[0]
    for i, d_ref in enumerate((dq, dk, dv)):
        out_ref[i] = mm_tn(h[...], d_ref[...]).astype(BF16)
    terms = mm_tn(e_own[...], mixed[:half, :]) + mm_tn(e_other[...], mixed[half:, :])
    out_ref[3] = terms.astype(BF16)


def self_grads(scal, rows, branch, narrow, rest):
    count, width = rows.shape
    cols = narrow[0].shape[1]
    return pl.pallas_call(
        self_grads_kernel,
        out_shape=sized(rest.shape, BF16),
        grid_spec=pltpu.PrefetchScalarGridSpec(
            num_scalar_prefetch=1,
            grid=(cols // LANES,),
            in_specs=[whole((count, width))]
            + [whole((count // 2, width))] * 2
            + [columns(count, LANES)] * 4
            + [pl.BlockSpec(memory_space=pl.ANY)],
            out_specs=weight_block(4, 0, width, LANES),
        ),
        input_output_aliases={8: 0},
        compiler_params=params(),
        cost_estimate=pl.CostEstimate(
            flops=8 * count * width * cols,
            transcendentals=0,
            bytes_accessed=8 * width * cols + 8 * count * cols + 4 * count * width,
        ),
        name="self_grads",
    )(scal, rows, *branch, *narrow, rest)


SUMS = 32
PICKS = 64
WEIGHT_LANE = 126
ID_LANE = 127
TURNED = 8


def column_bias(vocab, step, block):
    column = lax.broadcasted_iota(jnp.int32, (1, block), 1) + step * block
    return jnp.where(column < vocab, 0.0, MASKED_OUT)


def head_kernel(vocab, scale, rows_ref, table_ref, ids_ref, prob_ref, stat_ref, turned_ref):
    step = pl.program_id(0)
    block = table_ref.shape[1]
    table = table_ref[...]
    chunk = 128
    bias = column_bias(vocab, step, block)
    column = lax.broadcasted_iota(jnp.int32, (1, block), 1)
    lane = lax.broadcasted_iota(jnp.int32, (chunk, LANES), 1)
    for start in range(0, rows_ref.shape[0], chunk):
        part = pl.ds(start, chunk)
        products = mm(rows_ref[part, :], table) + bias
        highest = jnp.max(products, -1, keepdims=True)
        raised = jnp.exp2((products - highest) * (scale * LOG2_E))
        prob_ref[part, :] = raised.astype(BF16)
        totals = jnp.sum(raised, -1, keepdims=True)
        target = ids_ref[part, :] - step * block
        picked = jnp.sum(jnp.where(column == target, products, 0.0), -1, keepdims=True)
        stats = jnp.where(step == 0, 0.0, stat_ref[part, :])
        stats = jnp.where(lane == step, highest * scale, stats)
        stats = jnp.where(lane == SUMS + step, totals, stats)
        stat_ref[part, :] = jnp.where(lane == PICKS + step, picked * scale, stats)

    @pl.when(step == pl.num_programs(0) - 1)
    def _():
        stats = stat_ref[...].T
        steps = pl.num_programs(0)
        row = lax.broadcasted_iota(jnp.int32, (SUMS, stats.shape[1]), 0)
        tops = jnp.where(row < steps, stats[:SUMS], MASKED_OUT)
        highest = jnp.max(tops, 0, keepdims=True)
        totals = jnp.sum(stats[SUMS:PICKS] * jnp.exp(tops - highest), 0, keepdims=True)
        picked = jnp.sum(stats[PICKS : PICKS + SUMS], 0, keepdims=True)
        row = lax.broadcasted_iota(jnp.int32, (TURNED, stats.shape[1]), 0)
        turned_ref[...] = jnp.where(row == 0, highest, jnp.where(row == 1, totals, picked))


def head_forward(rows, table, ids, scale):
    count, width = rows.shape
    vocab = table.shape[1]
    steps = pl.cdiv(vocab, VOCAB_BLOCK)
    return pl.pallas_call(
        functools.partial(head_kernel, vocab, scale),
        out_shape=(
            jax.ShapeDtypeStruct((count, vocab), BF16),
            jax.ShapeDtypeStruct((count, LANES), F32),
            jax.ShapeDtypeStruct((TURNED, count), F32),
        ),
        grid=(steps,),
        in_specs=[
            pl.BlockSpec((count, width), lambda j: (0, 0)),
            pl.BlockSpec((width, VOCAB_BLOCK), lambda j: (0, j)),
            pl.BlockSpec((count, 1), lambda j: (0, 0)),
        ],
        out_specs=(
            pl.BlockSpec((count, VOCAB_BLOCK), lambda j: (0, j)),
            pl.BlockSpec((count, LANES), lambda j: (0, 0)),
            pl.BlockSpec((TURNED, count), lambda j: (0, 0)),
        ),
        compiler_params=params(),
        cost_estimate=pl.CostEstimate(
            flops=2 * count * width * vocab,
            transcendentals=count * vocab,
            bytes_accessed=2 * (count + width) * vocab + 2 * count * width,
        ),
        name="head_forward",
    )(rows, table, ids)


def combine_kernel(near_stat_ref, far_stat_ref, *refs):
    share_refs, (info_ref, near_ref, far_ref, loss_ref) = refs[:4], refs[4:]
    half = near_stat_ref.shape[0]
    count = 2 * half
    own = count // 4
    shares = [
        jnp.concatenate(
            [ref[:, (slot ^ step) * own : ((slot ^ step) + 1) * own] for slot in range(4)], axis=1
        )
        for step, ref in enumerate(share_refs)
    ]
    highest = functools.reduce(jnp.maximum, [share[0:1] for share in shares])
    totals = sum(share[1:2] * jnp.exp(share[0:1] - highest) for share in shares)
    picked = sum(share[2:3] for share in shares)
    log_totals = highest + jnp.log(totals)
    info = info_ref[...]
    loss_ref[...] = jnp.broadcast_to((log_totals - picked) * info[1:2], (TURNED, count))
    row = lax.broadcasted_iota(jnp.int32, (LANES, count), 0)
    turned = jnp.where(row == 0, log_totals, jnp.where(row == 1, info[0:1], info[2:3])).T
    lane = lax.broadcasted_iota(jnp.int32, (half, LANES), 1)
    for stat_ref, coef_ref, start in ((near_stat_ref, near_ref, 0), (far_stat_ref, far_ref, half)):
        part = turned[start : start + half]
        weight = part[:, 1:2]
        coef = weight * jnp.exp(jnp.minimum(stat_ref[...] - part[:, 0:1], 0.0))
        coef = jnp.where(lane == WEIGHT_LANE, weight, coef)
        coef_ref[...] = jnp.where(lane == ID_LANE, part[:, 2:3], coef)


def combine(near_stats, far_stats, shares, info):
    half = near_stats.shape[0]
    return pl.pallas_call(
        combine_kernel,
        out_shape=(
            sized((half, LANES), F32),
            sized((half, LANES), F32),
            sized((TURNED, 2 * half), F32),
        ),
        compiler_params=pltpu.CompilerParams(vmem_limit_bytes=VMEM_LIMIT),
        cost_estimate=pl.CostEstimate(
            flops=20 * half * LANES,
            transcendentals=2 * half * LANES,
            bytes_accessed=16 * half * LANES,
        ),
        name="combine",
    )(near_stats, far_stats, *shares, info)


def logit_grads(vocab, step, part, prob_ref, coef_ref):
    block = prob_ref.shape[1]
    coef = coef_ref[part, :]
    lane = lax.broadcasted_iota(jnp.int32, coef.shape, 1)
    factor = jnp.sum(jnp.where(lane == step, coef, 0.0), -1, keepdims=True)
    weight = coef[:, WEIGHT_LANE : WEIGHT_LANE + 1]
    target = coef[:, ID_LANE : ID_LANE + 1].astype(jnp.int32) - step * block
    column = lax.broadcasted_iota(jnp.int32, (1, block), 1)
    inside = column < vocab - step * block
    prob = prob_ref[part, :].astype(F32)
    grads = prob * factor - jnp.where(column == target, weight, 0.0)
    return jnp.where(inside, grads, 0.0).astype(BF16)


def table_block(vocab, step, table_ref):
    table = table_ref[...]
    column = lax.broadcasted_iota(jnp.int32, (1, table.shape[1]), 1) + step * table.shape[1]
    return jnp.where(column < vocab, table, jnp.zeros_like(table))


def add_up(step, out_ref, terms):
    @pl.when(step == 0)
    def _():
        out_ref[...] = terms

    @pl.when(step > 0)
    def _():
        out_ref[...] += terms


def rows_grad_kernel(vocab, table_ref, prob_ref, coef_ref, first_ref, second_ref, total):
    step = pl.program_id(0)
    grads = logit_grads(vocab, step, slice(None), prob_ref, coef_ref)
    add_up(step, total, mm_nt(grads, table_block(vocab, step, table_ref)))

    @pl.when(step == pl.num_programs(0) - 1)
    def _():
        half = first_ref.shape[0]
        first_ref[...] = total[:half, :].astype(first_ref.dtype)
        second_ref[...] = total[half:, :].astype(second_ref.dtype)


def rows_grad(table, prob, coef, dtype):
    width = table.shape[0]
    count, vocab = prob.shape
    half = whole((count // 2, width))
    return pl.pallas_call(
        functools.partial(rows_grad_kernel, vocab),
        out_shape=(sized((count // 2, width), dtype), sized((count // 2, width), BF16)),
        grid=(pl.cdiv(vocab, VOCAB_BLOCK),),
        in_specs=[
            columns(width, VOCAB_BLOCK),
            columns(count, VOCAB_BLOCK),
            whole((count, LANES)),
        ],
        out_specs=(half, half),
        scratch_shapes=[pltpu.VMEM((count, width), F32)],
        compiler_params=params(),
        cost_estimate=pl.CostEstimate(
            flops=2 * count * width * vocab,
            transcendentals=0,
            bytes_accessed=2 * (count + width) * vocab + 4 * count * width,
        ),
        name="rows_grad",
    )(table, prob, coef)


def table_grad_kernel(
    vocab, near_rows_ref, near_prob_ref, near_coef_ref, far_rows_ref, far_prob_ref, far_coef_ref, out_ref
):
    step = pl.program_id(0)
    near = logit_grads(vocab, step, slice(None), near_prob_ref, near_coef_ref)
    far = logit_grads(vocab, step, slice(None), far_prob_ref, far_coef_ref)
    out_ref[...] = (mm_tn(near_rows_ref[...], near) + mm_tn(far_rows_ref[...], far)).astype(BF16)


def table_grad(near, far):
    count, width = near[0].shape
    vocab = near[1].shape[1]
    specs = [whole((count, width)), columns(count, VOCAB_BLOCK), whole((count, LANES))]
    return pl.pallas_call(
        functools.partial(table_grad_kernel, vocab),
        out_shape=sized((width, vocab), BF16),
        grid=(pl.cdiv(vocab, VOCAB_BLOCK),),
        in_specs=specs * 2,
        out_specs=columns(width, VOCAB_BLOCK),
        compiler_params=params(),
        cost_estimate=pl.CostEstimate(
            flops=4 * count * width * vocab,
            transcendentals=0,
            bytes_accessed=(4 * count + 2 * width) * vocab + 4 * count * width,
        ),
        name="table_grad",
    )(*near, *far)


def gelu_tanh(values):
    return (
        0.5 * values * (1.0 + jnp.tanh(GELU_SCALE * (values + 0.044715 * values * values * values)))
    )


def gated_unit(gate_in, up_in):
    return gelu_tanh(gate_in) * up_in


def norm_rows(values, gain_vec):
    inverse = lax.rsqrt(jnp.mean(values * values, -1, keepdims=True) + EPSILON)
    return (values * inverse * gain_vec, inverse)


def norm_back(values, inverse, gain_vec, upstream):
    scaled = upstream * gain_vec
    inner_sum = jnp.mean(scaled * values, -1, keepdims=True)
    d_values = inverse * scaled - values * (inverse * inverse * inverse) * inner_sum
    d_gain = jnp.sum(upstream * values * inverse, axis=0)
    return (d_values, d_gain)


def step_back(values, inverse, gain, own, received, d_residual):
    upstream = own + sum(part.astype(F32) for part in received)
    d_values, d_gain = norm_back(values, inverse, gain, upstream)
    if d_residual is not None:
        d_values = d_residual + d_values
    return d_values, d_values.astype(BF16), d_gain


def pack_kernel(*refs):
    parts, out_ref = refs[:-1], refs[-1]
    slim = parts[0].shape[1]
    half = len(parts) // 2
    for i, part in enumerate(parts):
        side = i // half
        out_ref[i % half, :, side * slim : (side + 1) * slim] = part[...]


def pack_pairs(parts):
    depth, slim = parts[0].shape
    return pl.pallas_call(
        pack_kernel,
        out_shape=sized((len(parts) // 2, depth, 2 * slim), BF16),
        name="pack_pairs",
    )(*parts)


def join_kernel(*refs):
    parts, (moved_ref, out_ref) = refs[:-2], refs[-2:]
    slim = parts[0].shape[1]
    half = len(parts) // 2
    for i, part in enumerate(parts):
        side = i // half
        out_ref[i, :, :slim] = part[...]
        out_ref[i, :, slim:] = moved_ref[i % half, :, side * slim : (side + 1) * slim]


def join_slices(parts, moved):
    depth, slim = parts[0].shape
    return pl.pallas_call(
        join_kernel,
        out_shape=sized((len(parts), depth, 2 * slim), BF16),
        name="join_slices",
    )(*parts, moved)


def swap(values, step):
    return lax.ppermute(values, "mp", [(i, i ^ step) for i in range(4)])


def total_of_all(values):
    for axis in ("mp", "batch"):
        size, step = lax.axis_size(axis), 1
        while step < size:
            moved = lax.ppermute(values, axis, [(i, i ^ step) for i in range(size)])
            values, step = values + moved, 2 * step
    return values


def gather_batch(values, axis):
    return lax.all_gather(values, "batch", axis=axis, tiled=True)


def scatter_batch(values, axis):
    return lax.psum_scatter(values, "batch", scatter_dimension=axis, tiled=True)


def after(values, earlier):
    return lax.optimization_barrier((values, earlier))[0]


def both_slices(weights):
    return jnp.concatenate([weights, swap(weights, 2)], axis=-1)


def own_slice(grads):
    cut = grads.shape[-1] // 2
    return grads[..., :cut], swap(grads[..., cut:], 2)


def local(
    hidden_in,
    memory,
    tgt_len,
    src_len,
    target_ids,
    task_ids,
    task_weight,
    gain_self,
    q_self,
    k_self,
    v_self,
    o_self,
    gain_cross,
    q_cross,
    k_cross,
    v_cross,
    o_cross,
    gain_mlp,
    mlp_gate,
    mlp_up,
    mlp_down,
    gain_exit,
    embed_table,
):
    place = lax.axis_index("mp")
    pair = place // 2
    lower = pair == 0
    others = [place, place ^ 2, place ^ 1, place ^ 3]
    block = hidden_in.shape[1]
    own_rows = 2 * block
    width = hidden_in.shape[2]
    vocab = embed_table.shape[1]

    def of_pair(values):
        return jnp.where(lower, values[0], values[1])

    def of_other(values):
        return jnp.where(lower, values[1], values[0])

    def pair_rows(values):
        mine, other = of_pair(values), of_other(values)
        second = swap(other, 2)
        return [mine, second, swap(mine, 1), swap(second, 1)]

    def placed(own, received):
        far = received.astype(own.dtype)
        return jnp.stack([jnp.where(lower, own, far), jnp.where(lower, far, own)])

    pair_tgt = jnp.where(lower, tgt_len[0], tgt_len[1])
    pair_src = jnp.where(lower, src_len[0], src_len[1])
    self_scal = jnp.stack(others + [pair_tgt]).astype(jnp.int32)
    cross_scal = jnp.stack(others + [pair_src]).astype(jnp.int32)

    half_rows = 2 * own_rows
    slot_blocks = [
        (of, other)
        for of, order in ((pair, others), (1 - pair, [others[i] for i in (1, 0, 3, 2)]))
        for other in order
    ]
    row_order = jnp.stack([of * 4 + other for of, other in slot_blocks])
    ids = target_ids.reshape(8, block)[row_order].reshape(8 * block)
    local_ids = ids - place * vocab
    local_ids = jnp.where((local_ids >= 0) & (local_ids < vocab), local_ids, -1)
    positions = (
        jnp.stack([other * block for _, other in slot_blocks])[:, None] + jnp.arange(block)[None, :]
    ).reshape(8 * block)
    slot_pair = jnp.repeat(jnp.stack([pair, 1 - pair]), 4 * block)
    lengths = jnp.where(slot_pair == 0, tgt_len[0], tgt_len[1])
    valid = (positions < lengths).astype(F32)
    tasks = task_weight.shape[0]
    task_scale = jnp.sum(
        jnp.where(task_ids[:, None] == jnp.arange(tasks)[None, :], task_weight[None, :], 0.0), -1
    )
    logit_scale = width ** (-0.5)
    row_scale = jnp.where(slot_pair == 0, task_scale[0], task_scale[1]) * valid * logit_scale

    info = jnp.stack([row_scale, valid, local_ids.astype(F32)])
    info = jnp.concatenate([info, jnp.zeros((TURNED - 3, info.shape[1]), F32)])
    near_ids, far_ids = local_ids[:half_rows, None], local_ids[half_rows:, None]

    gain_size = gain_self.shape[0]
    gains = lax.all_gather(
        jnp.stack([gain_self, gain_cross, gain_mlp, gain_exit]), "batch", axis=1, tiled=True
    )
    attention = [q_self, k_self, v_self, o_self, q_cross, k_cross, v_cross, o_cross]
    slim = q_self.shape[1]
    moved = swap(pack_pairs(attention), 2)
    w_both, gains, self_scal, cross_scal = lax.optimization_barrier(
        (join_slices(attention, moved), gains.astype(F32), self_scal, cross_scal)
    )
    w_both = gather_batch(w_both, 1)
    gain_self, gain_cross, gain_mlp, gain_exit = (gains[i] for i in range(4))
    own_rows_in = of_pair(hidden_in)
    second = swap(after(of_other(hidden_in), moved), 2)
    pieces = [own_rows_in, second, swap(own_rows_in, 1), swap(second, 1)]
    mlp_part = both_slices(after(jnp.stack([mlp_gate, mlp_up, mlp_down]), moved))
    memory_pieces = pair_rows(after(memory, second))

    residual = jnp.concatenate(pieces[:2], axis=0).astype(F32)
    w_mlp = gather_batch(after(mlp_part, (w_both, pieces, memory_pieces[1])), 1)
    q_one, k_one, v_one, mixed_one, lse_one, rows_one, own_terms, other_terms = self_forward(
        self_scal, pieces, gain_self[None], w_both
    )
    memory_rows = jnp.concatenate(memory_pieces, axis=0)
    k_two = mm(memory_rows, w_both[5]).astype(BF16)
    v_two = mm(memory_rows, w_both[6]).astype(BF16)
    own_terms = after(own_terms, (k_two, v_two))
    residual_one = residual + own_terms + swap(other_terms, 1).astype(F32)

    normed_two, inverse_two = norm_rows(residual_one, gain_cross)
    own_two = normed_two.astype(BF16)
    rows_two = (own_two, swap(own_two, 1))
    q_two, mixed_two, lse_two, own_terms, other_terms = cross_forward(
        cross_scal, *rows_two, w_both, k_two, v_two
    )
    table = gather_batch(after(embed_table, (w_mlp, rows_two[1])), 0)
    residual_two = residual_one + own_terms + swap(other_terms, 1).astype(F32)

    normed_three, inverse_three = norm_rows(residual_two, gain_mlp)
    own_three = normed_three.astype(BF16)
    other_three, info, near_ids, far_ids = lax.optimization_barrier(
        (swap(own_three, 1), info, near_ids, far_ids)
    )
    rows_three = (own_three, other_three)
    gate, up_proj, hidden, own_terms, other_terms = mlp_forward(self_scal, *rows_three, w_mlp)
    residual_three = residual_two + own_terms + swap(other_terms, 1).astype(F32)
    finished = residual_three.astype(BF16)

    normed_four, inverse_four = norm_rows(residual_three, gain_exit)
    own_four = normed_four.astype(BF16)
    near_four = jnp.concatenate([own_four, swap(own_four, 1)], axis=0)
    far_four = (swap(own_four, 2), swap(own_four, 3))
    near_prob, near_stats, near_turned = head_forward(
        near_four, table, near_ids, logit_scale
    )
    far_four = jnp.concatenate(after(far_four, near_turned), axis=0)
    far_prob, far_stats, far_turned = head_forward(
        far_four, table, far_ids, logit_scale
    )
    mine = jnp.concatenate([near_turned, far_turned], axis=1)
    finished = after(finished, near_turned)
    finished_far = swap(finished[block:], 2)
    block_out = placed(finished[:block], finished_far)
    shares = [mine] + [swap(mine, step) for step in (1, 2, 3)]
    near_coef, far_coef, losses = combine(near_stats, far_stats, shares, info)
    half_sums = jnp.sum(losses[0].reshape(2, half_rows), -1)
    pair_sums = jnp.where(lower, half_sums, half_sums[::-1])
    pair_loss = pair_sums / tgt_len.astype(F32)

    table_terms = table_grad(
        (near_four, near_prob, near_coef), (far_four, far_prob, far_coef)
    )
    embed_sum = scatter_batch(table_terms, 0)
    far_two, far_three = rows_grad(table, far_prob, after(far_coef, table_terms), BF16)
    far_three = swap(far_three, 1)
    d_own, near_one = rows_grad(table, near_prob, after(near_coef, (far_two, finished_far)), F32)
    far_two = far_two.astype(F32) + after(far_three, near_one).astype(F32)
    received = (swap(near_one, 1), swap(far_two.astype(BF16), 2))
    d_residual, own_branch, exit_grad = step_back(
        residual_three, inverse_four, gain_exit, d_own, received, None
    )

    branch_three = (own_branch, swap(own_branch, 1))
    d_gate, d_up, own_terms, other_terms = mlp_back(self_scal, *branch_three, w_mlp, gate, up_proj)
    mlp_terms = mlp_grads(self_scal, rows_three, branch_three, d_gate, d_up, hidden)
    received = (after(swap(other_terms, 1), mlp_terms),)
    d_residual, own_branch, mlp_grad = step_back(
        residual_two, inverse_three, gain_mlp, own_terms, received, d_residual
    )

    branch_two = (own_branch, after(swap(own_branch, 1), embed_sum))
    mlp_scattered = scatter_batch(after(mlp_terms, branch_two[1]), 1)
    mlp_here, mlp_moved = own_slice(mlp_scattered)
    mlp_sum = mlp_here.astype(F32) + mlp_moved.astype(F32)
    dq_two, dk_two, dv_two, own_terms, other_terms = cross_back(
        cross_scal, *branch_two, w_both, q_two, k_two, v_two, lse_two
    )
    cross_terms = cross_grads(
        self_scal, rows_two, branch_two, memory_pieces, (dq_two, dk_two, dv_two, mixed_two)
    )
    received = (after(swap(other_terms, 1), cross_terms),)
    d_residual, own_branch, cross_grad = step_back(
        residual_one, inverse_two, gain_cross, own_terms, received, d_residual
    )

    memory_terms = mm_nt(dk_two, w_both[5]) + mm_nt(dv_two, w_both[6])
    branch_one = (own_branch, after(swap(own_branch, 1), memory_terms))
    half = memory_terms.shape[0] // 2
    memory_sent = after(memory_terms[half:].astype(BF16), branch_one[1])
    memory_received = swap(memory_sent, 1)
    memory_own = memory_terms[:half] + memory_received.astype(F32)
    dq_one, dk_one, dv_one, own_terms, other_terms, self_grad = self_back(
        self_scal, *branch_one, w_both, q_one, k_one, v_one, lse_one, pieces
    )
    last_grads = self_grads(
        self_scal,
        after(rows_one, (mlp_scattered, memory_received)),
        branch_one,
        (dq_one, dk_one, dv_one, mixed_one),
        cross_terms,
    )
    last_sum = scatter_batch(last_grads, 1)
    memory_far = swap(memory_own[half // 2 :].astype(BF16), 2)
    gain_grads = jnp.stack([self_grad[0], cross_grad, mlp_grad, exit_grad])
    gain_grads = total_of_all(after(gain_grads, last_grads))
    memory_far = after(memory_far, gain_grads)
    memory_grad = placed(memory_own[: half // 2], memory_far)
    received = (after(swap(other_terms, 1), (last_grads, mlp_moved)),)
    d_residual, _, _ = step_back(
        residual, norm_rows(residual, 1.0)[1], gain_self, own_terms, received, d_residual
    )
    hidden_far = swap(after(d_residual[block:].astype(BF16), memory_far), 2)
    hidden_grad = placed(d_residual[:block], hidden_far)
    gain_sums = lax.dynamic_slice_in_dim(
        gain_grads, lax.axis_index("batch") * gain_size, gain_size, axis=1
    )
    sent = last_sum[..., slim:]
    moved = swap(jnp.concatenate([sent[:4], sent[4:]], axis=-1), 2)
    self_sum = last_sum[:4, :, :slim].astype(F32) + moved[..., :slim].astype(F32)
    cross_sum = last_sum[4:, :, :slim].astype(F32) + moved[..., slim:].astype(F32)
    return (
        block_out,
        pair_loss,
        hidden_grad,
        memory_grad,
        gain_sums[0],
        self_sum[0],
        self_sum[1],
        self_sum[2],
        self_sum[3],
        gain_sums[1],
        cross_sum[0],
        cross_sum[1],
        cross_sum[2],
        cross_sum[3],
        gain_sums[2],
        mlp_sum[0],
        mlp_sum[1],
        mlp_sum[2],
        gain_sums[3],
        embed_sum.astype(F32),
    )


def solution(mesh):
    assert mesh.shape["mp"] == 4
    rows = P("batch", "mp", None)
    vector = P("batch")
    matrix = P("batch", "mp")
    sub = (vector, matrix, matrix, matrix, matrix)
    mlp = (vector, matrix, matrix, matrix)
    weights = sub + sub + mlp + (vector, matrix)
    in_specs = (rows, rows, vector, vector, P("batch", None), vector, P()) + weights
    out_specs = (rows, vector, rows, rows) + weights
    return jax.shard_map(local, mesh=mesh, in_specs=in_specs, out_specs=out_specs, check_vma=False)
```

```python
import functools

import jax
import jax.numpy as jnp
from jax import lax
from jax.experimental import pallas as pl
from jax.experimental.pallas import tpu as pltpu
from jax.sharding import PartitionSpec as P

DH = 64
LANES = 128
EPSILON = 1e-06
MASKED_OUT = -1000000000.0
GELU_SCALE = 0.7978845608028654
VMEM_LIMIT = 56 * 1024 * 1024
HEAD_LIMIT = 56 * 1024 * 1024
GRAD_BLOCK = 512
VOCAB_BLOCK = 2048
HIDDEN_BLOCK = 512
LOG2_E = 1.4426950408889634
BF16 = jnp.bfloat16
F32 = jnp.float32


def params(limit=VMEM_LIMIT):
    return pltpu.CompilerParams(dimension_semantics=("arbitrary",), vmem_limit_bytes=limit)


def mm(a, b):
    return lax.dot_general(a, b, (((1,), (0,)), ((), ())), preferred_element_type=F32)


def mm_nt(a, b):
    return lax.dot_general(a, b, (((1,), (1,)), ((), ())), preferred_element_type=F32)


def mm_tn(a, b):
    return lax.dot_general(a, b, (((0,), (0,)), ((), ())), preferred_element_type=F32)


def block_positions(scal_ref, size, dim):
    shape = (size, 1) if dim == 0 else (1, size)
    pieces = [lax.broadcasted_iota(jnp.int32, shape, dim) + scal_ref[i] * size for i in range(4)]
    return jnp.concatenate(pieces, axis=dim)


def score_bias(scal_ref, rows, keys, causal):
    key_pos = block_positions(scal_ref, keys // 4, 1)
    allowed = key_pos < scal_ref[4]
    if causal:
        row_pos = block_positions(scal_ref, rows // 4, 0)
        allowed = allowed & (key_pos <= row_pos)
    return jnp.where(allowed, 0.0, MASKED_OUT)


def head_lanes(rows, head):
    lane = lax.broadcasted_iota(jnp.int32, (rows, LANES), 1)
    return (lane < DH) if head == 0 else (lane >= DH)


def attend_heads(q, k, v, bias):
    rows = q.shape[0]
    outs, lses = [], []
    for head in range(2):
        q_head = jnp.where(head_lanes(rows, head), q, jnp.zeros_like(q))
        scores = mm_nt(q_head, k) + bias
        highest = jnp.max(scores, -1, keepdims=True)
        raised = jnp.exp(scores - highest)
        totals = jnp.sum(raised, -1, keepdims=True)
        outs.append(mm(raised.astype(BF16), v) * (1.0 / totals))
        lses.append(highest + jnp.log(totals))
    first = head_lanes(rows, 0)
    return jnp.where(first, outs[0], outs[1]).astype(BF16), jnp.where(first, lses[0], lses[1])


def attend_heads_back(q, k, v, lse, d_out, bias):
    rows, keys = q.shape[0], k.shape[0]
    dqs, dks, dvs = [], [], []
    for head in range(2):
        mine = head_lanes(rows, head)
        q_head = jnp.where(mine, q, jnp.zeros_like(q))
        d_head = jnp.where(mine, d_out, jnp.zeros_like(d_out))
        weights = jnp.exp(mm_nt(q_head, k) + bias - lse[:, head * DH : head * DH + 1])
        d_weights = mm_nt(d_head, v)
        inner = jnp.sum(weights * d_weights, -1, keepdims=True)
        d_scores = (weights * (d_weights - inner)).astype(BF16)
        dqs.append(mm(d_scores, k))
        dks.append(mm_tn(d_scores, q))
        dvs.append(mm_tn(weights.astype(BF16), d_out))
    first = head_lanes(keys, 0)
    return (
        jnp.where(head_lanes(rows, 0), dqs[0], dqs[1]).astype(BF16),
        jnp.where(first, dks[0], dks[1]).astype(BF16),
        jnp.where(first, dvs[0], dvs[1]).astype(BF16),
    )


def leave(total, own_ref, other_ref):
    @pl.when(pl.program_id(0) == pl.num_programs(0) - 1)
    def _():
        half = own_ref.shape[0]
        own_ref[...] = total[:half, :]
        other_ref[...] = total[half:, :].astype(BF16)


def stack_rows(own_ref, other_ref, rows):
    half = own_ref.shape[0]
    rows[:half, :] = own_ref[...]
    rows[half:, :] = other_ref[...]


def whole(shape):
    return pl.BlockSpec(shape, lambda j, *_: (0,) * len(shape))


def columns(rows, block):
    return pl.BlockSpec((rows, block), lambda j, *_: (0, j))


def weight_block(count, place, width, block):
    return pl.BlockSpec((count, width, block), lambda j, *_: (place, 0, j))


def sized(shape, dtype):
    return jax.ShapeDtypeStruct(shape, dtype)


def sublayer(kernel, name, scal, operands, specs, outs, out_specs, scratch, steps, flops, moved):
    return pl.pallas_call(
        kernel,
        out_shape=outs,
        grid_spec=pltpu.PrefetchScalarGridSpec(
            num_scalar_prefetch=1,
            grid=(steps,),
            in_specs=specs,
            out_specs=out_specs,
            scratch_shapes=scratch,
        ),
        compiler_params=params(),
        cost_estimate=pl.CostEstimate(flops=flops, transcendentals=0, bytes_accessed=moved),
        name=name,
    )(scal, *operands)


def self_forward_kernel(
    scal_ref, *refs
):
    pieces, (gain_ref, w_ref) = refs[:4], refs[4:6]
    q_ref, k_ref, v_ref, mixed_ref, lse_ref, rows_ref, own_ref, other_ref, total, bias = refs[6:]
    count = rows_ref.shape[0]

    @pl.when(pl.program_id(0) == 0)
    def _():
        size = pieces[0].shape[0]
        for i, piece in enumerate(pieces):
            normed, _ = norm_rows(piece[...].astype(F32), gain_ref[...])
            rows_ref[i * size : (i + 1) * size, :] = normed.astype(BF16)
        bias[...] = score_bias(scal_ref, count, count, True)
        total[...] = jnp.zeros_like(total)

    rows = rows_ref[...]
    q_ref[...] = mm(rows, w_ref[0]).astype(BF16)
    k_ref[...] = mm(rows, w_ref[1]).astype(BF16)
    v_ref[...] = mm(rows, w_ref[2]).astype(BF16)
    mixed, lse_ref[...] = attend_heads(q_ref[...], k_ref[...], v_ref[...], bias[...])
    mixed_ref[...] = mixed
    total[...] += mm_nt(mixed, w_ref[3])
    leave(total, own_ref, other_ref)


def self_forward(scal, pieces, gain, weights):
    block, width = pieces[0].shape
    count, cols = 4 * block, weights.shape[2]
    half = count // 2
    narrow = sized((count, cols), BF16)
    return sublayer(
        self_forward_kernel,
        "self_forward",
        scal,
        (*pieces, gain, weights),
        [whole((block, width))] * 4 + [whole((1, width)), weight_block(4, 0, width, LANES)],
        (narrow, narrow, narrow, narrow, sized((count, cols), F32))
        + (sized((count, width), BF16), sized((half, width), F32), sized((half, width), BF16)),
        [columns(count, LANES)] * 5
        + [whole((count, width)), whole((half, width)), whole((half, width))],
        [pltpu.VMEM((count, width), F32), pltpu.VMEM((count, count), F32)],
        cols // LANES,
        8 * count * width * cols + 8 * count * count * cols,
        8 * width * cols + 12 * count * cols + 8 * count * width,
    )


def cross_forward_kernel(
    scal_ref, h_own_ref, h_other_ref, w_ref, k_ref, v_ref,
    q_ref, mixed_ref, lse_ref, own_ref, other_ref, rows, total,
):
    @pl.when(pl.program_id(0) == 0)
    def _():
        stack_rows(h_own_ref, h_other_ref, rows)
        total[...] = jnp.zeros_like(total)

    bias = score_bias(scal_ref, rows.shape[0], k_ref.shape[0], False)
    q_ref[...] = mm(rows[...], w_ref[0]).astype(BF16)
    mixed, lse_ref[...] = attend_heads(q_ref[...], k_ref[...], v_ref[...], bias)
    mixed_ref[...] = mixed
    total[...] += mm_nt(mixed, w_ref[3])
    leave(total, own_ref, other_ref)


def cross_forward(scal, own, other, weights, k, v):
    half, width = own.shape
    count, cols, keys = 2 * half, weights.shape[2], k.shape[0]
    return sublayer(
        cross_forward_kernel,
        "cross_forward",
        scal,
        (own, other, weights, k, v),
        [whole((half, width))] * 2
        + [weight_block(4, 1, width, LANES), columns(keys, LANES), columns(keys, LANES)],
        (sized((count, cols), BF16), sized((count, cols), BF16), sized((count, cols), F32))
        + (sized((half, width), F32), sized((half, width), BF16)),
        [columns(count, LANES)] * 3 + [whole((half, width))] * 2,
        [pltpu.VMEM((count, width), BF16), pltpu.VMEM((count, width), F32)],
        cols // LANES,
        4 * count * width * cols + 8 * count * keys * cols,
        8 * width * cols + 8 * count * cols + 4 * keys * cols + 8 * count * width,
    )


def mlp_forward_kernel(
    scal_ref, h_own_ref, h_other_ref, w_ref,
    gate_ref, up_ref, hidden_ref, own_ref, other_ref, rows, total,
):
    @pl.when(pl.program_id(0) == 0)
    def _():
        stack_rows(h_own_ref, h_other_ref, rows)
        total[...] = jnp.zeros_like(total)

    gate = mm(rows[...], w_ref[0])
    up = mm(rows[...], w_ref[1])
    hidden = gated_unit(gate, up).astype(BF16)
    gate_ref[...] = gate
    up_ref[...] = up
    hidden_ref[...] = hidden
    total[...] += mm_nt(hidden, w_ref[2])
    leave(total, own_ref, other_ref)


def mlp_forward(scal, own, other, weights):
    half, width = own.shape
    count, cols = 2 * half, weights.shape[2]
    return sublayer(
        mlp_forward_kernel,
        "mlp_forward",
        scal,
        (own, other, weights),
        [whole((half, width))] * 2 + [weight_block(3, 0, width, HIDDEN_BLOCK)],
        (sized((count, cols), F32), sized((count, cols), F32), sized((count, cols), BF16))
        + (sized((half, width), F32), sized((half, width), BF16)),
        [columns(count, HIDDEN_BLOCK)] * 3 + [whole((half, width))] * 2,
        [pltpu.VMEM((count, width), BF16), pltpu.VMEM((count, width), F32)],
        cols // HIDDEN_BLOCK,
        6 * count * width * cols,
        6 * width * cols + 10 * count * cols + 5 * count * width,
    )


def mlp_back_kernel(
    scal_ref, e_own_ref, e_other_ref, w_ref, gate_ref, up_ref,
    d_gate_ref, d_up_ref, own_ref, other_ref, rows, total,
):
    @pl.when(pl.program_id(0) == 0)
    def _():
        stack_rows(e_own_ref, e_other_ref, rows)
        total[...] = jnp.zeros_like(total)

    d_hidden = mm(rows[...], w_ref[2])
    gate, up = gate_ref[...], up_ref[...]
    inner = GELU_SCALE * (gate + 0.044715 * gate * gate * gate)
    bent = jnp.tanh(inner)
    slope = GELU_SCALE * (1.0 + 3.0 * 0.044715 * gate * gate)
    d_gelu = 0.5 * (1.0 + bent) + 0.5 * gate * (1.0 - bent * bent) * slope
    d_gate = (d_hidden * up * d_gelu).astype(BF16)
    d_up = (d_hidden * (0.5 * gate * (1.0 + bent))).astype(BF16)
    d_gate_ref[...] = d_gate
    d_up_ref[...] = d_up
    total[...] += mm_nt(d_gate, w_ref[0]) + mm_nt(d_up, w_ref[1])
    leave(total, own_ref, other_ref)


def mlp_back(scal, own, other, weights, gate, up):
    half, width = own.shape
    count, cols = 2 * half, weights.shape[2]
    return sublayer(
        mlp_back_kernel,
        "mlp_back",
        scal,
        (own, other, weights, gate, up),
        [whole((half, width))] * 2
        + [weight_block(3, 0, width, HIDDEN_BLOCK)]
        + [columns(count, HIDDEN_BLOCK)] * 2,
        (sized((count, cols), BF16), sized((count, cols), BF16))
        + (sized((half, width), F32), sized((half, width), BF16)),
        [columns(count, HIDDEN_BLOCK)] * 2 + [whole((half, width))] * 2,
        [pltpu.VMEM((count, width), BF16), pltpu.VMEM((count, width), F32)],
        cols // HIDDEN_BLOCK,
        6 * count * width * cols,
        6 * width * cols + 12 * count * cols + 5 * count * width,
    )


def mlp_grads_kernel(
    scal_ref, h_own_ref, h_other_ref, e_own_ref, e_other_ref, d_gate_ref, d_up_ref, hidden_ref,
    out_ref,
):
    half = h_own_ref.shape[0]
    for i, (own, other, d_ref) in enumerate(
        (
            (h_own_ref, h_other_ref, d_gate_ref),
            (h_own_ref, h_other_ref, d_up_ref),
            (e_own_ref, e_other_ref, hidden_ref),
        )
    ):
        terms = mm_tn(own[...], d_ref[:half, :]) + mm_tn(other[...], d_ref[half:, :])
        out_ref[i] = terms.astype(BF16)


def mlp_grads(scal, rows, branch, d_gate, d_up, hidden):
    half, width = rows[0].shape
    count, cols = hidden.shape
    return sublayer(
        mlp_grads_kernel,
        "mlp_grads",
        scal,
        (*rows, *branch, d_gate, d_up, hidden),
        [whole((half, width))] * 4 + [columns(count, HIDDEN_BLOCK)] * 3,
        sized((3, width, cols), BF16),
        weight_block(3, 0, width, HIDDEN_BLOCK),
        [],
        cols // HIDDEN_BLOCK,
        6 * count * width * cols,
        6 * width * cols + 6 * count * cols + 4 * count * width,
    )


def attention_back_kernel(
    causal, scal_ref, e_own_ref, e_other_ref, w_ref, q_ref, k_ref, v_ref, lse_ref,
    dq_ref, dk_ref, dv_ref, own_ref, other_ref, gain_ref, rows, total, bias, *pieces,
):
    @pl.when(pl.program_id(0) == 0)
    def _():
        stack_rows(e_own_ref, e_other_ref, rows)
        total[...] = jnp.zeros_like(total)
        bias[...] = score_bias(scal_ref, rows.shape[0], k_ref.shape[0], causal)

    d_mixed = mm(rows[...], w_ref[3]).astype(BF16)
    dq, dk, dv = attend_heads_back(
        q_ref[...], k_ref[...], v_ref[...], lse_ref[...], d_mixed, bias[...]
    )
    dq_ref[...] = dq
    dk_ref[...] = dk
    dv_ref[...] = dv
    terms = mm_nt(dq, w_ref[0])
    if causal:
        terms += mm_nt(dk, w_ref[1]) + mm_nt(dv, w_ref[2])
    total[...] += terms
    leave(total, own_ref, other_ref)

    if causal:
        @pl.when(pl.program_id(0) == pl.num_programs(0) - 1)
        def _():
            size = pieces[0].shape[0]
            summed = 0.0
            for i, piece in enumerate(pieces):
                values = piece[...].astype(F32)
                unit, _ = norm_rows(values, 1.0)
                part = total[i * size : (i + 1) * size, :] * unit
                summed = summed + jnp.sum(part, 0, keepdims=True)
            gain_ref[...] = jnp.broadcast_to(summed, gain_ref.shape)


def cross_back(scal, own, other, weights, q, k, v, lse):
    half, width = own.shape
    count, cols, keys = 2 * half, weights.shape[2], k.shape[0]

    def kernel(scal_ref, *refs):
        attention_back_kernel(False, scal_ref, *refs[:12], None, *refs[12:])

    return sublayer(
        kernel,
        "cross_back",
        scal,
        (own, other, weights, q, k, v, lse),
        [whole((half, width))] * 2
        + [weight_block(4, 1, width, LANES), columns(count, LANES)]
        + [columns(keys, LANES)] * 2
        + [columns(count, LANES)],
        (sized((count, cols), BF16), sized((keys, cols), BF16), sized((keys, cols), BF16))
        + (sized((half, width), F32), sized((half, width), BF16)),
        [columns(count, LANES), columns(keys, LANES), columns(keys, LANES)]
        + [whole((half, width))] * 2,
        [
            pltpu.VMEM((count, width), BF16),
            pltpu.VMEM((count, width), F32),
            pltpu.VMEM((1, keys), F32),
        ],
        cols // LANES,
        4 * count * width * cols + 20 * count * keys * cols,
        8 * width * cols + 8 * count * cols + 8 * keys * cols + 8 * count * width,
    )


def self_back(scal, own, other, weights, q, k, v, lse, pieces):
    half, width = own.shape
    count, cols = 2 * half, weights.shape[2]
    block = pieces[0].shape[0]

    def kernel(scal_ref, *refs):
        attention_back_kernel(True, scal_ref, *refs[:7], *refs[11:], *refs[7:11])

    narrow = sized((count, cols), BF16)
    return sublayer(
        kernel,
        "self_back",
        scal,
        (own, other, weights, q, k, v, lse, *pieces),
        [whole((half, width))] * 2
        + [weight_block(4, 0, width, LANES)]
        + [columns(count, LANES)] * 4
        + [whole((block, width))] * 4,
        (narrow, narrow, narrow, sized((half, width), F32), sized((half, width), BF16))
        + (sized((8, width), F32),),
        [columns(count, LANES)] * 3 + [whole((half, width))] * 2 + [whole((8, width))],
        [
            pltpu.VMEM((count, width), BF16),
            pltpu.VMEM((count, width), F32),
            pltpu.VMEM((count, count), F32),
        ],
        cols // LANES,
        8 * count * width * cols + 20 * count * count * cols,
        8 * width * cols + 20 * count * cols + 10 * count * width,
    )


def cross_grads_kernel(scal_ref, h_own, h_other, e_own, e_other, *refs):
    memory, (dq, dk, dv, mixed, out_ref) = refs[:4], refs[4:]
    half = e_own.shape[0]

    def memory_grad(d_ref):
        size = memory[0].shape[0]
        terms = [mm_tn(m[...], d_ref[i * size : (i + 1) * size, :]) for i, m in enumerate(memory)]
        return sum(terms).astype(BF16)

    def split_grad(own, other, d_ref):
        return (mm_tn(own[...], d_ref[:half, :]) + mm_tn(other[...], d_ref[half:, :])).astype(BF16)

    out_ref[0] = split_grad(h_own, h_other, dq)
    out_ref[1] = memory_grad(dk)
    out_ref[2] = memory_grad(dv)
    out_ref[3] = split_grad(e_own, e_other, mixed)


def cross_grads(scal, rows, branch, memory, narrow):
    half, width = rows[0].shape
    cols, keys = narrow[0].shape[1], narrow[1].shape[0]
    return sublayer(
        cross_grads_kernel,
        "cross_grads",
        scal,
        (*rows, *branch, *memory, *narrow),
        [whole((half, width))] * 4
        + [whole((keys // 4, width))] * 4
        + [columns(array.shape[0], LANES) for array in narrow],
        sized((8, width, cols), BF16),
        weight_block(4, 1, width, LANES),
        [],
        cols // LANES,
        (8 * half + 4 * keys) * width * cols,
        8 * width * cols + (8 * half + 4 * keys) * cols + 8 * half * width,
    )


def self_grads_kernel(scal_ref, h, e_own, e_other, dq, dk, dv, mixed, rest_ref, out_ref):
    half = e_own.shape[0]
    for i, d_ref in enumerate((dq, dk, dv)):
        out_ref[i] = mm_tn(h[...], d_ref[...]).astype(BF16)
    terms = mm_tn(e_own[...], mixed[:half, :]) + mm_tn(e_other[...], mixed[half:, :])
    out_ref[3] = terms.astype(BF16)


def self_grads(scal, rows, branch, narrow, rest):
    count, width = rows.shape
    cols = narrow[0].shape[1]
    return pl.pallas_call(
        self_grads_kernel,
        out_shape=sized(rest.shape, BF16),
        grid_spec=pltpu.PrefetchScalarGridSpec(
            num_scalar_prefetch=1,
            grid=(cols // LANES,),
            in_specs=[whole((count, width))]
            + [whole((count // 2, width))] * 2
            + [columns(count, LANES)] * 4
            + [pl.BlockSpec(memory_space=pl.ANY)],
            out_specs=weight_block(4, 0, width, LANES),
        ),
        input_output_aliases={8: 0},
        compiler_params=params(),
        cost_estimate=pl.CostEstimate(
            flops=8 * count * width * cols,
            transcendentals=0,
            bytes_accessed=8 * width * cols + 8 * count * cols + 4 * count * width,
        ),
        name="self_grads",
    )(scal, rows, *branch, *narrow, rest)


SUMS = 32
PICKS = 64
WEIGHT_LANE = 126
ID_LANE = 127
TURNED = 8


def column_bias(vocab, step, block):
    column = lax.broadcasted_iota(jnp.int32, (1, block), 1) + step * block
    return jnp.where(column < vocab, 0.0, MASKED_OUT)


def head_kernel(vocab, scale, own_ref, other_ref, table_ref, ids_ref, prob_ref, stat_ref, turned_ref):
    step = pl.program_id(0)
    block = table_ref.shape[1]
    table = table_ref[...]
    chunk = 128
    bias = column_bias(vocab, step, block)
    column = lax.broadcasted_iota(jnp.int32, (1, block), 1)
    lane = lax.broadcasted_iota(jnp.int32, (chunk, LANES), 1)
    half = own_ref.shape[0]
    for start in range(0, 2 * half, chunk):
        part = pl.ds(start, chunk)
        rows_ref = own_ref if start < half else other_ref
        products = mm(rows_ref[pl.ds(start % half, chunk), :], table) + bias
        highest = jnp.max(products, -1, keepdims=True)
        raised = jnp.exp2((products - highest) * (scale * LOG2_E))
        prob_ref[part, :] = raised.astype(BF16)
        totals = jnp.sum(raised, -1, keepdims=True)
        target = ids_ref[part, :] - step * block
        picked = jnp.sum(jnp.where(column == target, products, 0.0), -1, keepdims=True)
        stats = jnp.where(step == 0, 0.0, stat_ref[part, :])
        stats = jnp.where(lane == step, highest * scale, stats)
        stats = jnp.where(lane == SUMS + step, totals, stats)
        stat_ref[part, :] = jnp.where(lane == PICKS + step, picked * scale, stats)

    @pl.when(step == pl.num_programs(0) - 1)
    def _():
        stats = stat_ref[...].T
        steps = pl.num_programs(0)
        row = lax.broadcasted_iota(jnp.int32, (SUMS, stats.shape[1]), 0)
        tops = jnp.where(row < steps, stats[:SUMS], MASKED_OUT)
        highest = jnp.max(tops, 0, keepdims=True)
        totals = jnp.sum(stats[SUMS:PICKS] * jnp.exp(tops - highest), 0, keepdims=True)
        picked = jnp.sum(stats[PICKS : PICKS + SUMS], 0, keepdims=True)
        row = lax.broadcasted_iota(jnp.int32, (TURNED, stats.shape[1]), 0)
        turned_ref[...] = jnp.where(row == 0, highest, jnp.where(row == 1, totals, picked))


def head_forward(rows, table, ids, scale):
    half, width = rows[0].shape
    count, vocab = 2 * half, table.shape[1]
    steps = pl.cdiv(vocab, VOCAB_BLOCK)
    return pl.pallas_call(
        functools.partial(head_kernel, vocab, scale),
        out_shape=(
            jax.ShapeDtypeStruct((count, steps * VOCAB_BLOCK), BF16),
            jax.ShapeDtypeStruct((count, LANES), F32),
            jax.ShapeDtypeStruct((TURNED, count), F32),
        ),
        grid=(steps,),
        in_specs=[
            whole((half, width)),
            whole((half, width)),
            pl.BlockSpec((width, VOCAB_BLOCK), lambda j: (0, j)),
            pl.BlockSpec((count, 1), lambda j: (0, 0)),
        ],
        out_specs=(
            columns(count, VOCAB_BLOCK),
            pl.BlockSpec((count, LANES), lambda j: (0, 0)),
            pl.BlockSpec((TURNED, count), lambda j: (0, 0)),
        ),
        compiler_params=params(HEAD_LIMIT),
        cost_estimate=pl.CostEstimate(
            flops=2 * count * width * vocab,
            transcendentals=count * vocab,
            bytes_accessed=2 * (count + width) * vocab + 2 * count * width,
        ),
        name="head_forward",
    )(*rows, table, ids)


def combine_kernel(near_stat_ref, far_stat_ref, *refs):
    share_refs, (info_ref, near_ref, far_ref, loss_ref) = refs[:4], refs[4:]
    half = near_stat_ref.shape[0]
    count = 2 * half
    own = count // 4
    shares = [
        jnp.concatenate(
            [ref[:, (slot ^ step) * own : ((slot ^ step) + 1) * own] for slot in range(4)], axis=1
        )
        for step, ref in enumerate(share_refs)
    ]
    highest = functools.reduce(jnp.maximum, [share[0:1] for share in shares])
    totals = sum(share[1:2] * jnp.exp(share[0:1] - highest) for share in shares)
    picked = sum(share[2:3] for share in shares)
    log_totals = highest + jnp.log(totals)
    info = info_ref[...]
    loss_ref[...] = jnp.broadcast_to((log_totals - picked) * info[1:2], (TURNED, count))
    row = lax.broadcasted_iota(jnp.int32, (LANES, count), 0)
    turned = jnp.where(row == 0, log_totals, jnp.where(row == 1, info[0:1], info[2:3])).T
    lane = lax.broadcasted_iota(jnp.int32, (half, LANES), 1)
    for stat_ref, coef_ref, start in ((near_stat_ref, near_ref, 0), (far_stat_ref, far_ref, half)):
        part = turned[start : start + half]
        weight = part[:, 1:2]
        coef = weight * jnp.exp(jnp.minimum(stat_ref[...] - part[:, 0:1], 0.0))
        coef = jnp.where(lane == WEIGHT_LANE, weight, coef)
        coef_ref[...] = jnp.where(lane == ID_LANE, part[:, 2:3], coef)


def combine(near_stats, far_stats, shares, info):
    half = near_stats.shape[0]
    return pl.pallas_call(
        combine_kernel,
        out_shape=(
            sized((half, LANES), F32),
            sized((half, LANES), F32),
            sized((TURNED, 2 * half), F32),
        ),
        compiler_params=pltpu.CompilerParams(vmem_limit_bytes=HEAD_LIMIT),
        cost_estimate=pl.CostEstimate(
            flops=20 * half * LANES,
            transcendentals=2 * half * LANES,
            bytes_accessed=16 * half * LANES,
        ),
        name="combine",
    )(near_stats, far_stats, *shares, info)


def row_coefs(step, coef_ref):
    coef = coef_ref[...]
    lane = lax.broadcasted_iota(jnp.int32, coef.shape, 1)
    factor = jnp.sum(jnp.where(lane == step, coef, 0.0), -1, keepdims=True)
    target = coef[:, ID_LANE : ID_LANE + 1].astype(jnp.int32)
    return factor, coef[:, WEIGHT_LANE : WEIGHT_LANE + 1], target - step * VOCAB_BLOCK


def logit_grads(start, prob_ref, coefs):
    factor, weight, target = coefs
    column = lax.broadcasted_iota(jnp.int32, (1, GRAD_BLOCK), 1) + start
    prob = prob_ref[:, start : start + GRAD_BLOCK].astype(F32)
    return (prob * factor - jnp.where(column == target, weight, 0.0)).astype(BF16)


def add_up(step, out_ref, terms):
    @pl.when(step == 0)
    def _():
        out_ref[...] = terms

    @pl.when(step > 0)
    def _():
        out_ref[...] += terms


def rows_grad_kernel(vocab, table_ref, prob_ref, coef_ref, first_ref, second_ref, total):
    step = pl.program_id(0)
    coefs = row_coefs(step, coef_ref)
    terms = 0.0
    for start in range(0, VOCAB_BLOCK, GRAD_BLOCK):
        table = table_ref[:, start : start + GRAD_BLOCK]
        column = lax.broadcasted_iota(jnp.int32, (1, GRAD_BLOCK), 1) + start
        table = jnp.where(column < vocab - step * VOCAB_BLOCK, table, jnp.zeros_like(table))
        terms += mm_nt(logit_grads(start, prob_ref, coefs), table)
    add_up(step, total, terms)

    @pl.when(step == pl.num_programs(0) - 1)
    def _():
        half = first_ref.shape[0]
        first_ref[...] = total[:half, :].astype(first_ref.dtype)
        second_ref[...] = total[half:, :].astype(second_ref.dtype)


def rows_grad(table, prob, coef, dtype):
    width, vocab = table.shape
    count = prob.shape[0]
    half = whole((count // 2, width))
    return pl.pallas_call(
        functools.partial(rows_grad_kernel, vocab),
        out_shape=(sized((count // 2, width), dtype), sized((count // 2, width), BF16)),
        grid=(pl.cdiv(vocab, VOCAB_BLOCK),),
        in_specs=[
            columns(width, VOCAB_BLOCK),
            columns(count, VOCAB_BLOCK),
            whole((count, LANES)),
        ],
        out_specs=(half, half),
        scratch_shapes=[pltpu.VMEM((count, width), F32)],
        compiler_params=params(HEAD_LIMIT),
        cost_estimate=pl.CostEstimate(
            flops=2 * count * width * vocab,
            transcendentals=0,
            bytes_accessed=2 * (count + width) * vocab + 4 * count * width,
        ),
        name="rows_grad",
    )(table, prob, coef)


def table_grad_kernel(
    near_own, near_other, near_prob_ref, near_coef_ref,
    far_own, far_other, far_prob_ref, far_coef_ref, out_ref,
):
    step = pl.program_id(0)
    near_coefs, far_coefs = row_coefs(step, near_coef_ref), row_coefs(step, far_coef_ref)
    for start in range(0, VOCAB_BLOCK, GRAD_BLOCK):
        near = logit_grads(start, near_prob_ref, near_coefs)
        far = logit_grads(start, far_prob_ref, far_coefs)
        half = near_own.shape[0]
        terms = mm_tn(near_own[...], near[:half]) + mm_tn(near_other[...], near[half:])
        terms += mm_tn(far_own[...], far[:half]) + mm_tn(far_other[...], far[half:])
        out_ref[:, start : start + GRAD_BLOCK] = terms.astype(BF16)


def table_grad(vocab, near, far):
    half, width = near[0].shape
    count = 2 * half
    specs = [whole((half, width))] * 2
    specs += [columns(count, VOCAB_BLOCK), whole((count, LANES))]
    return pl.pallas_call(
        table_grad_kernel,
        out_shape=sized((width, vocab), BF16),
        grid=(pl.cdiv(vocab, VOCAB_BLOCK),),
        in_specs=specs * 2,
        out_specs=columns(width, VOCAB_BLOCK),
        compiler_params=params(HEAD_LIMIT),
        cost_estimate=pl.CostEstimate(
            flops=4 * count * width * vocab,
            transcendentals=0,
            bytes_accessed=(4 * count + 2 * width) * vocab + 4 * count * width,
        ),
        name="table_grad",
    )(*near, *far)


def gelu_tanh(values):
    return (
        0.5 * values * (1.0 + jnp.tanh(GELU_SCALE * (values + 0.044715 * values * values * values)))
    )


def gated_unit(gate_in, up_in):
    return gelu_tanh(gate_in) * up_in


def norm_rows(values, gain_vec):
    inverse = lax.rsqrt(jnp.mean(values * values, -1, keepdims=True) + EPSILON)
    return (values * inverse * gain_vec, inverse)


def norm_back(values, inverse, gain_vec, upstream):
    scaled = upstream * gain_vec
    inner_sum = jnp.mean(scaled * values, -1, keepdims=True)
    d_values = inverse * scaled - values * (inverse * inverse * inverse) * inner_sum
    d_gain = jnp.sum(upstream * values * inverse, axis=0)
    return (d_values, d_gain)


def step_back(values, inverse, gain, own, received, d_residual):
    upstream = own + sum(part.astype(F32) for part in received)
    d_values, d_gain = norm_back(values, inverse, gain, upstream)
    if d_residual is not None:
        d_values = d_residual + d_values
    return d_values, d_values.astype(BF16), d_gain


def pack_kernel(*refs):
    parts, out_ref = refs[:-1], refs[-1]
    slim = parts[0].shape[1]
    half = len(parts) // 2
    for i, part in enumerate(parts):
        side = i // half
        out_ref[i % half, :, side * slim : (side + 1) * slim] = part[...]


def pack_pairs(parts):
    depth, slim = parts[0].shape
    return pl.pallas_call(
        pack_kernel,
        out_shape=sized((len(parts) // 2, depth, 2 * slim), BF16),
        name="pack_pairs",
    )(*parts)


def join_kernel(*refs):
    parts, (moved_ref, out_ref) = refs[:-2], refs[-2:]
    slim = parts[0].shape[1]
    half = len(parts) // 2
    for i, part in enumerate(parts):
        side = i // half
        out_ref[i, :, :slim] = part[...]
        out_ref[i, :, slim:] = moved_ref[i % half, :, side * slim : (side + 1) * slim]


def join_slices(parts, moved):
    depth, slim = parts[0].shape
    return pl.pallas_call(
        join_kernel,
        out_shape=sized((len(parts), depth, 2 * slim), BF16),
        name="join_slices",
    )(*parts, moved)


def swap(values, step):
    return lax.ppermute(values, "mp", [(i, i ^ step) for i in range(4)])


def total_of_all(values):
    for axis in ("mp", "batch"):
        size, step = lax.axis_size(axis), 1
        while step < size:
            moved = lax.ppermute(values, axis, [(i, i ^ step) for i in range(size)])
            values, step = values + moved, 2 * step
    return values


def gather_batch(values, axis):
    return lax.all_gather(values, "batch", axis=axis, tiled=True)


def scatter_batch(values, axis):
    return lax.psum_scatter(values, "batch", scatter_dimension=axis, tiled=True)


def after(values, earlier):
    return lax.optimization_barrier((values, earlier))[0]


def both_slices(weights):
    return jnp.concatenate([weights, swap(weights, 2)], axis=-1)


def own_slice(grads):
    cut = grads.shape[-1] // 2
    return grads[..., :cut], swap(grads[..., cut:], 2)


def local(
    hidden_in,
    memory,
    tgt_len,
    src_len,
    target_ids,
    task_ids,
    task_weight,
    gain_self,
    q_self,
    k_self,
    v_self,
    o_self,
    gain_cross,
    q_cross,
    k_cross,
    v_cross,
    o_cross,
    gain_mlp,
    mlp_gate,
    mlp_up,
    mlp_down,
    gain_exit,
    embed_table,
):
    place = lax.axis_index("mp")
    pair = place // 2
    lower = pair == 0
    others = [place, place ^ 2, place ^ 1, place ^ 3]
    block = hidden_in.shape[1]
    own_rows = 2 * block
    width = hidden_in.shape[2]
    vocab = embed_table.shape[1]

    def of_pair(values):
        return jnp.where(lower, values[0], values[1])

    def of_other(values):
        return jnp.where(lower, values[1], values[0])

    def placed(own, received):
        far = received.astype(own.dtype)
        return jnp.stack([jnp.where(lower, own, far), jnp.where(lower, far, own)])

    pair_tgt = jnp.where(lower, tgt_len[0], tgt_len[1])
    pair_src = jnp.where(lower, src_len[0], src_len[1])
    self_scal = jnp.stack(others + [pair_tgt]).astype(jnp.int32)
    cross_scal = jnp.stack(others + [pair_src]).astype(jnp.int32)

    half_rows = 2 * own_rows
    slot_blocks = [
        (of, other)
        for of, order in ((pair, others), (1 - pair, [others[i] for i in (1, 0, 3, 2)]))
        for other in order
    ]
    row_order = jnp.stack([of * 4 + other for of, other in slot_blocks])
    ids = target_ids.reshape(8, block)[row_order].reshape(8 * block)
    local_ids = ids - place * vocab
    local_ids = jnp.where((local_ids >= 0) & (local_ids < vocab), local_ids, -1)
    positions = (
        jnp.stack([other * block for _, other in slot_blocks])[:, None] + jnp.arange(block)[None, :]
    ).reshape(8 * block)
    slot_pair = jnp.repeat(jnp.stack([pair, 1 - pair]), 4 * block)
    lengths = jnp.where(slot_pair == 0, tgt_len[0], tgt_len[1])
    valid = (positions < lengths).astype(F32)
    tasks = task_weight.shape[0]
    task_scale = jnp.sum(
        jnp.where(task_ids[:, None] == jnp.arange(tasks)[None, :], task_weight[None, :], 0.0), -1
    )
    logit_scale = width ** (-0.5)
    row_scale = jnp.where(slot_pair == 0, task_scale[0], task_scale[1]) * valid * logit_scale

    info = jnp.stack([row_scale, valid, local_ids.astype(F32)])
    info = jnp.concatenate([info, jnp.zeros((TURNED - 3, info.shape[1]), F32)])
    near_ids, far_ids = local_ids[:half_rows, None], local_ids[half_rows:, None]

    gain_size = gain_self.shape[0]
    gains = lax.all_gather(
        jnp.stack([gain_self, gain_cross, gain_mlp, gain_exit]), "batch", axis=1, tiled=True
    )
    attention = [q_self, k_self, v_self, o_self, q_cross, k_cross, v_cross, o_cross]
    slim = q_self.shape[1]
    moved = swap(pack_pairs(attention), 2)
    w_both, gains, self_scal, cross_scal = lax.optimization_barrier(
        (join_slices(attention, moved), gains.astype(F32), self_scal, cross_scal)
    )
    w_both = gather_batch(w_both, 1)
    gain_self, gain_cross, gain_mlp, gain_exit = (gains[i] for i in range(4))
    own_rows_in = of_pair(hidden_in)
    second = swap(after(of_other(hidden_in), moved), 2)
    pieces = [own_rows_in, second, swap(own_rows_in, 1), swap(second, 1)]
    mlp_part = both_slices(after(jnp.stack([mlp_gate, mlp_up, mlp_down]), moved))
    memory_own = of_pair(memory)
    memory_second = swap(after(of_other(memory), second), 2)
    memory_pieces = [memory_own, memory_second, swap(after(memory_own, pieces[3]), 1)]
    memory_pieces += [swap(memory_second, 1)]

    residual = jnp.concatenate(pieces[:2], axis=0).astype(F32)
    w_mlp = gather_batch(after(mlp_part, (w_both, pieces, memory_pieces[1])), 1)
    q_one, k_one, v_one, mixed_one, lse_one, rows_one, own_terms, other_terms = self_forward(
        self_scal, pieces, gain_self[None], w_both
    )
    memory_rows = jnp.concatenate(memory_pieces, axis=0)
    k_two = mm(memory_rows, w_both[5]).astype(BF16)
    v_two = mm(memory_rows, w_both[6]).astype(BF16)
    own_terms = after(own_terms, (k_two, v_two))
    residual_one = residual + own_terms + swap(other_terms, 1).astype(F32)

    normed_two, inverse_two = norm_rows(residual_one, gain_cross)
    own_two = normed_two.astype(BF16)
    rows_two = (own_two, swap(own_two, 1))
    q_two, mixed_two, lse_two, own_terms, other_terms = cross_forward(
        cross_scal, *rows_two, w_both, k_two, v_two
    )
    table = gather_batch(after(embed_table, (w_mlp, rows_two[1])), 0)
    residual_two = residual_one + own_terms + swap(other_terms, 1).astype(F32)

    normed_three, inverse_three = norm_rows(residual_two, gain_mlp)
    own_three = normed_three.astype(BF16)
    other_three, info, near_ids, far_ids = lax.optimization_barrier(
        (swap(own_three, 1), info, near_ids, far_ids)
    )
    rows_three = (own_three, other_three)
    gate, up_proj, hidden, own_terms, other_terms = mlp_forward(self_scal, *rows_three, w_mlp)
    residual_three = residual_two + own_terms + swap(other_terms, 1).astype(F32)
    finished = residual_three.astype(BF16)

    normed_four, inverse_four = norm_rows(residual_three, gain_exit)
    own_four = normed_four.astype(BF16)
    near_four = (own_four, swap(own_four, 1))
    far_four = (swap(own_four, 2), swap(own_four, 3))
    near_prob, near_stats, near_turned = head_forward(
        near_four, table, near_ids, logit_scale
    )
    far_four = after(far_four, near_turned)
    far_prob, far_stats, far_turned = head_forward(
        far_four, table, far_ids, logit_scale
    )
    mine = jnp.concatenate([near_turned, far_turned], axis=1)
    shares = [mine] + [swap(mine, step) for step in (1, 2, 3)]
    near_coef, far_coef, losses = combine(near_stats, far_stats, shares, info)
    finished = after(finished, near_coef)
    finished_far = swap(finished[block:], 2)
    block_out = placed(finished[:block], finished_far)
    half_sums = jnp.sum(losses[0].reshape(2, half_rows), -1)
    pair_sums = jnp.where(lower, half_sums, half_sums[::-1])
    pair_loss = pair_sums / tgt_len.astype(F32)

    table_terms = table_grad(
        vocab, (*near_four, near_prob, near_coef), (*far_four, far_prob, far_coef)
    )
    embed_sum = scatter_batch(table_terms, 0)
    far_two, far_three = rows_grad(table, far_prob, after(far_coef, table_terms), BF16)
    far_three = swap(far_three, 1)
    d_own, near_one = rows_grad(table, near_prob, after(near_coef, (far_two, finished_far)), F32)
    far_two = far_two.astype(F32) + after(far_three, near_one).astype(F32)
    received = (swap(near_one, 1), swap(far_two.astype(BF16), 2))
    d_residual, own_branch, exit_grad = step_back(
        residual_three, inverse_four, gain_exit, d_own, received, None
    )

    branch_three = (own_branch, swap(own_branch, 1))
    d_gate, d_up, own_terms, other_terms = mlp_back(self_scal, *branch_three, w_mlp, gate, up_proj)
    mlp_terms = mlp_grads(self_scal, rows_three, branch_three, d_gate, d_up, hidden)
    received = (after(swap(other_terms, 1), mlp_terms),)
    d_residual, own_branch, mlp_grad = step_back(
        residual_two, inverse_three, gain_mlp, own_terms, received, d_residual
    )

    branch_two = (own_branch, after(swap(own_branch, 1), embed_sum))
    mlp_scattered = scatter_batch(after(mlp_terms, branch_two[1]), 1)
    mlp_here, mlp_moved = own_slice(mlp_scattered)
    mlp_sum = mlp_here.astype(F32) + mlp_moved.astype(F32)
    dq_two, dk_two, dv_two, own_terms, other_terms = cross_back(
        cross_scal, *branch_two, w_both, q_two, k_two, v_two, lse_two
    )
    cross_terms = cross_grads(
        self_scal, rows_two, branch_two, memory_pieces, (dq_two, dk_two, dv_two, mixed_two)
    )
    received = (after(swap(other_terms, 1), cross_terms),)
    d_residual, own_branch, cross_grad = step_back(
        residual_one, inverse_two, gain_cross, own_terms, received, d_residual
    )

    memory_terms = mm_nt(dk_two, w_both[5]) + mm_nt(dv_two, w_both[6])
    branch_one = (own_branch, after(swap(own_branch, 1), memory_terms))
    half = memory_terms.shape[0] // 2
    memory_sent = after(memory_terms[half:].astype(BF16), branch_one[1])
    memory_received = swap(memory_sent, 1)
    memory_own = memory_terms[:half] + memory_received.astype(F32)
    dq_one, dk_one, dv_one, own_terms, other_terms, self_grad = self_back(
        self_scal, *branch_one, w_both, q_one, k_one, v_one, lse_one, pieces
    )
    last_grads = self_grads(
        self_scal,
        after(rows_one, (mlp_scattered, memory_received)),
        branch_one,
        (dq_one, dk_one, dv_one, mixed_one),
        cross_terms,
    )
    last_sum = scatter_batch(last_grads, 1)
    memory_far = swap(memory_own[half // 2 :].astype(BF16), 2)
    gain_grads = jnp.stack([self_grad[0], cross_grad, mlp_grad, exit_grad])
    gain_grads = total_of_all(after(gain_grads, last_grads))
    memory_far = after(memory_far, gain_grads)
    memory_grad = placed(memory_own[: half // 2], memory_far)
    received = (after(swap(other_terms, 1), (last_grads, mlp_moved)),)
    d_residual, _, _ = step_back(
        residual, norm_rows(residual, 1.0)[1], gain_self, own_terms, received, d_residual
    )
    hidden_far = swap(after(d_residual[block:].astype(BF16), memory_far), 2)
    hidden_grad = placed(d_residual[:block], hidden_far)
    gain_sums = lax.dynamic_slice_in_dim(
        gain_grads, lax.axis_index("batch") * gain_size, gain_size, axis=1
    )
    sent = last_sum[..., slim:]
    moved = swap(jnp.concatenate([sent[:4], sent[4:]], axis=-1), 2)
    self_sum = last_sum[:4, :, :slim].astype(F32) + moved[..., :slim].astype(F32)
    cross_sum = last_sum[4:, :, :slim].astype(F32) + moved[..., slim:].astype(F32)
    return (
        block_out,
        pair_loss,
        hidden_grad,
        memory_grad,
        gain_sums[0],
        self_sum[0],
        self_sum[1],
        self_sum[2],
        self_sum[3],
        gain_sums[1],
        cross_sum[0],
        cross_sum[1],
        cross_sum[2],
        cross_sum[3],
        gain_sums[2],
        mlp_sum[0],
        mlp_sum[1],
        mlp_sum[2],
        gain_sums[3],
        embed_sum.astype(F32),
    )


def solution(mesh):
    assert mesh.shape["mp"] == 4
    rows = P("batch", "mp", None)
    vector = P("batch")
    matrix = P("batch", "mp")
    sub = (vector, matrix, matrix, matrix, matrix)
    mlp = (vector, matrix, matrix, matrix)
    weights = sub + sub + mlp + (vector, matrix)
    in_specs = (rows, rows, vector, vector, P("batch", None), vector, P()) + weights
    out_specs = (rows, vector, rows, rows) + weights
    return jax.shard_map(local, mesh=mesh, in_specs=in_specs, out_specs=out_specs, check_vma=False)
```

```python
import functools

import jax
import jax.numpy as jnp
from jax import lax
from jax.experimental import pallas as pl
from jax.experimental.pallas import tpu as pltpu
from jax.sharding import PartitionSpec as P

DH = 64
LANES = 128
EPSILON = 1e-06
MASKED_OUT = -1000000000.0
GELU_SCALE = 0.7978845608028654
VMEM_LIMIT = 56 * 1024 * 1024
HEAD_LIMIT = 56 * 1024 * 1024
GRAD_BLOCK = 512
VOCAB_BLOCK = 2048
HIDDEN_BLOCK = 512
LOG2_E = 1.4426950408889634
BF16 = jnp.bfloat16
F32 = jnp.float32


def params(limit=VMEM_LIMIT):
    return pltpu.CompilerParams(dimension_semantics=("arbitrary",), vmem_limit_bytes=limit)


def mm(a, b):
    return lax.dot_general(a, b, (((1,), (0,)), ((), ())), preferred_element_type=F32)


def mm_nt(a, b):
    return lax.dot_general(a, b, (((1,), (1,)), ((), ())), preferred_element_type=F32)


def mm_tn(a, b):
    return lax.dot_general(a, b, (((0,), (0,)), ((), ())), preferred_element_type=F32)


def block_positions(scal_ref, size, dim):
    shape = (size, 1) if dim == 0 else (1, size)
    pieces = [lax.broadcasted_iota(jnp.int32, shape, dim) + scal_ref[i] * size for i in range(4)]
    return jnp.concatenate(pieces, axis=dim)


def score_bias(scal_ref, rows, keys, causal):
    key_pos = block_positions(scal_ref, keys // 4, 1)
    allowed = key_pos < scal_ref[4]
    if causal:
        row_pos = block_positions(scal_ref, rows // 4, 0)
        allowed = allowed & (key_pos <= row_pos)
    return jnp.where(allowed, 0.0, MASKED_OUT)


def head_lanes(rows, head):
    lane = lax.broadcasted_iota(jnp.int32, (rows, LANES), 1)
    return (lane < DH) if head == 0 else (lane >= DH)


def attend_heads(q, k, v, bias):
    rows = q.shape[0]
    outs, lses = [], []
    for head in range(2):
        q_head = jnp.where(head_lanes(rows, head), q, jnp.zeros_like(q))
        scores = mm_nt(q_head, k) + bias
        highest = jnp.max(scores, -1, keepdims=True)
        raised = jnp.exp(scores - highest)
        totals = jnp.sum(raised, -1, keepdims=True)
        outs.append(mm(raised.astype(BF16), v) * (1.0 / totals))
        lses.append(highest + jnp.log(totals))
    first = head_lanes(rows, 0)
    return jnp.where(first, outs[0], outs[1]).astype(BF16), jnp.where(first, lses[0], lses[1])


def attend_heads_back(q, k, v, lse, d_out, bias):
    rows, keys = q.shape[0], k.shape[0]
    dqs, dks, dvs = [], [], []
    for head in range(2):
        mine = head_lanes(rows, head)
        q_head = jnp.where(mine, q, jnp.zeros_like(q))
        d_head = jnp.where(mine, d_out, jnp.zeros_like(d_out))
        weights = jnp.exp(mm_nt(q_head, k) + bias - lse[:, head * DH : head * DH + 1])
        d_weights = mm_nt(d_head, v)
        inner = jnp.sum(weights * d_weights, -1, keepdims=True)
        d_scores = (weights * (d_weights - inner)).astype(BF16)
        dqs.append(mm(d_scores, k))
        dks.append(mm_tn(d_scores, q))
        dvs.append(mm_tn(weights.astype(BF16), d_out))
    first = head_lanes(keys, 0)
    return (
        jnp.where(head_lanes(rows, 0), dqs[0], dqs[1]).astype(BF16),
        jnp.where(first, dks[0], dks[1]).astype(BF16),
        jnp.where(first, dvs[0], dvs[1]).astype(BF16),
    )


def leave(total, own_ref, other_ref):
    @pl.when(pl.program_id(0) == pl.num_programs(0) - 1)
    def _():
        half = own_ref.shape[0]
        own_ref[...] = total[:half, :]
        other_ref[...] = total[half:, :].astype(BF16)


def stack_rows(own_ref, other_ref, rows):
    half = own_ref.shape[0]
    rows[:half, :] = own_ref[...]
    rows[half:, :] = other_ref[...]


def whole(shape):
    return pl.BlockSpec(shape, lambda j, *_: (0,) * len(shape))


def columns(rows, block):
    return pl.BlockSpec((rows, block), lambda j, *_: (0, j))


def weight_block(count, place, width, block):
    return pl.BlockSpec((count, width, block), lambda j, *_: (place, 0, j))


def sized(shape, dtype):
    return jax.ShapeDtypeStruct(shape, dtype)


def sublayer(kernel, name, scal, operands, specs, outs, out_specs, scratch, steps, flops, moved):
    return pl.pallas_call(
        kernel,
        out_shape=outs,
        grid_spec=pltpu.PrefetchScalarGridSpec(
            num_scalar_prefetch=1,
            grid=(steps,),
            in_specs=specs,
            out_specs=out_specs,
            scratch_shapes=scratch,
        ),
        compiler_params=params(),
        cost_estimate=pl.CostEstimate(flops=flops, transcendentals=0, bytes_accessed=moved),
        name=name,
    )(scal, *operands)


def self_forward_kernel(
    scal_ref, *refs
):
    pieces, (gain_ref, w_ref) = refs[:4], refs[4:6]
    q_ref, k_ref, v_ref, mixed_ref, lse_ref, rows_ref, own_ref, other_ref, total, bias = refs[6:]
    count = rows_ref.shape[0]

    @pl.when(pl.program_id(0) == 0)
    def _():
        size = pieces[0].shape[0]
        for i, piece in enumerate(pieces):
            normed, _ = norm_rows(piece[...].astype(F32), gain_ref[...])
            rows_ref[i * size : (i + 1) * size, :] = normed.astype(BF16)
        bias[...] = score_bias(scal_ref, count, count, True)
        total[...] = jnp.zeros_like(total)

    rows = rows_ref[...]
    q_ref[...] = mm(rows, w_ref[0]).astype(BF16)
    k_ref[...] = mm(rows, w_ref[1]).astype(BF16)
    v_ref[...] = mm(rows, w_ref[2]).astype(BF16)
    mixed, lse_ref[...] = attend_heads(q_ref[...], k_ref[...], v_ref[...], bias[...])
    mixed_ref[...] = mixed
    total[...] += mm_nt(mixed, w_ref[3])
    leave(total, own_ref, other_ref)


def self_forward(scal, pieces, gain, weights):
    block, width = pieces[0].shape
    count, cols = 4 * block, weights.shape[2]
    half = count // 2
    narrow = sized((count, cols), BF16)
    return sublayer(
        self_forward_kernel,
        "self_forward",
        scal,
        (*pieces, gain, weights),
        [whole((block, width))] * 4 + [whole((1, width)), weight_block(4, 0, width, LANES)],
        (narrow, narrow, narrow, narrow, sized((count, cols), F32))
        + (sized((count, width), BF16), sized((half, width), F32), sized((half, width), BF16)),
        [columns(count, LANES)] * 5
        + [whole((count, width)), whole((half, width)), whole((half, width))],
        [pltpu.VMEM((count, width), F32), pltpu.VMEM((count, count), F32)],
        cols // LANES,
        8 * count * width * cols + 8 * count * count * cols,
        8 * width * cols + 12 * count * cols + 8 * count * width,
    )


def cross_forward_kernel(
    scal_ref, h_own_ref, h_other_ref, w_ref, k_ref, v_ref,
    q_ref, mixed_ref, lse_ref, own_ref, other_ref, rows, total,
):
    @pl.when(pl.program_id(0) == 0)
    def _():
        stack_rows(h_own_ref, h_other_ref, rows)
        total[...] = jnp.zeros_like(total)

    bias = score_bias(scal_ref, rows.shape[0], k_ref.shape[0], False)
    q_ref[...] = mm(rows[...], w_ref[0]).astype(BF16)
    mixed, lse_ref[...] = attend_heads(q_ref[...], k_ref[...], v_ref[...], bias)
    mixed_ref[...] = mixed
    total[...] += mm_nt(mixed, w_ref[3])
    leave(total, own_ref, other_ref)


def cross_forward(scal, own, other, weights, k, v):
    half, width = own.shape
    count, cols, keys = 2 * half, weights.shape[2], k.shape[0]
    return sublayer(
        cross_forward_kernel,
        "cross_forward",
        scal,
        (own, other, weights, k, v),
        [whole((half, width))] * 2
        + [weight_block(4, 1, width, LANES), columns(keys, LANES), columns(keys, LANES)],
        (sized((count, cols), BF16), sized((count, cols), BF16), sized((count, cols), F32))
        + (sized((half, width), F32), sized((half, width), BF16)),
        [columns(count, LANES)] * 3 + [whole((half, width))] * 2,
        [pltpu.VMEM((count, width), BF16), pltpu.VMEM((count, width), F32)],
        cols // LANES,
        4 * count * width * cols + 8 * count * keys * cols,
        8 * width * cols + 8 * count * cols + 4 * keys * cols + 8 * count * width,
    )


def mlp_forward_kernel(
    scal_ref, h_own_ref, h_other_ref, w_ref,
    gate_ref, up_ref, hidden_ref, own_ref, other_ref, rows, total,
):
    @pl.when(pl.program_id(0) == 0)
    def _():
        stack_rows(h_own_ref, h_other_ref, rows)
        total[...] = jnp.zeros_like(total)

    gate = mm(rows[...], w_ref[0])
    up = mm(rows[...], w_ref[1])
    hidden = gated_unit(gate, up).astype(BF16)
    gate_ref[...] = gate
    up_ref[...] = up
    hidden_ref[...] = hidden
    total[...] += mm_nt(hidden, w_ref[2])
    leave(total, own_ref, other_ref)


def mlp_forward(scal, own, other, weights):
    half, width = own.shape
    count, cols = 2 * half, weights.shape[2]
    return sublayer(
        mlp_forward_kernel,
        "mlp_forward",
        scal,
        (own, other, weights),
        [whole((half, width))] * 2 + [weight_block(3, 0, width, HIDDEN_BLOCK)],
        (sized((count, cols), F32), sized((count, cols), F32), sized((count, cols), BF16))
        + (sized((half, width), F32), sized((half, width), BF16)),
        [columns(count, HIDDEN_BLOCK)] * 3 + [whole((half, width))] * 2,
        [pltpu.VMEM((count, width), BF16), pltpu.VMEM((count, width), F32)],
        cols // HIDDEN_BLOCK,
        6 * count * width * cols,
        6 * width * cols + 10 * count * cols + 5 * count * width,
    )


def mlp_back_kernel(
    scal_ref, e_own_ref, e_other_ref, w_ref, gate_ref, up_ref,
    d_gate_ref, d_up_ref, own_ref, other_ref, rows, total,
):
    @pl.when(pl.program_id(0) == 0)
    def _():
        stack_rows(e_own_ref, e_other_ref, rows)
        total[...] = jnp.zeros_like(total)

    d_hidden = mm(rows[...], w_ref[2])
    gate, up = gate_ref[...], up_ref[...]
    inner = GELU_SCALE * (gate + 0.044715 * gate * gate * gate)
    bent = jnp.tanh(inner)
    slope = GELU_SCALE * (1.0 + 3.0 * 0.044715 * gate * gate)
    d_gelu = 0.5 * (1.0 + bent) + 0.5 * gate * (1.0 - bent * bent) * slope
    d_gate = (d_hidden * up * d_gelu).astype(BF16)
    d_up = (d_hidden * (0.5 * gate * (1.0 + bent))).astype(BF16)
    d_gate_ref[...] = d_gate
    d_up_ref[...] = d_up
    total[...] += mm_nt(d_gate, w_ref[0]) + mm_nt(d_up, w_ref[1])
    leave(total, own_ref, other_ref)


def mlp_back(scal, own, other, weights, gate, up):
    half, width = own.shape
    count, cols = 2 * half, weights.shape[2]
    return sublayer(
        mlp_back_kernel,
        "mlp_back",
        scal,
        (own, other, weights, gate, up),
        [whole((half, width))] * 2
        + [weight_block(3, 0, width, HIDDEN_BLOCK)]
        + [columns(count, HIDDEN_BLOCK)] * 2,
        (sized((count, cols), BF16), sized((count, cols), BF16))
        + (sized((half, width), F32), sized((half, width), BF16)),
        [columns(count, HIDDEN_BLOCK)] * 2 + [whole((half, width))] * 2,
        [pltpu.VMEM((count, width), BF16), pltpu.VMEM((count, width), F32)],
        cols // HIDDEN_BLOCK,
        6 * count * width * cols,
        6 * width * cols + 12 * count * cols + 5 * count * width,
    )


def mlp_grads_kernel(
    scal_ref, h_own_ref, h_other_ref, e_own_ref, e_other_ref, d_gate_ref, d_up_ref, hidden_ref,
    out_ref,
):
    half = h_own_ref.shape[0]
    for i, (own, other, d_ref) in enumerate(
        (
            (h_own_ref, h_other_ref, d_gate_ref),
            (h_own_ref, h_other_ref, d_up_ref),
            (e_own_ref, e_other_ref, hidden_ref),
        )
    ):
        terms = mm_tn(own[...], d_ref[:half, :]) + mm_tn(other[...], d_ref[half:, :])
        out_ref[i] = terms.astype(BF16)


def mlp_grads(scal, rows, branch, d_gate, d_up, hidden):
    half, width = rows[0].shape
    count, cols = hidden.shape
    return sublayer(
        mlp_grads_kernel,
        "mlp_grads",
        scal,
        (*rows, *branch, d_gate, d_up, hidden),
        [whole((half, width))] * 4 + [columns(count, HIDDEN_BLOCK)] * 3,
        sized((3, width, cols), BF16),
        weight_block(3, 0, width, HIDDEN_BLOCK),
        [],
        cols // HIDDEN_BLOCK,
        6 * count * width * cols,
        6 * width * cols + 6 * count * cols + 4 * count * width,
    )


def attention_back_kernel(
    causal, scal_ref, e_own_ref, e_other_ref, w_ref, q_ref, k_ref, v_ref, lse_ref,
    dq_ref, dk_ref, dv_ref, own_ref, other_ref, gain_ref, rows, total, bias, *pieces,
):
    @pl.when(pl.program_id(0) == 0)
    def _():
        stack_rows(e_own_ref, e_other_ref, rows)
        total[...] = jnp.zeros_like(total)
        bias[...] = score_bias(scal_ref, rows.shape[0], k_ref.shape[0], causal)

    d_mixed = mm(rows[...], w_ref[3]).astype(BF16)
    dq, dk, dv = attend_heads_back(
        q_ref[...], k_ref[...], v_ref[...], lse_ref[...], d_mixed, bias[...]
    )
    dq_ref[...] = dq
    dk_ref[...] = dk
    dv_ref[...] = dv
    terms = mm_nt(dq, w_ref[0])
    if causal:
        terms += mm_nt(dk, w_ref[1]) + mm_nt(dv, w_ref[2])
    total[...] += terms
    leave(total, own_ref, other_ref)

    if causal:
        @pl.when(pl.program_id(0) == pl.num_programs(0) - 1)
        def _():
            size = pieces[0].shape[0]
            summed = 0.0
            for i, piece in enumerate(pieces):
                values = piece[...].astype(F32)
                unit, _ = norm_rows(values, 1.0)
                part = total[i * size : (i + 1) * size, :] * unit
                summed = summed + jnp.sum(part, 0, keepdims=True)
            gain_ref[...] = jnp.broadcast_to(summed, gain_ref.shape)


def cross_back(scal, own, other, weights, q, k, v, lse):
    half, width = own.shape
    count, cols, keys = 2 * half, weights.shape[2], k.shape[0]

    def kernel(scal_ref, *refs):
        attention_back_kernel(False, scal_ref, *refs[:12], None, *refs[12:])

    return sublayer(
        kernel,
        "cross_back",
        scal,
        (own, other, weights, q, k, v, lse),
        [whole((half, width))] * 2
        + [weight_block(4, 1, width, LANES), columns(count, LANES)]
        + [columns(keys, LANES)] * 2
        + [columns(count, LANES)],
        (sized((count, cols), BF16), sized((keys, cols), BF16), sized((keys, cols), BF16))
        + (sized((half, width), F32), sized((half, width), BF16)),
        [columns(count, LANES), columns(keys, LANES), columns(keys, LANES)]
        + [whole((half, width))] * 2,
        [
            pltpu.VMEM((count, width), BF16),
            pltpu.VMEM((count, width), F32),
            pltpu.VMEM((1, keys), F32),
        ],
        cols // LANES,
        4 * count * width * cols + 20 * count * keys * cols,
        8 * width * cols + 8 * count * cols + 8 * keys * cols + 8 * count * width,
    )


def self_back(scal, own, other, weights, q, k, v, lse, pieces):
    half, width = own.shape
    count, cols = 2 * half, weights.shape[2]
    block = pieces[0].shape[0]

    def kernel(scal_ref, *refs):
        attention_back_kernel(True, scal_ref, *refs[:7], *refs[11:], *refs[7:11])

    narrow = sized((count, cols), BF16)
    return sublayer(
        kernel,
        "self_back",
        scal,
        (own, other, weights, q, k, v, lse, *pieces),
        [whole((half, width))] * 2
        + [weight_block(4, 0, width, LANES)]
        + [columns(count, LANES)] * 4
        + [whole((block, width))] * 4,
        (narrow, narrow, narrow, sized((half, width), F32), sized((half, width), BF16))
        + (sized((8, width), F32),),
        [columns(count, LANES)] * 3 + [whole((half, width))] * 2 + [whole((8, width))],
        [
            pltpu.VMEM((count, width), BF16),
            pltpu.VMEM((count, width), F32),
            pltpu.VMEM((count, count), F32),
        ],
        cols // LANES,
        8 * count * width * cols + 20 * count * count * cols,
        8 * width * cols + 20 * count * cols + 10 * count * width,
    )


def cross_grads_kernel(scal_ref, h_own, h_other, e_own, e_other, *refs):
    memory, (dq, dk, dv, mixed, out_ref) = refs[:4], refs[4:]
    half = e_own.shape[0]

    def memory_grad(d_ref):
        size = memory[0].shape[0]
        terms = [mm_tn(m[...], d_ref[i * size : (i + 1) * size, :]) for i, m in enumerate(memory)]
        return sum(terms).astype(BF16)

    def split_grad(own, other, d_ref):
        return (mm_tn(own[...], d_ref[:half, :]) + mm_tn(other[...], d_ref[half:, :])).astype(BF16)

    out_ref[0] = split_grad(h_own, h_other, dq)
    out_ref[1] = memory_grad(dk)
    out_ref[2] = memory_grad(dv)
    out_ref[3] = split_grad(e_own, e_other, mixed)


def cross_grads(scal, rows, branch, memory, narrow):
    half, width = rows[0].shape
    cols, keys = narrow[0].shape[1], narrow[1].shape[0]
    return sublayer(
        cross_grads_kernel,
        "cross_grads",
        scal,
        (*rows, *branch, *memory, *narrow),
        [whole((half, width))] * 4
        + [whole((keys // 4, width))] * 4
        + [columns(array.shape[0], LANES) for array in narrow],
        sized((8, width, cols), BF16),
        weight_block(4, 1, width, LANES),
        [],
        cols // LANES,
        (8 * half + 4 * keys) * width * cols,
        8 * width * cols + (8 * half + 4 * keys) * cols + 8 * half * width,
    )


def self_grads_kernel(scal_ref, h, e_own, e_other, dq, dk, dv, mixed, rest_ref, out_ref):
    half = e_own.shape[0]
    for i, d_ref in enumerate((dq, dk, dv)):
        out_ref[i] = mm_tn(h[...], d_ref[...]).astype(BF16)
    terms = mm_tn(e_own[...], mixed[:half, :]) + mm_tn(e_other[...], mixed[half:, :])
    out_ref[3] = terms.astype(BF16)


def self_grads(scal, rows, branch, narrow, rest):
    count, width = rows.shape
    cols = narrow[0].shape[1]
    return pl.pallas_call(
        self_grads_kernel,
        out_shape=sized(rest.shape, BF16),
        grid_spec=pltpu.PrefetchScalarGridSpec(
            num_scalar_prefetch=1,
            grid=(cols // LANES,),
            in_specs=[whole((count, width))]
            + [whole((count // 2, width))] * 2
            + [columns(count, LANES)] * 4
            + [pl.BlockSpec(memory_space=pl.ANY)],
            out_specs=weight_block(4, 0, width, LANES),
        ),
        input_output_aliases={8: 0},
        compiler_params=params(),
        cost_estimate=pl.CostEstimate(
            flops=8 * count * width * cols,
            transcendentals=0,
            bytes_accessed=8 * width * cols + 8 * count * cols + 4 * count * width,
        ),
        name="self_grads",
    )(scal, rows, *branch, *narrow, rest)


SUMS = 32
PICKS = 64
WEIGHT_LANE = 126
ID_LANE = 127
TURNED = 8


def column_bias(vocab, step, block):
    column = lax.broadcasted_iota(jnp.int32, (1, block), 1) + step * block
    return jnp.where(column < vocab, 0.0, MASKED_OUT)


def head_kernel(vocab, scale, own_ref, other_ref, table_ref, ids_ref, prob_ref, stat_ref, turned_ref):
    step = pl.program_id(0)
    block = table_ref.shape[1]
    table = table_ref[...]
    chunk = 128
    bias = column_bias(vocab, step, block)
    column = lax.broadcasted_iota(jnp.int32, (1, block), 1)
    lane = lax.broadcasted_iota(jnp.int32, (chunk, LANES), 1)
    half = own_ref.shape[0]
    for start in range(0, 2 * half, chunk):
        part = pl.ds(start, chunk)
        rows_ref = own_ref if start < half else other_ref
        products = mm(rows_ref[pl.ds(start % half, chunk), :], table) + bias
        highest = jnp.max(products, -1, keepdims=True)
        raised = jnp.exp2((products - highest) * (scale * LOG2_E))
        prob_ref[part, :] = raised.astype(BF16)
        totals = jnp.sum(raised, -1, keepdims=True)
        target = ids_ref[part, :] - step * block
        picked = jnp.sum(jnp.where(column == target, products, 0.0), -1, keepdims=True)
        stats = jnp.where(step == 0, 0.0, stat_ref[part, :])
        stats = jnp.where(lane == step, highest * scale, stats)
        stats = jnp.where(lane == SUMS + step, totals, stats)
        stat_ref[part, :] = jnp.where(lane == PICKS + step, picked * scale, stats)

    @pl.when(step == pl.num_programs(0) - 1)
    def _():
        stats = stat_ref[...].T
        steps = pl.num_programs(0)
        row = lax.broadcasted_iota(jnp.int32, (SUMS, stats.shape[1]), 0)
        tops = jnp.where(row < steps, stats[:SUMS], MASKED_OUT)
        highest = jnp.max(tops, 0, keepdims=True)
        totals = jnp.sum(stats[SUMS:PICKS] * jnp.exp(tops - highest), 0, keepdims=True)
        picked = jnp.sum(stats[PICKS : PICKS + SUMS], 0, keepdims=True)
        row = lax.broadcasted_iota(jnp.int32, (TURNED, stats.shape[1]), 0)
        turned_ref[...] = jnp.where(row == 0, highest, jnp.where(row == 1, totals, picked))


def head_forward(rows, table, ids, scale):
    half, width = rows[0].shape
    count, vocab = 2 * half, table.shape[1]
    steps = pl.cdiv(vocab, VOCAB_BLOCK)
    return pl.pallas_call(
        functools.partial(head_kernel, vocab, scale),
        out_shape=(
            jax.ShapeDtypeStruct((count, steps * VOCAB_BLOCK), BF16),
            jax.ShapeDtypeStruct((count, LANES), F32),
            jax.ShapeDtypeStruct((TURNED, count), F32),
        ),
        grid=(steps,),
        in_specs=[
            whole((half, width)),
            whole((half, width)),
            pl.BlockSpec((width, VOCAB_BLOCK), lambda j: (0, j)),
            pl.BlockSpec((count, 1), lambda j: (0, 0)),
        ],
        out_specs=(
            columns(count, VOCAB_BLOCK),
            pl.BlockSpec((count, LANES), lambda j: (0, 0)),
            pl.BlockSpec((TURNED, count), lambda j: (0, 0)),
        ),
        compiler_params=params(HEAD_LIMIT),
        cost_estimate=pl.CostEstimate(
            flops=2 * count * width * vocab,
            transcendentals=count * vocab,
            bytes_accessed=2 * (count + width) * vocab + 2 * count * width,
        ),
        name="head_forward",
    )(*rows, table, ids)


def combine_kernel(near_stat_ref, far_stat_ref, *refs):
    share_refs, (info_ref, near_ref, far_ref, loss_ref) = refs[:4], refs[4:]
    half = near_stat_ref.shape[0]
    count = 2 * half
    own = count // 4
    shares = [
        jnp.concatenate(
            [ref[:, (slot ^ step) * own : ((slot ^ step) + 1) * own] for slot in range(4)], axis=1
        )
        for step, ref in enumerate(share_refs)
    ]
    highest = functools.reduce(jnp.maximum, [share[0:1] for share in shares])
    totals = sum(share[1:2] * jnp.exp(share[0:1] - highest) for share in shares)
    picked = sum(share[2:3] for share in shares)
    log_totals = highest + jnp.log(totals)
    info = info_ref[...]
    loss_ref[...] = jnp.broadcast_to((log_totals - picked) * info[1:2], (TURNED, count))
    row = lax.broadcasted_iota(jnp.int32, (LANES, count), 0)
    turned = jnp.where(row == 0, log_totals, jnp.where(row == 1, info[0:1], info[2:3])).T
    lane = lax.broadcasted_iota(jnp.int32, (half, LANES), 1)
    for stat_ref, coef_ref, start in ((near_stat_ref, near_ref, 0), (far_stat_ref, far_ref, half)):
        part = turned[start : start + half]
        weight = part[:, 1:2]
        coef = weight * jnp.exp(jnp.minimum(stat_ref[...] - part[:, 0:1], 0.0))
        coef = jnp.where(lane == WEIGHT_LANE, weight, coef)
        coef_ref[...] = jnp.where(lane == ID_LANE, part[:, 2:3], coef)


def combine(near_stats, far_stats, shares, info):
    half = near_stats.shape[0]
    return pl.pallas_call(
        combine_kernel,
        out_shape=(
            sized((half, LANES), F32),
            sized((half, LANES), F32),
            sized((TURNED, 2 * half), F32),
        ),
        compiler_params=pltpu.CompilerParams(vmem_limit_bytes=HEAD_LIMIT),
        cost_estimate=pl.CostEstimate(
            flops=20 * half * LANES,
            transcendentals=2 * half * LANES,
            bytes_accessed=16 * half * LANES,
        ),
        name="combine",
    )(near_stats, far_stats, *shares, info)


def row_coefs(step, coef_ref):
    coef = coef_ref[...]
    lane = lax.broadcasted_iota(jnp.int32, coef.shape, 1)
    factor = jnp.sum(jnp.where(lane == step, coef, 0.0), -1, keepdims=True)
    target = coef[:, ID_LANE : ID_LANE + 1].astype(jnp.int32)
    return factor, coef[:, WEIGHT_LANE : WEIGHT_LANE + 1], target - step * VOCAB_BLOCK


def logit_grads(start, prob_ref, coefs):
    factor, weight, target = coefs
    column = lax.broadcasted_iota(jnp.int32, (1, GRAD_BLOCK), 1) + start
    prob = prob_ref[:, start : start + GRAD_BLOCK].astype(F32)
    return (prob * factor - jnp.where(column == target, weight, 0.0)).astype(BF16)


def add_up(step, out_ref, terms):
    @pl.when(step == 0)
    def _():
        out_ref[...] = terms

    @pl.when(step > 0)
    def _():
        out_ref[...] += terms


def rows_grad_kernel(vocab, table_ref, prob_ref, coef_ref, first_ref, second_ref, total):
    step = pl.program_id(0)
    coefs = row_coefs(step, coef_ref)
    terms = 0.0
    for start in range(0, VOCAB_BLOCK, GRAD_BLOCK):
        table = table_ref[:, start : start + GRAD_BLOCK]
        column = lax.broadcasted_iota(jnp.int32, (1, GRAD_BLOCK), 1) + start
        table = jnp.where(column < vocab - step * VOCAB_BLOCK, table, jnp.zeros_like(table))
        terms += mm_nt(logit_grads(start, prob_ref, coefs), table)
    add_up(step, total, terms)

    @pl.when(step == pl.num_programs(0) - 1)
    def _():
        half = first_ref.shape[0]
        first_ref[...] = total[:half, :].astype(first_ref.dtype)
        second_ref[...] = total[half:, :].astype(second_ref.dtype)


def rows_grad(table, prob, coef, dtype):
    width, vocab = table.shape
    count = prob.shape[0]
    half = whole((count // 2, width))
    return pl.pallas_call(
        functools.partial(rows_grad_kernel, vocab),
        out_shape=(sized((count // 2, width), dtype), sized((count // 2, width), BF16)),
        grid=(pl.cdiv(vocab, VOCAB_BLOCK),),
        in_specs=[
            columns(width, VOCAB_BLOCK),
            columns(count, VOCAB_BLOCK),
            whole((count, LANES)),
        ],
        out_specs=(half, half),
        scratch_shapes=[pltpu.VMEM((count, width), F32)],
        compiler_params=params(HEAD_LIMIT),
        cost_estimate=pl.CostEstimate(
            flops=2 * count * width * vocab,
            transcendentals=0,
            bytes_accessed=2 * (count + width) * vocab + 4 * count * width,
        ),
        name="rows_grad",
    )(table, prob, coef)


def table_grad_kernel(
    near_own, near_other, near_prob_ref, near_coef_ref,
    far_own, far_other, far_prob_ref, far_coef_ref, out_ref,
):
    step = pl.program_id(0)
    near_coefs, far_coefs = row_coefs(step, near_coef_ref), row_coefs(step, far_coef_ref)
    for start in range(0, VOCAB_BLOCK, GRAD_BLOCK):
        near = logit_grads(start, near_prob_ref, near_coefs)
        far = logit_grads(start, far_prob_ref, far_coefs)
        half = near_own.shape[0]
        terms = mm_tn(near_own[...], near[:half]) + mm_tn(near_other[...], near[half:])
        terms += mm_tn(far_own[...], far[:half]) + mm_tn(far_other[...], far[half:])
        out_ref[:, start : start + GRAD_BLOCK] = terms.astype(BF16)


def table_grad(vocab, near, far):
    half, width = near[0].shape
    count = 2 * half
    specs = [whole((half, width))] * 2
    specs += [columns(count, VOCAB_BLOCK), whole((count, LANES))]
    return pl.pallas_call(
        table_grad_kernel,
        out_shape=sized((width, vocab), BF16),
        grid=(pl.cdiv(vocab, VOCAB_BLOCK),),
        in_specs=specs * 2,
        out_specs=columns(width, VOCAB_BLOCK),
        compiler_params=params(HEAD_LIMIT),
        cost_estimate=pl.CostEstimate(
            flops=4 * count * width * vocab,
            transcendentals=0,
            bytes_accessed=(4 * count + 2 * width) * vocab + 4 * count * width,
        ),
        name="table_grad",
    )(*near, *far)


def gelu_tanh(values):
    return (
        0.5 * values * (1.0 + jnp.tanh(GELU_SCALE * (values + 0.044715 * values * values * values)))
    )


def gated_unit(gate_in, up_in):
    return gelu_tanh(gate_in) * up_in


def norm_rows(values, gain_vec):
    inverse = lax.rsqrt(jnp.mean(values * values, -1, keepdims=True) + EPSILON)
    return (values * inverse * gain_vec, inverse)


def norm_back(values, inverse, gain_vec, upstream):
    scaled = upstream * gain_vec
    inner_sum = jnp.mean(scaled * values, -1, keepdims=True)
    d_values = inverse * scaled - values * (inverse * inverse * inverse) * inner_sum
    d_gain = jnp.sum(upstream * values * inverse, axis=0)
    return (d_values, d_gain)


def step_back(values, inverse, gain, own, received, d_residual):
    upstream = own + sum(part.astype(F32) for part in received)
    d_values, d_gain = norm_back(values, inverse, gain, upstream)
    if d_residual is not None:
        d_values = d_residual + d_values
    return d_values, d_values.astype(BF16), d_gain


def pack_kernel(*refs):
    parts, out_ref = refs[:-1], refs[-1]
    slim = parts[0].shape[1]
    half = len(parts) // 2
    for i, part in enumerate(parts):
        side = i // half
        out_ref[i % half, :, side * slim : (side + 1) * slim] = part[...]


def pack_pairs(parts):
    depth, slim = parts[0].shape
    return pl.pallas_call(
        pack_kernel,
        out_shape=sized((len(parts) // 2, depth, 2 * slim), BF16),
        name="pack_pairs",
    )(*parts)


def join_kernel(*refs):
    parts, (moved_ref, out_ref) = refs[:-2], refs[-2:]
    slim = parts[0].shape[1]
    half = len(parts) // 2
    for i, part in enumerate(parts):
        side = i // half
        out_ref[i, :, :slim] = part[...]
        out_ref[i, :, slim:] = moved_ref[i % half, :, side * slim : (side + 1) * slim]


def join_slices(parts, moved):
    depth, slim = parts[0].shape
    return pl.pallas_call(
        join_kernel,
        out_shape=sized((len(parts), depth, 2 * slim), BF16),
        name="join_slices",
    )(*parts, moved)


def swap(values, step):
    return lax.ppermute(values, "mp", [(i, i ^ step) for i in range(4)])


def total_of_all(values):
    for axis in ("mp", "batch"):
        size, step = lax.axis_size(axis), 1
        while step < size:
            moved = lax.ppermute(values, axis, [(i, i ^ step) for i in range(size)])
            values, step = values + moved, 2 * step
    return values


def gather_batch(values, axis):
    return lax.all_gather(values, "batch", axis=axis, tiled=True)


def scatter_batch(values, axis):
    return lax.psum_scatter(values, "batch", scatter_dimension=axis, tiled=True)


def after(values, earlier):
    return lax.optimization_barrier((values, earlier))[0]


def both_slices(weights):
    return jnp.concatenate([weights, swap(weights, 2)], axis=-1)


def own_slice(grads):
    cut = grads.shape[-1] // 2
    return grads[..., :cut], swap(grads[..., cut:], 2)


def local(
    hidden_in,
    memory,
    tgt_len,
    src_len,
    target_ids,
    task_ids,
    task_weight,
    gain_self,
    q_self,
    k_self,
    v_self,
    o_self,
    gain_cross,
    q_cross,
    k_cross,
    v_cross,
    o_cross,
    gain_mlp,
    mlp_gate,
    mlp_up,
    mlp_down,
    gain_exit,
    embed_table,
):
    place = lax.axis_index("mp")
    pair = place // 2
    lower = pair == 0
    others = [place, place ^ 2, place ^ 1, place ^ 3]
    block = hidden_in.shape[1]
    own_rows = 2 * block
    width = hidden_in.shape[2]
    vocab = embed_table.shape[1]

    def of_pair(values):
        return jnp.where(lower, values[0], values[1])

    def of_other(values):
        return jnp.where(lower, values[1], values[0])

    def placed(own, received):
        far = received.astype(own.dtype)
        return jnp.stack([jnp.where(lower, own, far), jnp.where(lower, far, own)])

    pair_tgt = jnp.where(lower, tgt_len[0], tgt_len[1])
    pair_src = jnp.where(lower, src_len[0], src_len[1])
    self_scal = jnp.stack(others + [pair_tgt]).astype(jnp.int32)
    cross_scal = jnp.stack(others + [pair_src]).astype(jnp.int32)

    half_rows = 2 * own_rows
    slot_blocks = [
        (of, other)
        for of, order in ((pair, others), (1 - pair, [others[i] for i in (1, 0, 3, 2)]))
        for other in order
    ]
    row_order = jnp.stack([of * 4 + other for of, other in slot_blocks])
    ids = target_ids.reshape(8, block)[row_order].reshape(8 * block)
    local_ids = ids - place * vocab
    local_ids = jnp.where((local_ids >= 0) & (local_ids < vocab), local_ids, -1)
    positions = (
        jnp.stack([other * block for _, other in slot_blocks])[:, None] + jnp.arange(block)[None, :]
    ).reshape(8 * block)
    slot_pair = jnp.repeat(jnp.stack([pair, 1 - pair]), 4 * block)
    lengths = jnp.where(slot_pair == 0, tgt_len[0], tgt_len[1])
    valid = (positions < lengths).astype(F32)
    tasks = task_weight.shape[0]
    task_scale = jnp.sum(
        jnp.where(task_ids[:, None] == jnp.arange(tasks)[None, :], task_weight[None, :], 0.0), -1
    )
    logit_scale = width ** (-0.5)
    row_scale = jnp.where(slot_pair == 0, task_scale[0], task_scale[1]) * valid * logit_scale

    info = jnp.stack([row_scale, valid, local_ids.astype(F32)])
    info = jnp.concatenate([info, jnp.zeros((TURNED - 3, info.shape[1]), F32)])
    near_ids, far_ids = local_ids[:half_rows, None], local_ids[half_rows:, None]

    gain_size = gain_self.shape[0]
    gains = lax.all_gather(
        jnp.stack([gain_self, gain_cross, gain_mlp, gain_exit]), "batch", axis=1, tiled=True
    )
    attention = [q_self, k_self, v_self, o_self, q_cross, k_cross, v_cross, o_cross]
    slim = q_self.shape[1]
    moved = swap(pack_pairs(attention), 2)
    w_both, gains, self_scal, cross_scal = lax.optimization_barrier(
        (join_slices(attention, moved), gains.astype(F32), self_scal, cross_scal)
    )
    w_both = gather_batch(w_both, 1)
    gain_self, gain_cross, gain_mlp, gain_exit = (gains[i] for i in range(4))
    own_rows_in = of_pair(hidden_in)
    second = swap(after(of_other(hidden_in), moved), 2)
    pieces = [own_rows_in, second, swap(own_rows_in, 1), swap(second, 1)]
    mlp_part = both_slices(after(jnp.stack([mlp_gate, mlp_up, mlp_down]), moved))
    memory_own = of_pair(memory)
    memory_second = swap(after(of_other(memory), second), 2)
    memory_pieces = [memory_own, memory_second, swap(after(memory_own, pieces[3]), 1)]
    memory_pieces += [swap(memory_second, 1)]

    residual = jnp.concatenate(pieces[:2], axis=0).astype(F32)
    w_mlp = gather_batch(after(mlp_part, (w_both, pieces, memory_pieces[1])), 1)
    q_one, k_one, v_one, mixed_one, lse_one, rows_one, own_terms, other_terms = self_forward(
        self_scal, pieces, gain_self[None], w_both
    )
    memory_rows = jnp.concatenate(memory_pieces, axis=0)
    k_two = mm(memory_rows, w_both[5]).astype(BF16)
    v_two = mm(memory_rows, w_both[6]).astype(BF16)
    own_terms = after(own_terms, (k_two, v_two))
    residual_one = residual + own_terms + swap(other_terms, 1).astype(F32)

    normed_two, inverse_two = norm_rows(residual_one, gain_cross)
    own_two = normed_two.astype(BF16)
    other_two, info, near_ids, far_ids = lax.optimization_barrier(
        (swap(own_two, 1), info, near_ids, far_ids)
    )
    rows_two = (own_two, other_two)
    q_two, mixed_two, lse_two, own_terms, other_terms = cross_forward(
        cross_scal, *rows_two, w_both, k_two, v_two
    )
    table = gather_batch(after(embed_table, (w_mlp, rows_two[1])), 0)
    residual_two = residual_one + own_terms + swap(other_terms, 1).astype(F32)

    normed_three, inverse_three = norm_rows(residual_two, gain_mlp)
    own_three = normed_three.astype(BF16)
    rows_three = (own_three, swap(own_three, 1))
    gate, up_proj, hidden, own_terms, other_terms = mlp_forward(self_scal, *rows_three, w_mlp)
    residual_three = residual_two + own_terms + swap(other_terms, 1).astype(F32)
    finished = residual_three.astype(BF16)

    normed_four, inverse_four = norm_rows(residual_three, gain_exit)
    own_four = normed_four.astype(BF16)
    near_four = (own_four, swap(own_four, 1))
    far_four = (swap(own_four, 2), swap(own_four, 3))
    near_prob, near_stats, near_turned = head_forward(
        near_four, table, near_ids, logit_scale
    )
    far_four = after(far_four, near_turned)
    far_prob, far_stats, far_turned = head_forward(
        far_four, table, far_ids, logit_scale
    )
    mine = jnp.concatenate([near_turned, far_turned], axis=1)
    shares = [mine] + [swap(mine, step) for step in (1, 2, 3)]
    near_coef, far_coef, losses = combine(near_stats, far_stats, shares, info)
    finished = after(finished, near_coef)
    finished_far = swap(finished[block:], 2)
    block_out = placed(finished[:block], finished_far)
    half_sums = jnp.sum(losses[0].reshape(2, half_rows), -1)
    pair_sums = jnp.where(lower, half_sums, half_sums[::-1])
    pair_loss = pair_sums / tgt_len.astype(F32)

    table_terms = table_grad(
        vocab, (*near_four, near_prob, near_coef), (*far_four, far_prob, far_coef)
    )
    embed_sum = scatter_batch(table_terms, 0)
    far_two, far_three = rows_grad(table, far_prob, after(far_coef, table_terms), BF16)
    far_three = swap(far_three, 1)
    d_own, near_one = rows_grad(table, near_prob, after(near_coef, (far_two, finished_far)), F32)
    far_two = far_two.astype(F32) + after(far_three, near_one).astype(F32)
    received = (swap(near_one, 1), swap(far_two.astype(BF16), 2))
    d_residual, own_branch, exit_grad = step_back(
        residual_three, inverse_four, gain_exit, d_own, received, None
    )

    branch_three = (own_branch, swap(own_branch, 1))
    d_gate, d_up, own_terms, other_terms = mlp_back(self_scal, *branch_three, w_mlp, gate, up_proj)
    mlp_terms = mlp_grads(self_scal, rows_three, branch_three, d_gate, d_up, hidden)
    received = (after(swap(other_terms, 1), mlp_terms),)
    d_residual, own_branch, mlp_grad = step_back(
        residual_two, inverse_three, gain_mlp, own_terms, received, d_residual
    )

    branch_two = (own_branch, after(swap(own_branch, 1), embed_sum))
    mlp_scattered = scatter_batch(after(mlp_terms, branch_two[1]), 1)
    mlp_here, mlp_moved = own_slice(mlp_scattered)
    mlp_sum = mlp_here.astype(F32) + mlp_moved.astype(F32)
    dq_two, dk_two, dv_two, own_terms, other_terms = cross_back(
        cross_scal, *branch_two, w_both, q_two, k_two, v_two, lse_two
    )
    cross_terms = cross_grads(
        self_scal, rows_two, branch_two, memory_pieces, (dq_two, dk_two, dv_two, mixed_two)
    )
    received = (after(swap(other_terms, 1), cross_terms),)
    d_residual, own_branch, cross_grad = step_back(
        residual_one, inverse_two, gain_cross, own_terms, received, d_residual
    )

    memory_terms = mm_nt(dk_two, w_both[5]) + mm_nt(dv_two, w_both[6])
    branch_one = (own_branch, after(swap(own_branch, 1), memory_terms))
    half = memory_terms.shape[0] // 2
    memory_sent = after(memory_terms[half:].astype(BF16), branch_one[1])
    memory_received = swap(memory_sent, 1)
    memory_own = memory_terms[:half] + memory_received.astype(F32)
    dq_one, dk_one, dv_one, own_terms, other_terms, self_grad = self_back(
        self_scal, *branch_one, w_both, q_one, k_one, v_one, lse_one, pieces
    )
    last_grads = self_grads(
        self_scal,
        after(rows_one, (mlp_scattered, memory_received)),
        branch_one,
        (dq_one, dk_one, dv_one, mixed_one),
        cross_terms,
    )
    last_sum = scatter_batch(last_grads, 1)
    memory_far = swap(memory_own[half // 2 :].astype(BF16), 2)
    gain_grads = jnp.stack([self_grad[0], cross_grad, mlp_grad, exit_grad])
    gain_grads = total_of_all(after(gain_grads, last_grads))
    memory_far = after(memory_far, gain_grads)
    memory_grad = placed(memory_own[: half // 2], memory_far)
    received = (after(swap(other_terms, 1), (last_grads, mlp_moved)),)
    d_residual, _, _ = step_back(
        residual, norm_rows(residual, 1.0)[1], gain_self, own_terms, received, d_residual
    )
    hidden_far = swap(after(d_residual[block:].astype(BF16), memory_far), 2)
    hidden_grad = placed(d_residual[:block], hidden_far)
    gain_sums = lax.dynamic_slice_in_dim(
        gain_grads, lax.axis_index("batch") * gain_size, gain_size, axis=1
    )
    sent = last_sum[..., slim:]
    moved = swap(jnp.concatenate([sent[:4], sent[4:]], axis=-1), 2)
    self_sum = last_sum[:4, :, :slim].astype(F32) + moved[..., :slim].astype(F32)
    cross_sum = last_sum[4:, :, :slim].astype(F32) + moved[..., slim:].astype(F32)
    return (
        block_out,
        pair_loss,
        hidden_grad,
        memory_grad,
        gain_sums[0],
        self_sum[0],
        self_sum[1],
        self_sum[2],
        self_sum[3],
        gain_sums[1],
        cross_sum[0],
        cross_sum[1],
        cross_sum[2],
        cross_sum[3],
        gain_sums[2],
        mlp_sum[0],
        mlp_sum[1],
        mlp_sum[2],
        gain_sums[3],
        embed_sum.astype(F32),
    )


def solution(mesh):
    assert mesh.shape["mp"] == 4
    rows = P("batch", "mp", None)
    vector = P("batch")
    matrix = P("batch", "mp")
    sub = (vector, matrix, matrix, matrix, matrix)
    mlp = (vector, matrix, matrix, matrix)
    weights = sub + sub + mlp + (vector, matrix)
    in_specs = (rows, rows, vector, vector, P("batch", None), vector, P()) + weights
    out_specs = (rows, vector, rows, rows) + weights
    return jax.shard_map(local, mesh=mesh, in_specs=in_specs, out_specs=out_specs, check_vma=False)
```
